32 devices in a mesh: dp: 2 (over y), row: 4 (over x, core), col: 4 (over z).
Axes of the slice: x: 2, y: 2, z: 4, core: 2. Of those that a mesh axis runs over, the one named last changes fastest.
Arguments:
- tokens: bfloat16 [8192, 1024], P(('dp', 'col'), 'row'), may hold values from -6 to 6
- encoder: bfloat16 [8192, 1024], P(('dp', 'col'), 'row'), may hold values from -6 to 6
- cotangent: bfloat16 [8192, 1024], P(('dp', 'col'), 'row'), may hold values from -6 to 6
- prefixes: int32 [2], P('dp'), may hold values from 409 to 2048
- selfqkv: bfloat16 [1024, 3, 1024], P('row', None, 'col'), may hold values from -0.1875 to 0.1875
- selfbias: float32 [2, 1024], P(None, 'col'), may hold values from -0.3 to 0.3
- selfproj: bfloat16 [1024, 1024], P('col', 'row'), may hold values from -3 to 3
- selfshift: float32 [1024], P('row'), may hold values from -3 to 3
- crossquery: bfloat16 [1024, 1024], P('row', 'col'), may hold values from -0.1875 to 0.1875
- crosskv: bfloat16 [1024, 2, 1024], P('row', None, 'col'), may hold values from -0.1875 to 0.1875
- crossbias: float32 [2, 1024], P(None, 'col'), may hold values from -0.3 to 0.3
- crossproj: bfloat16 [1024, 1024], P('col', 'row'), may hold values from -4 to 4
- crossshift: float32 [1024], P('row'), may hold values from -3 to 3
- upweight: bfloat16 [1024, 4096], P('row', 'col'), may hold values from -0.1875 to 0.1875
- upbias: float32 [4096], P('col'), may hold values from -6 to 6
- downweight: bfloat16 [4096, 1024], P('col', 'row'), may hold values from -0.09375 to 0.09375
- downbias: float32 [1024], P('row'), may hold values from -3 to 3
- normgain: float32 [3, 1024], P(None, 'row'), may hold values from 0.5 to 1.5
- normshift: float32 [3, 1024], P(None, 'row'), may hold values from -3 to 3
Outputs:
- layer_out: bfloat16 [8192, 1024], P(('dp', 'col'), 'row')
- tokens_grad: float32 [8192, 1024], P(('dp', 'col'), 'row')
- encoder_grad: float32 [8192, 1024], P(('dp', 'col'), 'row')
- selfqkv_grad: float32 [1024, 3, 1024], P('row', None, 'col')
- selfbias_grad: float32 [2, 1024], P(None, 'col')
- selfproj_grad: float32 [1024, 1024], P('col', 'row')
- selfshift_grad: float32 [1024], P('row')
- crossquery_grad: float32 [1024, 1024], P('row', 'col')
- crosskv_grad: float32 [1024, 2, 1024], P('row', None, 'col')
- crossbias_grad: float32 [2, 1024], P(None, 'col')
- crossproj_grad: float32 [1024, 1024], P('col', 'row')
- crossshift_grad: float32 [1024], P('row')
- upweight_grad: float32 [1024, 4096], P('row', 'col')
- upbias_grad: float32 [4096], P('col')
- downweight_grad: float32 [4096, 1024], P('col', 'row')
- downbias_grad: float32 [1024], P('row')
- normgain_grad: float32 [3, 1024], P(None, 'row')
- normshift_grad: float32 [3, 1024], P(None, 'row')
The draws below stay inside these ranges and needn't reach their ends.
Inputs may be any that keep to these rules, and one draw needn't show every extreme that they name: prefixes counts each sequence's leading tokens that see one another both ways.
All inputs are finite; a program needn't handle non-finite values.
Results may differ from the reference program's by a relative error of at most 0.018.
Values may be sent and summed in bfloat16 or wider, within the bound.
No kernel may reach another device: no remote copies, remote signals or barrier semaphores. Data moves between devices by JAX's collectives and lax.ppermute only.
A program may use at most 384 MiB of HBM per device.

```python
import jax
import jax.numpy as jnp
from jax import lax

D = 1024
HEADS = 16
HD = 64
FF = 4096
SEQ_LEN = 4096
TOKENS = 8192
SEQS = 2
ENC_TOKENS = 8192


def bounded_normal(key, shape, scale, limit):
    return jnp.clip(jax.random.normal(key, shape, jnp.float32) * scale, -limit, limit)


def draw_tokens(key, part):
    return bounded_normal(jax.random.fold_in(key, 11), (TOKENS, D), 1.0, 6.0).astype(jnp.bfloat16)


def draw_encoder(key, part):
    return bounded_normal(jax.random.fold_in(key, 12), (ENC_TOKENS, D), 1.0, 6.0).astype(jnp.bfloat16)


def draw_selfbias(key, part):
    return bounded_normal(jax.random.fold_in(key, 13), (2, D), 0.05, 0.3)


def draw_crossbias(key, part):
    return bounded_normal(jax.random.fold_in(key, 14), (2, D), 0.05, 0.3)


def block_scale(key, extent, split, low, high):
    gain = 1.0
    for position, parts in split:
        draws = jax.random.uniform(jax.random.fold_in(jax.random.fold_in(key, 6), position), (parts,), jnp.float32, low / len(split), high / len(split))
        gain = gain * jnp.repeat(jnp.exp(draws), extent[position] // parts).reshape((-1,) + (1,) * (len(extent) - 1 - position))
    return gain


def bell_draw(own_key, dims, deviation, reach, cuts=(), kind=jnp.bfloat16):
    array = deviation * jax.random.normal(own_key, dims, jnp.float32)
    if cuts:
        array = array * block_scale(own_key, dims, cuts, -0.22, 0.18)
    return jnp.clip(array, -reach, reach).astype(kind)


def setup_inputs(seed: int = 0) -> dict:
    streams_of = jax.random.split(jax.random.key(seed), 20)
    return {
        "tokens": draw_tokens(jax.random.fold_in(streams_of[19], 71), 0),
        "encoder": draw_encoder(jax.random.fold_in(streams_of[19], 71), 0),
        "cotangent": bell_draw(streams_of[2], (TOKENS, D), 1.0, 6.0, ((0, 8), (1, 4))),
        "prefixes": jax.random.randint(streams_of[3], (SEQS,), SEQ_LEN // 10, SEQ_LEN // 2 + 1).astype(jnp.int32),
        "selfqkv": bell_draw(streams_of[4], (D, 3, D), D ** -0.5, 0.1875, ((0, 4), (2, 4))),
        "selfbias": draw_selfbias(jax.random.fold_in(streams_of[19], 71), 0),
        "selfproj": bell_draw(streams_of[6], (D, D), 4 ** -0.5, 3.0, ((0, 4), (1, 4))),
        "selfshift": bell_draw(streams_of[7], (D,), 0.2, 3.0, ((0, 4),), jnp.float32),
        "crossquery": bell_draw(streams_of[8], (D, D), D ** -0.5, 0.1875, ((0, 4), (1, 4))),
        "crosskv": bell_draw(streams_of[9], (D, 2, D), D ** -0.5, 0.1875, ((0, 4), (2, 4))),
        "crossbias": draw_crossbias(jax.random.fold_in(streams_of[19], 71), 0),
        "crossproj": bell_draw(streams_of[11], (D, D), 2 ** -0.5, 4.0, ((0, 4), (1, 4))),
        "crossshift": bell_draw(streams_of[12], (D,), 0.2, 3.0, ((0, 4),), jnp.float32),
        "upweight": bell_draw(streams_of[13], (D, FF), D ** -0.5, 0.1875, ((0, 4), (1, 4))),
        "upbias": bell_draw(streams_of[14], (FF,), 0.5, 6.0, ((0, 4),), jnp.float32),
        "downweight": bell_draw(streams_of[15], (FF, D), FF ** -0.5, 0.09375, ((0, 4), (1, 4))),
        "downbias": bell_draw(streams_of[16], (D,), 0.2, 3.0, ((0, 4),), jnp.float32),
        "normgain": jnp.clip(1.0 + 0.1 * jax.random.normal(streams_of[17], (3, D), jnp.float32), 0.5, 1.5),
        "normshift": bell_draw(streams_of[18], (3, D), 0.2, 3.0, ((1, 4),), jnp.float32),
    }


@jax.custom_vjp
def low(v):
    return lax.optimization_barrier(v.astype(jnp.bfloat16)).astype(jnp.float32)

@jax.custom_vjp
def low_back(v):
    return v

def low_keep(v):
    return (low(v), None)

def low_pass(kept, grad):
    return (grad,)

def back_keep(v):
    return (v, None)

def back_low(kept, grad):
    return (low(grad),)
low.defvjp(low_keep, low_pass)
low_back.defvjp(back_keep, back_low)

def matmul(left_side, right_side):
    return jnp.dot(left_side, right_side, precision=lax.Precision.HIGHEST, preferred_element_type=jnp.float32)

def normalize(hidden, gain_row, shift_row):
    average = lax.optimization_barrier(jnp.mean(hidden, axis=-1, keepdims=True))
    square = lax.optimization_barrier(jnp.mean(hidden * hidden, axis=-1, keepdims=True))
    inverse = lax.rsqrt(square - average * average + 1e-05)
    return (hidden - average) * inverse * gain_row + shift_row

def one_head(queries, key_set, value_set, allowed):
    scores = low_back(matmul(queries, key_set.T))
    scores = jnp.where(allowed, scores, -1e+30)
    row_peak = lax.optimization_barrier(jnp.max(scores, axis=-1, keepdims=True))
    exponent = jnp.exp(scores - row_peak)
    probability = exponent / lax.optimization_barrier(jnp.sum(exponent, axis=-1, keepdims=True))
    return matmul(low(probability), value_set)

def split_heads(matrix):
    return matrix.reshape(matrix.shape[0], HEADS, HD).transpose(1, 0, 2)

def attend_sequence(queries, key_set, value_set, limit_len, masked):
    length_q = queries.shape[0]
    length_k = key_set.shape[0]
    if masked:
        query_pos = jnp.arange(length_q, dtype=jnp.int32)[:, None]
        key_pos = jnp.arange(length_k, dtype=jnp.int32)[None, :]
        allowed = (key_pos < limit_len) | (key_pos <= query_pos)
    else:
        allowed = jnp.ones((length_q, length_k), dtype=jnp.bool_)

    def head_fn(packed):
        return one_head(packed[0], packed[1], packed[2], allowed)
    by_head = lax.map(jax.checkpoint(head_fn), (split_heads(queries), split_heads(key_set), split_heads(value_set)))
    return by_head.transpose(1, 0, 2).reshape(length_q, HEADS * HD)

def attend_all(queries, key_set, value_set, prefixes, masked):
    sequences = prefixes.shape[0]

    def per_sequence(packed):
        return attend_sequence(packed[0], packed[1], packed[2], packed[3], masked)
    stacked = lax.map(per_sequence, (queries.reshape(sequences, -1, queries.shape[1]), key_set.reshape(sequences, -1, key_set.shape[1]), value_set.reshape(sequences, -1, value_set.shape[1]), prefixes))
    return stacked.reshape(queries.shape)

def layer(tokens, encoder, selfqkv, selfbias, selfproj, selfshift, crossquery, crosskv, crossbias, crossproj, crossshift, upweight, upbias, downweight, downbias, normgain, normshift, prefixes):
    query_scale = HD ** (-0.5)
    mixed = matmul(tokens, selfqkv.reshape(D, 3 * D)).reshape(-1, 3, D)
    queries = low(low_back((mixed[:, 0] + selfbias[0]) * query_scale))
    key_set = low(low_back(mixed[:, 1]))
    value_set = low(low_back(mixed[:, 2] + selfbias[1]))
    attended = low(low_back(attend_all(queries, key_set, value_set, prefixes, True)))
    first = normalize(tokens + low_back(matmul(attended, selfproj) + selfshift), normgain[0], normshift[0])
    cross_queries = low(low_back((matmul(low(first), crossquery) + crossbias[0]) * query_scale))
    encoded = matmul(encoder, crosskv.reshape(D, 2 * D)).reshape(-1, 2, D)
    cross_keys = low(low_back(encoded[:, 0]))
    cross_values = low(low_back(encoded[:, 1] + crossbias[1]))
    crossed = low(low_back(attend_all(cross_queries, cross_keys, cross_values, prefixes, False)))
    second = normalize(first + low_back(matmul(crossed, crossproj) + crossshift), normgain[1], normshift[1])
    hidden_pre = low_back(matmul(low(second), upweight) + upbias)
    hidden_act = low(jax.nn.gelu(hidden_pre, approximate=False))
    feed = low_back(matmul(hidden_act, downweight) + downbias)
    return normalize(second + feed, normgain[2], normshift[2])

def reference(tokens, encoder, cotangent, prefixes, selfqkv, selfbias, selfproj, selfshift, crossquery, crosskv, crossbias, crossproj, crossshift, upweight, upbias, downweight, downbias, normgain, normshift):
    floats = (tokens.astype(jnp.float32), encoder.astype(jnp.float32), selfqkv.astype(jnp.float32), selfbias.astype(jnp.float32), selfproj.astype(jnp.float32), selfshift.astype(jnp.float32), crossquery.astype(jnp.float32), crosskv.astype(jnp.float32), crossbias.astype(jnp.float32), crossproj.astype(jnp.float32), crossshift.astype(jnp.float32), upweight.astype(jnp.float32), upbias.astype(jnp.float32), downweight.astype(jnp.float32), downbias.astype(jnp.float32), normgain.astype(jnp.float32), normshift.astype(jnp.float32))

    def forward(*params):
        return layer(*params, prefixes)
    layer_out, pullback = jax.vjp(forward, *floats)
    grads = pullback(cotangent.astype(jnp.float32))
    return (layer_out.astype(jnp.bfloat16), grads[0], grads[1], grads[2], grads[3], grads[4], grads[5], grads[6], grads[7], grads[8], grads[9], grads[10], grads[11], grads[12], grads[13], grads[14], grads[15], grads[16])
```

```python
import functools
import jax
import jax.numpy as jnp
from jax import lax
from jax.experimental import pallas as pl
from jax.experimental.pallas import tpu as pltpu
from jax.sharding import Mesh
from jax.sharding import PartitionSpec as P

HD = 64
NEGATIVE = -1e30
F32 = jnp.float32
BF16 = jnp.bfloat16


def dot_nn(a, b):
    return lax.dot_general(a, b, (((1,), (0,)), ((), ())), preferred_element_type=F32)


def allowed_mask(first_key, first_query, prefix, shape):
    key_pos = first_key + lax.broadcasted_iota(jnp.int32, shape, 0)
    query_pos = first_query + lax.broadcasted_iota(jnp.int32, shape, 1)
    return (key_pos < prefix) | (key_pos <= query_pos)


def forward_kernel(masked, bq, bk, prefix_ref, q_ref, k_ref, v_ref, o_ref, low_ref, lse_ref, keys, values, acc, peak):
    chunks, _, chunk = k_ref.shape
    per = chunk // bk
    blocks = chunks * per
    step = pl.program_id(0)
    prefix = prefix_ref[0]

    @pl.when(step == 0)
    def _():
        for c in range(chunks):
            for b in range(per):
                i = c * per + b
                keys[i] = k_ref[c, :, b * bk:(b + 1) * bk].T
                values[i, :HD, :] = v_ref[c, :, b * bk:(b + 1) * bk]
                rows = lax.broadcasted_iota(jnp.int32, (16, bk), 0)
                values[i, HD:, :] = jnp.where(rows == 0, 1.0, 0.0).astype(BF16)

    first_query = step * bq
    query = q_ref[0]
    peak[...] = jnp.full(peak.shape, NEGATIVE, F32)
    acc[...] = jnp.zeros(acc.shape, F32)

    def visit(i, use_mask):
        scores = dot_nn(keys[i], query)
        if use_mask:
            scores = jnp.where(allowed_mask(i * bk, first_query, prefix, scores.shape), scores, NEGATIVE)
        old = peak[...]
        new = jnp.maximum(old, jnp.max(scores, axis=0, keepdims=True))
        weight = jnp.exp(scores - new).astype(BF16)
        acc[...] = acc[...] * jnp.exp(old - new) + dot_nn(values[i], weight)
        peak[...] = new

    if masked:
        full = jnp.maximum(prefix, first_query + 1) // bk
        stop = (jnp.maximum(prefix, first_query + bq) + bk - 1) // bk
        lax.fori_loop(0, full, lambda i, c: (visit(i, False), c)[1], 0)
        lax.fori_loop(full, stop, lambda i, c: (visit(i, True), c)[1], 0)
    else:
        lax.fori_loop(0, blocks, lambda i, c: (visit(i, False), c)[1], 0)
    total = acc[HD:HD + 1, :]
    out = acc[:HD, :] / total
    o_ref[0] = out
    low_ref[0] = out.astype(BF16)
    lse_ref[0] = peak[...] + jnp.log(total)


def flash_forward(prefix, queries, q_part, pairs, k_part, v_part, masked, bq=1024, bk=1024):
    chunks, _, chunk = queries.shape
    length = chunks * chunk
    per = chunk // bq
    whole = lambda part: pl.BlockSpec((chunks, HD, chunk), lambda i, p: (0, part, 0))
    mine = lambda rows: pl.BlockSpec((1, rows, bq), lambda i, p: (i // per, 0, i % per))
    return pl.pallas_call(
        functools.partial(forward_kernel, masked, bq, bk),
        out_shape=(
            jax.ShapeDtypeStruct((chunks, HD, chunk), F32),
            jax.ShapeDtypeStruct((chunks, HD, chunk), BF16),
            jax.ShapeDtypeStruct((chunks, 1, chunk), F32),
        ),
        grid_spec=pltpu.PrefetchScalarGridSpec(
            num_scalar_prefetch=1,
            grid=(length // bq,),
            in_specs=[
                pl.BlockSpec((1, HD, bq), lambda i, p: (i // per, q_part, i % per)),
                whole(k_part),
                whole(v_part),
            ],
            out_specs=[mine(HD), mine(HD), mine(1)],
            scratch_shapes=[
                pltpu.VMEM((length // bk, bk, HD), BF16),
                pltpu.VMEM((length // bk, HD + 16, bk), BF16),
                pltpu.VMEM((HD + 16, bq), F32),
                pltpu.VMEM((1, bq), F32),
            ],
        ),
        cost_estimate=pl.CostEstimate(
            flops=4 * HD * length * length, transcendentals=length * length, bytes_accessed=14 * HD * length
        ),
        name="attend_self" if masked else "attend_cross",
    )(prefix, queries, pairs, pairs)


def backward_kernel(masked, bq, bk, prefix_ref, q_ref, g_ref, o_ref, lse_ref, k_ref, v_ref,
                    dq_ref, dk_ref, dv_ref, rows_q, rows_g, delta, dq_acc, dk_acc, dv_acc):
    chunks, _, chunk = q_ref.shape
    per = chunk // bq
    blocks = chunks * per
    step = pl.program_id(0)
    prefix = prefix_ref[0]

    @pl.when(step == 0)
    def _():
        for c in range(chunks):
            for b in range(per):
                i = c * per + b
                at = slice(b * bq, (b + 1) * bq)
                grad = g_ref[c, :, at]
                rows_q[i] = q_ref[c, :, at].T
                rows_g[i] = grad.T
                delta[i] = jnp.sum(grad.astype(F32) * o_ref[c, :, at], axis=0, keepdims=True)
        dq_acc[...] = jnp.zeros(dq_acc.shape, F32)

    first_key = step * bk
    key_cols = k_ref[0]
    key_rows = key_cols.T
    value_rows = v_ref[0].T
    dk_acc[...] = jnp.zeros(dk_acc.shape, F32)
    dv_acc[...] = jnp.zeros(dv_acc.shape, F32)

    def visit(i, use_mask):
        c, at = i // per, pl.ds(pl.multiple_of((i % per) * bq, bq), bq)
        scores = dot_nn(key_rows, q_ref[c, :, at])
        if use_mask:
            scores = jnp.where(allowed_mask(first_key, i * bq, prefix, scores.shape), scores, NEGATIVE)
        probs = jnp.exp(scores - lse_ref[c, :, at])
        dprobs = dot_nn(value_rows, g_ref[c, :, at])
        dscore = (probs * (dprobs - delta[i])).astype(BF16)
        dv_acc[...] += dot_nn(probs.astype(BF16), rows_g[i])
        dk_acc[...] += dot_nn(dscore, rows_q[i])
        dq_acc[i] += dot_nn(key_cols, dscore)

    if masked:
        inside = first_key + bk <= prefix
        start = jnp.where(first_key < prefix, 0, first_key // bq)
        free = jnp.where(inside, 0, jnp.minimum((first_key + bk - 1 + bq - 1) // bq, blocks))
        lax.fori_loop(start, free, lambda i, c: (visit(i, True), c)[1], 0)
        lax.fori_loop(jnp.maximum(start, free), blocks, lambda i, c: (visit(i, False), c)[1], 0)
    else:
        lax.fori_loop(0, blocks, lambda i, c: (visit(i, False), c)[1], 0)
    dk_ref[0] = dk_acc[...].T.astype(BF16)
    dv_ref[0] = dv_acc[...].T.astype(BF16)

    @pl.when(step == pl.num_programs(0) - 1)
    def _():
        for c in range(chunks):
            for b in range(per):
                low = dq_acc[c * per + b].astype(BF16)
                dq_ref[c, :, b * bq:(b + 1) * bq] = low * jnp.asarray(HD ** -0.5, BF16)


def flash_backward(prefix, queries, q_part, pairs, k_part, v_part, grads, outputs, lse, masked, bq=1024, bk=1024):
    chunks, _, chunk = queries.shape
    length = chunks * chunk
    per = chunk // bk
    whole = lambda part, rows=HD: pl.BlockSpec((chunks, rows, chunk), lambda i, p: (0, part, 0))
    mine = lambda part: pl.BlockSpec((1, HD, bk), lambda i, p: (i // per, part, i % per))
    shape = jax.ShapeDtypeStruct((chunks, HD, chunk), BF16)
    return pl.pallas_call(
        functools.partial(backward_kernel, masked, bq, bk),
        out_shape=(shape, shape, shape),
        grid_spec=pltpu.PrefetchScalarGridSpec(
            num_scalar_prefetch=1,
            grid=(length // bk,),
            in_specs=[whole(q_part), whole(0), whole(0), whole(0, 1), mine(k_part), mine(v_part)],
            out_specs=[whole(0), mine(0), mine(0)],
            scratch_shapes=[
                pltpu.VMEM((length // bq, bq, HD), BF16),
                pltpu.VMEM((length // bq, bq, HD), BF16),
                pltpu.VMEM((length // bq, 1, bq), F32),
                pltpu.VMEM((length // bq, HD, bq), F32),
                pltpu.VMEM((bk, HD), F32),
                pltpu.VMEM((bk, HD), F32),
            ],
        ),
        cost_estimate=pl.CostEstimate(
            flops=10 * HD * length * length, transcendentals=length * length, bytes_accessed=20 * HD * length
        ),
        name="attend_self_back" if masked else "attend_cross_back",
    )(prefix, queries, grads, outputs, lse, pairs, pairs)


EPSILON = 1e-05
SCALE = HD ** -0.5


def contract(left, right, left_dim, right_dim):
    return lax.dot_general(
        left, right, (((left_dim,), (right_dim,)), ((), ())), preferred_element_type=F32
    )


class Layout:
    def __init__(self, sizes):
        self.sizes = sizes
        keep = lambda names: tuple(n for n in names if sizes[n] > 1) or names[-1:]
        self.team = ("rx", "rc")
        self.cols = keep(("sq", "cs"))
        self.ring = keep(("rb", "cs"))
        self.every = ("dp", "rb", "rx", "rc", "sq", "cs")

    def count(self, names):
        total = 1
        for name in names:
            total *= self.sizes[name]
        return total

    def me(self):
        return lax.axis_index("rx") * 2 + lax.axis_index("rc")

    def swap(self, value, bits):
        if bits == 1:
            return lax.ppermute(value, "rc", [(0, 1), (1, 0)])
        if bits == 2:
            return lax.ppermute(value, "rx", [(0, 1), (1, 0)])
        return lax.ppermute(value, self.team, [(i, i ^ 3) for i in range(4)])

    def place(self, parts, spots):
        out = jnp.zeros((len(parts),) + parts[0].shape, parts[0].dtype)
        for part, spot in zip(parts, spots):
            out = lax.dynamic_update_index_in_dim(out, part, spot, 0)
        return out

    def team_gather(self, value):
        me = self.me()
        core, across = self.swap(value, 1), self.swap(value, 2)
        diagonal = self.swap(across, 1)
        return self.place([value, core, across, diagonal], [me, me ^ 1, me ^ 2, me ^ 3])

    def team_exchange(self, blocks):
        me = self.me()
        pick = lambda bits: lax.dynamic_index_in_dim(blocks, me ^ bits, 0, keepdims=False)
        parts = [pick(0)] + [self.swap(pick(bits), bits) for bits in (1, 2, 3)]
        return self.place(parts, [me, me ^ 1, me ^ 2, me ^ 3])

    def team_reduce(self, blocks):
        rx, rc = lax.axis_index("rx"), lax.axis_index("rc")
        grid = blocks.reshape((2, 2) + blocks.shape[1:])
        away = lax.dynamic_index_in_dim(grid, 1 - rc, 1, keepdims=False).astype(BF16)
        home = lax.dynamic_index_in_dim(grid, rc, 1, keepdims=False) + self.swap(away, 1).astype(F32)
        away = lax.dynamic_index_in_dim(home, 1 - rx, 0, keepdims=False).astype(BF16)
        return lax.dynamic_index_in_dim(home, rx, 0, keepdims=False) + self.swap(away, 2).astype(F32)

    def ring_index(self):
        return lax.axis_index("cs") * self.sizes["rb"] + lax.axis_index("rb")

    def flip(self, blocks, first, second):
        first, second = self.sizes[first], self.sizes[second]
        if first == 1 or second == 1:
            return blocks
        return blocks.reshape((first, second) + blocks.shape[1:]).swapaxes(0, 1).reshape(blocks.shape)

    def ring_exchange(self, blocks):
        blocks = lax.all_to_all(self.flip(blocks, "cs", "rb"), self.ring, 0, 0, tiled=True)
        return self.flip(blocks, "rb", "cs")

    def ring_trickle(self, blocks):
        size = self.count(self.ring)
        me = lax.axis_index(self.ring)
        blocks = self.flip(blocks, "cs", "rb")
        pick = lambda step: lax.dynamic_index_in_dim(blocks, (me + step) % size, 0, keepdims=False)
        parts, spots = [pick(0)], [me]
        for step in range(1, size):
            parts.append(lax.ppermute(pick(step), self.ring, [(i, (i + step) % size) for i in range(size)]))
            spots.append((me + size - step) % size)
        return self.flip(self.place(parts, spots), "rb", "cs")

    def block_sum(self, value):
        return lax.psum_scatter(value, self.cols, scatter_dimension=0, tiled=True)

    def halves(self, value):
        if self.sizes["rb"] == 1:
            return value
        return lax.all_to_all(value, "rb", 0, 1, tiled=True)

    def unhalves(self, value):
        if self.sizes["rb"] == 1:
            return value
        return lax.all_to_all(value, "rb", 1, 0, tiled=True)

    def feature_blocks(self, value):
        rb = self.sizes["rb"]
        parts = value.reshape(value.shape[0], rb, 4, -1).transpose(2, 0, 1, 3)
        return parts.reshape(4, value.shape[0], -1)

    def join_features(self, blocks):
        rb = self.sizes["rb"]
        count = blocks.shape[1]
        return blocks.reshape(4, count, rb, -1).transpose(1, 2, 0, 3).reshape(count, -1)

    def weight(self, blocks):
        mine = self.team_exchange(blocks).transpose(1, 0, 2)
        mine = mine.reshape(mine.shape[0], -1)
        if self.sizes["rb"] > 1:
            mine = lax.all_gather(mine, "rb", axis=1, tiled=True)
        return lax.all_gather(mine, self.cols, axis=0, tiled=True)

    def weight_grad(self, partial):
        total = self.block_sum(partial.astype(BF16))
        if self.sizes["rb"] > 1:
            total = lax.psum_scatter(total, "rb", scatter_dimension=1, tiled=True)
        blocks = total.reshape(total.shape[0], 4, -1).transpose(1, 0, 2)
        low = self.team_exchange(blocks)
        if self.sizes["dp"] == 2:
            return low.astype(F32) + lax.ppermute(low, "dp", [(0, 1), (1, 0)]).astype(F32)
        return lax.psum(low.astype(F32), "dp")


def norm_forward(hidden, gain_row, shift_row):
    average = jnp.mean(hidden, axis=1, keepdims=True)
    square = jnp.mean(hidden * hidden, axis=1, keepdims=True)
    inverse = lax.rsqrt(square - average * average + EPSILON)
    normed = (hidden - average) * inverse
    return normed * gain_row + shift_row, normed, inverse


def norm_backward(upstream, normed, inverse, gain_row):
    scaled = upstream * gain_row
    first = jnp.mean(scaled, axis=1, keepdims=True)
    second = jnp.mean(scaled * normed, axis=1, keepdims=True)
    grad = inverse * (scaled - first - normed * second)
    return grad, jnp.sum(upstream * normed, axis=0), jnp.sum(upstream, axis=0)


def exact_gelu(inputs):
    return jax.nn.gelu(inputs, approximate=False)


def column_rows(weight):
    features, parts, width = weight.shape
    blocks = weight.reshape(features, parts, 4, width // 4).transpose(2, 1, 3, 0)
    return blocks.reshape(4, -1, features)


def column_rows_back(blocks, parts):
    features = blocks.shape[2]
    return blocks.reshape(4, parts, -1, features).transpose(3, 1, 0, 2).reshape(features, parts, -1)


def shards(
    layout, tokens, encoder, cotangent, prefixes, selfqkv, selfbias, selfproj, selfshift, crossquery,
    crosskv, crossbias, crossproj, crossshift, upweight, upbias, downweight, downbias, normgain, normshift,
):
    me = layout.me()
    split_rows = lambda weight: weight.reshape(4, -1, weight.shape[1])
    qkv_w = layout.weight(column_rows(selfqkv))
    tokens_all = layout.join_features(layout.team_gather(layout.halves(tokens)))
    width = tokens_all.shape[1]
    group = tokens_all.shape[0]
    own_rows = group // 4
    columns = layout.count(layout.cols)
    heads = columns

    by_col = jnp.concatenate([selfbias.reshape(-1), crossbias.reshape(-1), upbias])
    by_col = lax.all_gather(by_col, layout.cols, axis=0, tiled=False).reshape(columns, -1)
    block = selfbias.shape[1]
    head_biases = lax.dynamic_index_in_dim(
        by_col[:, : 4 * block].reshape(columns, 4, 4, HD), me, 2, keepdims=False
    )
    up_bias = lax.dynamic_index_in_dim(
        by_col[:, 4 * block:].reshape(columns, 4, -1), me, 1, keepdims=False
    ).reshape(1, -1)
    by_row = jnp.concatenate([selfshift[None], crossshift[None], downbias[None], normgain, normshift])
    by_row = lax.all_gather(by_row, ("rb", "rx", "rc"), axis=1, tiled=True)
    self_shift, cross_shift, down_bias = by_row[0], by_row[1], by_row[2]
    gains, shifts = by_row[3:6], by_row[6:9]

    def gather_tokens(own):
        return layout.team_gather(own).reshape(group, width)

    def reduce_tokens(partial):
        return layout.team_reduce(partial.reshape(4, own_rows, width))

    sequence_prefix = prefixes
    if layout.sizes["sq"] > 1:
        sequence_prefix = lax.dynamic_slice_in_dim(prefixes, lax.axis_index("sq"), 1, 0)

    qkv = contract(qkv_w, tokens_all, 1, 1).reshape(heads, 3, HD, group)
    qkv_bias = jnp.stack([head_biases[:, 0], jnp.zeros_like(head_biases[:, 0]), head_biases[:, 1]], axis=1)
    factor = jnp.array([SCALE, 1.0, 1.0], F32)[None, :, None, None]
    qkv = ((qkv + qkv_bias[..., None]) * factor).astype(BF16).reshape(heads, 3 * HD, group)
    self_set = layout.ring_exchange(qkv)
    self_out, self_low, self_lse = flash_forward(sequence_prefix, self_set, 0, self_set, 1, 2, True)
    attended = layout.ring_exchange(self_low).reshape(heads * HD, group)

    self_w = layout.weight(split_rows(selfproj))
    encoder_all = layout.join_features(layout.team_gather(layout.halves(encoder)))
    kv_w = layout.weight(column_rows(crosskv))
    query_w = layout.weight(column_rows(crossquery[:, None]))
    cross_w = layout.weight(split_rows(crossproj))
    up_w = layout.weight(column_rows(upweight[:, None]))
    down_w = layout.weight(split_rows(downweight))
    pair = contract(kv_w, encoder_all, 1, 1).reshape(heads, 2, HD, group)
    pair_bias = jnp.stack([jnp.zeros_like(head_biases[:, 3]), head_biases[:, 3]], axis=1)
    pair = (pair + pair_bias[..., None]).astype(BF16).reshape(heads, 2 * HD, group)
    cross_set = layout.ring_trickle(pair)
    upstream = layout.join_features(
        layout.team_exchange(layout.halves(cotangent).reshape(4, own_rows, -1))
    ).astype(F32)

    own_tokens = lax.dynamic_slice_in_dim(tokens_all, me * own_rows, own_rows, 0).astype(F32)
    first_sum = own_tokens + (reduce_tokens(contract(attended, self_w, 0, 0)) + self_shift)
    first_out, first_normed, first_inverse = norm_forward(first_sum, gains[0], shifts[0])
    first_all = gather_tokens(first_out.astype(BF16))

    query = contract(query_w, first_all, 1, 1).reshape(heads, HD, group)
    query = ((query + head_biases[:, 2][..., None]) * SCALE).astype(BF16)
    cross_query = layout.ring_exchange(query)
    cross_out, cross_low, cross_lse = flash_forward(sequence_prefix, cross_query, 0, cross_set, 0, 1, False)
    crossed = layout.ring_exchange(cross_low).reshape(heads * HD, group)
    second_sum = first_out + (reduce_tokens(contract(crossed, cross_w, 0, 0)) + cross_shift)
    second_out, second_normed, second_inverse = norm_forward(second_sum, gains[1], shifts[1])
    second_all = gather_tokens(second_out.astype(BF16))

    hidden_pre = contract(second_all, up_w, 1, 1) + up_bias
    hidden_act = exact_gelu(hidden_pre).astype(BF16)
    third_sum = second_out + (reduce_tokens(contract(hidden_act, down_w, 1, 0)) + down_bias)
    third_out, third_normed, third_inverse = norm_forward(third_sum, gains[2], shifts[2])
    layer_out = third_out.astype(BF16)
    layer_out = layout.team_exchange(layout.feature_blocks(layer_out))
    layer_out = layout.unhalves(layer_out.reshape(group, -1))

    third_grad, third_gain, third_shift = norm_backward(upstream, third_normed, third_inverse, gains[2])
    down_own = third_grad.astype(BF16)
    down_all = gather_tokens(down_own)
    act_grad = contract(down_all, down_w, 1, 1)
    pre_low = jax.vjp(exact_gelu, hidden_pre)[1](act_grad)[0].astype(BF16)
    second_grad = third_grad + reduce_tokens(contract(pre_low, up_w, 1, 0))
    downweight_grad = layout.weight_grad(contract(hidden_act, down_all, 0, 0))
    upweight_grad = layout.weight_grad(contract(pre_low, second_all, 0, 0))
    mid_grad, second_gain, second_shift = norm_backward(second_grad, second_normed, second_inverse, gains[1])
    cross_own = mid_grad.astype(BF16)
    cross_all = gather_tokens(cross_own)
    crossed_grad = contract(cross_w, cross_all, 1, 1).astype(BF16).reshape(heads, HD, group)
    crossed_grad = layout.ring_exchange(crossed_grad)
    crossproj_grad = layout.weight_grad(contract(crossed, cross_all, 1, 0))
    dquery, dkeys, dvalues = flash_backward(
        sequence_prefix, cross_query, 0, cross_set, 0, 1, crossed_grad, cross_out, cross_lse, False
    )
    cross_bias_sums = (jnp.sum(dquery.astype(F32), axis=(0, 2)), jnp.sum(dvalues.astype(F32), axis=(0, 2)))
    dquery = layout.ring_exchange(dquery).reshape(heads * HD, group)
    first_grad = mid_grad + reduce_tokens(contract(dquery, query_w, 0, 0))
    dpair = layout.ring_trickle(jnp.concatenate([dkeys, dvalues], axis=1)).reshape(heads * 2 * HD, group)
    crossquery_grad = layout.weight_grad(contract(dquery, first_all, 1, 0))
    crosskv_grad = layout.weight_grad(contract(dpair, encoder_all, 1, 0))
    encoder_grad = layout.team_reduce(layout.feature_blocks(contract(dpair, kv_w, 0, 0)))
    encoder_grad = layout.unhalves(encoder_grad)
    low_grad, first_gain, first_shift = norm_backward(first_grad, first_normed, first_inverse, gains[0])
    self_own = low_grad.astype(BF16)
    self_all = gather_tokens(self_own)
    attended_grad = contract(self_w, self_all, 1, 1).astype(BF16).reshape(heads, HD, group)
    attended_grad = layout.ring_exchange(attended_grad)
    selfproj_grad = layout.weight_grad(contract(attended, self_all, 1, 0))
    dq, dk, dv = flash_backward(
        sequence_prefix, self_set, 0, self_set, 1, 2, attended_grad, self_out, self_lse, True
    )
    self_bias_sums = (jnp.sum(dq.astype(F32), axis=(0, 2)), jnp.sum(dv.astype(F32), axis=(0, 2)))
    dqkv = layout.ring_exchange(jnp.concatenate([dq, dk, dv], axis=1)).reshape(heads * 3 * HD, group)
    selfqkv_grad = layout.weight_grad(contract(dqkv, tokens_all, 1, 0))
    tokens_part = contract(dqkv, qkv_w, 0, 0)
    mine = lax.dynamic_slice_in_dim(tokens_part, me * own_rows, own_rows, 0) + low_grad
    tokens_part = lax.dynamic_update_slice_in_dim(tokens_part, mine, me * own_rows, 0)
    tokens_grad = layout.unhalves(layout.team_reduce(layout.feature_blocks(tokens_part)))

    def at_head(sums):
        spot = (layout.ring_index() * 4 + me) * HD
        return lax.dynamic_update_slice_in_dim(jnp.zeros((width,), F32), sums, spot, 0)

    up_sums = jnp.zeros((columns, 4, pre_low.shape[1] // columns), F32)
    up_sums = lax.dynamic_update_index_in_dim(
        up_sums, jnp.sum(pre_low.astype(F32), axis=0).reshape(columns, -1), me, 1
    )
    column_sum = lambda low: jnp.sum(low.astype(F32), axis=0)
    rows = jnp.stack([
        first_gain, second_gain, third_gain, first_shift, second_shift, third_shift,
        column_sum(self_own), column_sum(cross_own), column_sum(down_own),
        at_head(cross_bias_sums[0]), at_head(cross_bias_sums[1]),
    ])
    rows, up_sums = lax.psum((rows, up_sums), layout.every)
    late = lax.psum(jnp.stack([at_head(self_bias_sums[0]), at_head(self_bias_sums[1])]), layout.every)
    row_at = (lax.axis_index("rb") * 4 + me) * normgain.shape[1]
    col_at = lax.axis_index(layout.cols)
    by_row = lax.dynamic_slice_in_dim(rows[:9], row_at, normgain.shape[1], 1)
    crossbias_grad = lax.dynamic_slice_in_dim(rows[9:], col_at * block, block, 1)
    selfbias_grad = lax.dynamic_slice_in_dim(late, col_at * block, block, 1)
    upbias_grad = lax.dynamic_index_in_dim(up_sums, col_at, 0, keepdims=False).reshape(-1)
    join_rows = lambda blocks: blocks.reshape(-1, blocks.shape[2])
    return (
        layer_out,
        tokens_grad,
        encoder_grad,
        column_rows_back(selfqkv_grad, 3),
        selfbias_grad,
        join_rows(selfproj_grad),
        by_row[6],
        column_rows_back(crossquery_grad, 1)[:, 0],
        column_rows_back(crosskv_grad, 2),
        crossbias_grad,
        join_rows(crossproj_grad),
        by_row[7],
        column_rows_back(upweight_grad, 1)[:, 0],
        upbias_grad,
        join_rows(downweight_grad),
        by_row[8],
        by_row[:3],
        by_row[3:6],
    )


def solution(mesh):
    def run(*arrays):
        dp, row, col = (mesh.shape[name] for name in ("dp", "row", "col"))
        per_col = arrays[4].shape[2] // HD // col
        seqs = arrays[3].shape[0] // dp
        assert per_col == 4 and row % 4 == 0 and col % seqs == 0
        assert (row // 4) * (col // seqs) == col
        sizes = {"dp": dp, "rb": row // 4, "rx": 2, "rc": 2, "sq": seqs, "cs": col // seqs}
        grid = Mesh(mesh.devices.reshape(tuple(sizes.values())), tuple(sizes))
        rows, cols, tokens = ("rb", "rx", "rc"), ("sq", "cs"), ("dp", "sq", "cs")
        specs = {
            "tokens": P(tokens, rows), "rc": P(rows, cols), "cr": P(cols, rows), "r3c": P(rows, None, cols),
            "c": P(cols), "r": P(rows), "2c": P(None, cols), "2r": P(None, rows),
        }
        ins = (
            "tokens", "tokens", "tokens", "dp", "r3c", "2c", "cr", "r", "rc", "r3c", "2c", "cr", "r", "rc", "c", "cr", "r", "2r", "2r",
        )
        outs = (
            "tokens", "tokens", "tokens", "r3c", "2c", "cr", "r", "rc", "r3c", "2c", "cr", "r", "rc", "c", "cr", "r", "2r", "2r",
        )
        specs["dp"] = P("dp")
        body = functools.partial(shards, Layout(sizes))
        return jax.shard_map(
            body, mesh=grid, in_specs=tuple(specs[s] for s in ins), out_specs=tuple(specs[s] for s in outs),
            check_vma=False,
        )(*arrays)

    return run
```

```python
import functools
import jax
import jax.numpy as jnp
from jax import lax
from jax.experimental import pallas as pl
from jax.experimental.pallas import tpu as pltpu
from jax.sharding import Mesh
from jax.sharding import PartitionSpec as P

HD = 64
NEGATIVE = -1e30
F32 = jnp.float32
BF16 = jnp.bfloat16


def dot_nn(a, b):
    return lax.dot_general(a, b, (((1,), (0,)), ((), ())), preferred_element_type=F32)


def allowed_mask(first_key, first_query, prefix, shape):
    key_pos = first_key + lax.broadcasted_iota(jnp.int32, shape, 0)
    query_pos = first_query + lax.broadcasted_iota(jnp.int32, shape, 1)
    return (key_pos < prefix) | (key_pos <= query_pos)


def forward_kernel(masked, bq, bk, prefix_ref, q_ref, k_ref, v_ref, o_ref, low_ref, lse_ref, keys, values, acc, peak):
    chunks, _, chunk = k_ref.shape
    per = chunk // bk
    blocks = chunks * per
    step = pl.program_id(0)
    prefix = prefix_ref[0]

    @pl.when(step == 0)
    def _():
        for c in range(chunks):
            for b in range(per):
                i = c * per + b
                keys[i] = k_ref[c, :, b * bk:(b + 1) * bk].T
                values[i, :HD, :] = v_ref[c, :, b * bk:(b + 1) * bk]
                rows = lax.broadcasted_iota(jnp.int32, (16, bk), 0)
                values[i, HD:, :] = jnp.where(rows == 0, 1.0, 0.0).astype(BF16)

    first_query = step * bq
    query = q_ref[0]
    peak[...] = jnp.full(peak.shape, NEGATIVE, F32)
    acc[...] = jnp.zeros(acc.shape, F32)

    def visit(i, use_mask):
        scores = dot_nn(keys[i], query)
        if use_mask:
            scores = jnp.where(allowed_mask(i * bk, first_query, prefix, scores.shape), scores, NEGATIVE)
        old = peak[...]
        new = jnp.maximum(old, jnp.max(scores, axis=0, keepdims=True))
        weight = jnp.exp(scores - new).astype(BF16)
        acc[...] = acc[...] * jnp.exp(old - new) + dot_nn(values[i], weight)
        peak[...] = new

    if masked:
        full = jnp.maximum(prefix, first_query + 1) // bk
        stop = (jnp.maximum(prefix, first_query + bq) + bk - 1) // bk
        lax.fori_loop(0, full, lambda i, c: (visit(i, False), c)[1], 0)
        lax.fori_loop(full, stop, lambda i, c: (visit(i, True), c)[1], 0)
    else:
        lax.fori_loop(0, blocks, lambda i, c: (visit(i, False), c)[1], 0)
    total = acc[HD:HD + 1, :]
    out = acc[:HD, :] / total
    o_ref[0] = out
    low_ref[0] = out.astype(BF16)
    lse_ref[0] = peak[...] + jnp.log(total)


def flash_forward(prefix, queries, q_part, pairs, k_part, v_part, masked, bq=1024, bk=1024):
    chunks, _, chunk = queries.shape
    length = chunks * chunk
    per = chunk // bq
    whole = lambda part: pl.BlockSpec((chunks, HD, chunk), lambda i, p: (0, part, 0))
    mine = lambda rows: pl.BlockSpec((1, rows, bq), lambda i, p: (i // per, 0, i % per))
    return pl.pallas_call(
        functools.partial(forward_kernel, masked, bq, bk),
        out_shape=(
            jax.ShapeDtypeStruct((chunks, HD, chunk), F32),
            jax.ShapeDtypeStruct((chunks, HD, chunk), BF16),
            jax.ShapeDtypeStruct((chunks, 1, chunk), F32),
        ),
        grid_spec=pltpu.PrefetchScalarGridSpec(
            num_scalar_prefetch=1,
            grid=(length // bq,),
            in_specs=[
                pl.BlockSpec((1, HD, bq), lambda i, p: (i // per, q_part, i % per)),
                whole(k_part),
                whole(v_part),
            ],
            out_specs=[mine(HD), mine(HD), mine(1)],
            scratch_shapes=[
                pltpu.VMEM((length // bk, bk, HD), BF16),
                pltpu.VMEM((length // bk, HD + 16, bk), BF16),
                pltpu.VMEM((HD + 16, bq), F32),
                pltpu.VMEM((1, bq), F32),
            ],
        ),
        cost_estimate=pl.CostEstimate(
            flops=4 * HD * length * length, transcendentals=length * length, bytes_accessed=14 * HD * length
        ),
        name="attend_self" if masked else "attend_cross",
    )(prefix, queries, pairs, pairs)


def backward_kernel(masked, bq, bk, prefix_ref, q_ref, g_ref, o_ref, lse_ref, k_ref, v_ref,
                    dq_ref, dk_ref, dv_ref, rows_q, rows_g, delta, dq_acc, dk_acc, dv_acc):
    chunks, _, chunk = q_ref.shape
    per = chunk // bq
    blocks = chunks * per
    step = pl.program_id(0)
    prefix = prefix_ref[0]

    @pl.when(step == 0)
    def _():
        for c in range(chunks):
            for b in range(per):
                i = c * per + b
                at = slice(b * bq, (b + 1) * bq)
                grad = g_ref[c, :, at]
                rows_q[i] = q_ref[c, :, at].T
                rows_g[i] = grad.T
                delta[i] = jnp.sum(grad.astype(F32) * o_ref[c, :, at], axis=0, keepdims=True)
        dq_acc[...] = jnp.zeros(dq_acc.shape, F32)

    first_key = step * bk
    key_cols = k_ref[0]
    key_rows = key_cols.T
    value_rows = v_ref[0].T
    dk_acc[...] = jnp.zeros(dk_acc.shape, F32)
    dv_acc[...] = jnp.zeros(dv_acc.shape, F32)

    def visit(i, use_mask):
        c, at = i // per, pl.ds(pl.multiple_of((i % per) * bq, bq), bq)
        scores = dot_nn(key_rows, q_ref[c, :, at])
        if use_mask:
            scores = jnp.where(allowed_mask(first_key, i * bq, prefix, scores.shape), scores, NEGATIVE)
        probs = jnp.exp(scores - lse_ref[c, :, at])
        dprobs = dot_nn(value_rows, g_ref[c, :, at])
        dscore = (probs * (dprobs - delta[i])).astype(BF16)
        dv_acc[...] += dot_nn(probs.astype(BF16), rows_g[i])
        dk_acc[...] += dot_nn(dscore, rows_q[i])
        dq_acc[i] += dot_nn(key_cols, dscore)

    if masked:
        inside = first_key + bk <= prefix
        start = jnp.where(first_key < prefix, 0, first_key // bq)
        free = jnp.where(inside, 0, jnp.minimum((first_key + bk - 1 + bq - 1) // bq, blocks))
        lax.fori_loop(start, free, lambda i, c: (visit(i, True), c)[1], 0)
        lax.fori_loop(jnp.maximum(start, free), blocks, lambda i, c: (visit(i, False), c)[1], 0)
    else:
        lax.fori_loop(0, blocks, lambda i, c: (visit(i, False), c)[1], 0)
    dk_ref[0] = dk_acc[...].T.astype(BF16)
    dv_ref[0] = dv_acc[...].T.astype(BF16)

    @pl.when(step == pl.num_programs(0) - 1)
    def _():
        for c in range(chunks):
            for b in range(per):
                low = dq_acc[c * per + b].astype(BF16)
                dq_ref[c, :, b * bq:(b + 1) * bq] = low * jnp.asarray(HD ** -0.5, BF16)


def flash_backward(prefix, queries, q_part, pairs, k_part, v_part, grads, outputs, lse, masked, bq=1024, bk=1024):
    chunks, _, chunk = queries.shape
    length = chunks * chunk
    per = chunk // bk
    whole = lambda part, rows=HD: pl.BlockSpec((chunks, rows, chunk), lambda i, p: (0, part, 0))
    mine = lambda part: pl.BlockSpec((1, HD, bk), lambda i, p: (i // per, part, i % per))
    shape = jax.ShapeDtypeStruct((chunks, HD, chunk), BF16)
    return pl.pallas_call(
        functools.partial(backward_kernel, masked, bq, bk),
        out_shape=(shape, shape, shape),
        grid_spec=pltpu.PrefetchScalarGridSpec(
            num_scalar_prefetch=1,
            grid=(length // bk,),
            in_specs=[whole(q_part), whole(0), whole(0), whole(0, 1), mine(k_part), mine(v_part)],
            out_specs=[whole(0), mine(0), mine(0)],
            scratch_shapes=[
                pltpu.VMEM((length // bq, bq, HD), BF16),
                pltpu.VMEM((length // bq, bq, HD), BF16),
                pltpu.VMEM((length // bq, 1, bq), F32),
                pltpu.VMEM((length // bq, HD, bq), F32),
                pltpu.VMEM((bk, HD), F32),
                pltpu.VMEM((bk, HD), F32),
            ],
        ),
        cost_estimate=pl.CostEstimate(
            flops=10 * HD * length * length, transcendentals=length * length, bytes_accessed=20 * HD * length
        ),
        name="attend_self_back" if masked else "attend_cross_back",
    )(prefix, queries, grads, outputs, lse, pairs, pairs)


EPSILON = 1e-05
SCALE = HD ** -0.5


def contract(left, right, left_dim, right_dim):
    return lax.dot_general(
        left, right, (((left_dim,), (right_dim,)), ((), ())), preferred_element_type=F32
    )


class Layout:
    def __init__(self, sizes):
        self.sizes = sizes
        keep = lambda names: tuple(n for n in names if sizes[n] > 1) or names[-1:]
        self.team = ("rx", "rc")
        self.cols = keep(("sq", "cs"))
        self.ring = keep(("rb", "cs"))
        self.every = ("dp", "rb", "rx", "rc", "sq", "cs")

    def count(self, names):
        total = 1
        for name in names:
            total *= self.sizes[name]
        return total

    def me(self):
        return lax.axis_index("rx") * 2 + lax.axis_index("rc")

    def swap(self, value, bits):
        if bits == 1:
            return lax.ppermute(value, "rc", [(0, 1), (1, 0)])
        if bits == 2:
            return lax.ppermute(value, "rx", [(0, 1), (1, 0)])
        return lax.ppermute(value, self.team, [(i, i ^ 3) for i in range(4)])

    def place(self, parts, spots):
        out = jnp.zeros((len(parts),) + parts[0].shape, parts[0].dtype)
        for part, spot in zip(parts, spots):
            out = lax.dynamic_update_index_in_dim(out, part, spot, 0)
        return lax.optimization_barrier(out)

    def spots(self):
        me = self.me()
        return [me, me ^ 1, me ^ 2, me ^ 3]

    def team_parts(self, value):
        core, across = self.swap(value, 1), self.swap(value, 2)
        return [value, core, across, self.swap(across, 1)]

    def pick(self, blocks):
        return [lax.dynamic_index_in_dim(blocks, spot, 0, keepdims=False) for spot in self.spots()]

    def team_send(self, parts):
        return [parts[0]] + [self.swap(parts[bits], bits) for bits in (1, 2, 3)]

    def team_total(self, parts):
        away = self.swap(jnp.stack([parts[1].astype(BF16), parts[3].astype(BF16)]), 1).astype(F32)
        away_across = self.swap((parts[2] + away[1]).astype(BF16), 2).astype(F32)
        return (parts[0] + away[0]) + away_across

    def total(self, value):
        for name in self.every:
            bits = 1
            while bits < self.sizes[name]:
                pairs = [(i, i ^ bits) for i in range(self.sizes[name])]
                value = value + lax.ppermute(value, name, pairs)
                bits *= 2
        return value

    def ring_index(self):
        return lax.axis_index("cs") * self.sizes["rb"] + lax.axis_index("rb")

    def flip(self, blocks, first, second):
        first, second = self.sizes[first], self.sizes[second]
        if first == 1 or second == 1:
            return blocks
        return blocks.reshape((first, second) + blocks.shape[1:]).swapaxes(0, 1).reshape(blocks.shape)

    def ring_exchange(self, blocks):
        blocks = lax.all_to_all(self.flip(blocks, "cs", "rb"), self.ring, 0, 0, tiled=True)
        return self.flip(blocks, "rb", "cs")

    def ring_trickle(self, blocks):
        size = self.count(self.ring)
        me = lax.axis_index(self.ring)
        blocks = self.flip(blocks, "cs", "rb")
        pick = lambda step: lax.dynamic_index_in_dim(blocks, (me + step) % size, 0, keepdims=False)
        parts, spots = [pick(0)], [me]
        for step in range(1, size):
            parts.append(lax.ppermute(pick(step), self.ring, [(i, (i + step) % size) for i in range(size)]))
            spots.append((me + size - step) % size)
        return self.flip(self.place(parts, spots), "rb", "cs")

    def block_sum(self, value):
        return lax.psum_scatter(value, self.cols, scatter_dimension=0, tiled=True)

    def halves(self, value):
        if self.sizes["rb"] == 1:
            return value
        return lax.all_to_all(value, "rb", 0, 1, tiled=True)

    def unhalves(self, value):
        if self.sizes["rb"] == 1:
            return value
        return lax.all_to_all(value, "rb", 1, 0, tiled=True)

    def feature_parts(self, value):
        width = value.shape[1] // 4
        return [value[:, i * width:(i + 1) * width] for i in range(4)]

    def team_features(self, blocks):
        rb, rows = self.sizes["rb"], blocks.shape[1]
        return blocks.reshape(4, rows, rb, -1).transpose(1, 2, 0, 3).reshape(rows, -1)

    def member_blocks(self, value):
        rb, rows = self.sizes["rb"], value.shape[0]
        return value.reshape(rows, rb, 4, -1).transpose(2, 0, 1, 3).reshape(4, rows, -1)

    def widen(self, piece):
        if self.sizes["rb"] > 1:
            piece = lax.all_gather(piece, "rb", axis=2, tiled=True)
        piece = piece.reshape(piece.shape[0], -1)
        return lax.all_gather(piece[None], self.cols, axis=0, tiled=True)

    def in_order(self, weight):
        rb = self.sizes["rb"]
        if rb == 1:
            return weight
        parts = weight.reshape(weight.shape[:-1] + (4, rb, -1))
        return jnp.swapaxes(parts, -3, -2).reshape(weight.shape)

    def out_of_order(self, weight):
        rb = self.sizes["rb"]
        if rb == 1:
            return weight
        parts = weight.reshape(weight.shape[:-1] + (rb, 4, -1))
        return jnp.swapaxes(parts, -3, -2).reshape(weight.shape)

    def over_columns(self, partial):
        total = lax.psum_scatter(partial.astype(BF16), self.cols, scatter_dimension=0, tiled=True)
        total = total.reshape(total.shape[0], 4, -1)
        if self.sizes["rb"] > 1:
            total = lax.psum_scatter(total, "rb", scatter_dimension=2, tiled=True)
        return total

    def weight_grads(self, relative, absolute):
        flat = [[piece[:, i] for i in range(4)] for piece in relative]
        flat += [self.pick(piece.transpose(1, 0, 2)) for piece in absolute]
        sizes = [piece[0].shape[0] for piece in flat]
        parts = self.team_send([jnp.concatenate([piece[i] for piece in flat]) for i in range(4)])
        low = jnp.stack(parts)
        if self.sizes["dp"] == 2:
            low = low.astype(F32) + lax.ppermute(low, "dp", [(0, 1), (1, 0)]).astype(F32)
        else:
            low = lax.psum(low.astype(F32), "dp")
        parts = [low[i] for i in range(4)]
        low = self.place(parts, self.spots())
        out, at = [], 0
        for size in sizes:
            out.append(low[:, at:at + size])
            at += size
        return out


def norm_forward(hidden, gain_row, shift_row):
    average = jnp.mean(hidden, axis=1, keepdims=True)
    square = jnp.mean(hidden * hidden, axis=1, keepdims=True)
    inverse = lax.rsqrt(square - average * average + EPSILON)
    normed = (hidden - average) * inverse
    return normed * gain_row + shift_row, normed, inverse


def norm_backward(upstream, normed, inverse, gain_row):
    scaled = upstream * gain_row
    first = jnp.mean(scaled, axis=1, keepdims=True)
    second = jnp.mean(scaled * normed, axis=1, keepdims=True)
    grad = inverse * (scaled - first - normed * second)
    return grad, jnp.sum(upstream * normed, axis=0), jnp.sum(upstream, axis=0)


def exact_gelu(inputs):
    return jax.nn.gelu(inputs, approximate=False)


def column_rows(weight):
    features, parts, width = weight.shape
    blocks = weight.reshape(features, parts, 4, width // 4).transpose(2, 1, 3, 0)
    return blocks.reshape(4, -1, features)


def column_rows_back(blocks, parts):
    features = blocks.shape[2]
    return blocks.reshape(4, parts, -1, features).transpose(3, 1, 0, 2).reshape(features, parts, -1)


def shards(
    layout, tokens, encoder, cotangent, prefixes, selfqkv, selfbias, selfproj, selfshift, crossquery,
    crosskv, crossbias, crossproj, crossshift, upweight, upbias, downweight, downbias, normgain, normshift,
):
    me = layout.me()
    split_rows = lambda weight: weight.reshape(4, -1, weight.shape[1])

    def by_token(rows):
        return layout.halves(rows)

    def gather_weights(relative, absolute, order=None):
        pieces = relative + absolute
        if order is not None:
            pieces, _ = lax.optimization_barrier((pieces, order))
        sizes = [piece.shape[1] for piece in pieces]
        parts = layout.team_send(layout.pick(jnp.concatenate(pieces, axis=1)))
        at = sum(piece.shape[1] for piece in relative)
        groups = []
        if relative:
            groups.append(jnp.stack([part[:at] for part in parts], axis=1))
        if absolute:
            groups.append(layout.place([part[at:] for part in parts], layout.spots()).transpose(1, 0, 2))
        wide = layout.widen(jnp.concatenate(groups))
        out, at = [], 0
        for index, size in enumerate(sizes):
            weight = wide[:, at:at + size].reshape(-1, wide.shape[2])
            out.append(weight if index < len(relative) else layout.in_order(weight))
            at += size
        return out

    (qkv_w,) = gather_weights([column_rows(selfqkv)], [])
    token_parts = layout.team_parts(by_token(tokens))
    tokens_all = jnp.concatenate(token_parts, axis=1)
    width = tokens_all.shape[1]
    group = tokens_all.shape[0]
    own_rows = group // 4
    columns = layout.count(layout.cols)
    heads = columns

    by_col = jnp.concatenate([selfbias.reshape(-1), crossbias.reshape(-1), upbias])
    by_col = lax.all_gather(by_col, layout.cols, axis=0, tiled=False).reshape(columns, -1)
    block = selfbias.shape[1]
    head_biases = lax.dynamic_index_in_dim(
        by_col[:, : 4 * block].reshape(columns, 4, 4, HD), me, 2, keepdims=False
    )
    up_bias = lax.dynamic_index_in_dim(
        by_col[:, 4 * block:].reshape(columns, 4, -1), me, 1, keepdims=False
    ).reshape(1, -1)
    by_row = jnp.concatenate([selfshift[None], crossshift[None], downbias[None], normgain, normshift])
    by_row = lax.all_gather(by_row, ("rb", "rx", "rc"), axis=1, tiled=True)
    self_shift, cross_shift, down_bias = by_row[0], by_row[1], by_row[2]
    gains, shifts = by_row[3:6], by_row[6:9]

    def gather_tokens(own):
        return jnp.concatenate(layout.team_parts(own))

    def reduce_tokens(partial):
        return layout.team_total([partial[i * own_rows:(i + 1) * own_rows] for i in range(4)])

    sequence_prefix = prefixes
    if layout.sizes["sq"] > 1:
        sequence_prefix = lax.dynamic_slice_in_dim(prefixes, lax.axis_index("sq"), 1, 0)

    qkv = contract(qkv_w, tokens_all, 1, 1).reshape(heads, 3, HD, group)
    qkv_bias = jnp.stack([head_biases[:, 0], jnp.zeros_like(head_biases[:, 0]), head_biases[:, 1]], axis=1)
    factor = jnp.array([SCALE, 1.0, 1.0], F32)[None, :, None, None]
    qkv = ((qkv + qkv_bias[..., None]) * factor).astype(BF16).reshape(heads, 3 * HD, group)
    self_set = layout.ring_exchange(qkv)
    self_out, self_low, self_lse = flash_forward(sequence_prefix, self_set, 0, self_set, 1, 2, True)
    attended = layout.ring_exchange(self_low).reshape(heads * HD, group)

    kv_w, self_w, query_w, cross_w = gather_weights(
        [column_rows(crosskv)],
        [split_rows(selfproj), column_rows(crossquery[:, None]), split_rows(crossproj)],
        tokens_all,
    )
    encoder_all = jnp.concatenate(layout.team_parts(by_token(encoder)), axis=1)
    up_w, down_w = gather_weights([], [column_rows(upweight[:, None]), split_rows(downweight)], encoder_all)
    pair = contract(kv_w, encoder_all, 1, 1).reshape(heads, 2, HD, group)
    pair_bias = jnp.stack([jnp.zeros_like(head_biases[:, 3]), head_biases[:, 3]], axis=1)
    pair = (pair + pair_bias[..., None]).astype(BF16).reshape(heads, 2 * HD, group)
    cross_set = layout.ring_trickle(pair)
    spots = layout.spots()
    upstream = layout.team_send(layout.pick(by_token(cotangent).reshape(4, own_rows, -1)))
    upstream = layout.team_features(layout.place(upstream, spots)).astype(F32)

    own_tokens = lax.dynamic_slice_in_dim(tokens_all, me * own_rows, own_rows, 0)
    own_tokens = layout.place(layout.feature_parts(own_tokens), spots)
    own_tokens = layout.team_features(own_tokens).astype(F32)
    self_partial = contract(attended, self_w, 0, 0).reshape(4, own_rows, width)
    first_sum = own_tokens + (layout.team_total(layout.pick(self_partial)) + self_shift)
    first_out, first_normed, first_inverse = norm_forward(first_sum, gains[0], shifts[0])
    first_all = gather_tokens(first_out.astype(BF16))

    query = contract(query_w, first_all, 1, 1).reshape(heads, HD, group)
    query = ((query + head_biases[:, 2][..., None]) * SCALE).astype(BF16)
    cross_query = layout.ring_exchange(query)
    cross_out, cross_low, cross_lse = flash_forward(sequence_prefix, cross_query, 0, cross_set, 0, 1, False)
    crossed = layout.ring_exchange(cross_low).reshape(heads * HD, group)
    second_sum = first_out + (reduce_tokens(contract(crossed, cross_w, 0, 0)) + cross_shift)
    second_out, second_normed, second_inverse = norm_forward(second_sum, gains[1], shifts[1])
    second_all = gather_tokens(second_out.astype(BF16))

    hidden_pre = contract(second_all, up_w, 1, 1) + up_bias
    hidden_act = exact_gelu(hidden_pre).astype(BF16)
    third_sum = second_out + (reduce_tokens(contract(hidden_act, down_w, 1, 0)) + down_bias)
    third_out, third_normed, third_inverse = norm_forward(third_sum, gains[2], shifts[2])
    layer_out = third_out.astype(BF16)
    layer_out = layout.team_send(layout.pick(layout.member_blocks(layer_out)))
    layer_out = layout.unhalves(layout.place(layer_out, spots).reshape(group, -1))

    third_grad, third_gain, third_shift = norm_backward(upstream, third_normed, third_inverse, gains[2])
    down_own = third_grad.astype(BF16)
    down_all = gather_tokens(down_own)
    act_grad = contract(down_all, down_w, 1, 1)
    pre_low = jax.vjp(exact_gelu, hidden_pre)[1](act_grad)[0].astype(BF16)
    second_grad = third_grad + reduce_tokens(contract(pre_low, up_w, 1, 0))
    down_sum = layout.over_columns(layout.out_of_order(contract(hidden_act, down_all, 0, 0)))
    up_sum = layout.over_columns(layout.out_of_order(contract(pre_low, second_all, 0, 0)))
    upweight_grad, downweight_grad = layout.weight_grads([], [up_sum, down_sum])
    mid_grad, second_gain, second_shift = norm_backward(second_grad, second_normed, second_inverse, gains[1])
    cross_own = mid_grad.astype(BF16)
    cross_all = gather_tokens(cross_own)
    crossed_grad = contract(cross_w, cross_all, 1, 1).astype(BF16).reshape(heads, HD, group)
    crossed_grad = layout.ring_exchange(crossed_grad)
    crossproj_sum = layout.over_columns(layout.out_of_order(contract(crossed, cross_all, 1, 0)))
    dquery, dkeys, dvalues = flash_backward(
        sequence_prefix, cross_query, 0, cross_set, 0, 1, crossed_grad, cross_out, cross_lse, False
    )
    cross_bias_sums = (jnp.sum(dquery.astype(F32), axis=(0, 2)), jnp.sum(dvalues.astype(F32), axis=(0, 2)))
    dquery = layout.ring_exchange(dquery).reshape(heads * HD, group)
    first_grad = mid_grad + reduce_tokens(contract(dquery, query_w, 0, 0))
    dpair = layout.ring_trickle(jnp.concatenate([dkeys, dvalues], axis=1)).reshape(heads * 2 * HD, group)
    crossquery_sum = layout.over_columns(layout.out_of_order(contract(dquery, first_all, 1, 0)))
    crosskv_sum = layout.over_columns(contract(dpair, encoder_all, 1, 0))
    crosskv_grad, crossproj_grad, crossquery_grad = layout.weight_grads(
        [crosskv_sum], [crossproj_sum, crossquery_sum]
    )
    encoder_grad = layout.team_total(layout.feature_parts(contract(dpair, kv_w, 0, 0)))
    encoder_grad = layout.unhalves(encoder_grad)
    low_grad, first_gain, first_shift = norm_backward(first_grad, first_normed, first_inverse, gains[0])
    self_own = low_grad.astype(BF16)
    self_all = layout.place(layout.team_parts(self_own), spots).reshape(group, width)
    attended_grad = contract(self_w, self_all, 1, 1).astype(BF16).reshape(heads, HD, group)
    attended_grad = layout.ring_exchange(attended_grad)
    selfproj_sum = layout.over_columns(layout.out_of_order(contract(attended, self_all, 1, 0)))
    dq, dk, dv = flash_backward(
        sequence_prefix, self_set, 0, self_set, 1, 2, attended_grad, self_out, self_lse, True
    )
    self_bias_sums = (jnp.sum(dq.astype(F32), axis=(0, 2)), jnp.sum(dv.astype(F32), axis=(0, 2)))
    dqkv = layout.ring_exchange(jnp.concatenate([dq, dk, dv], axis=1)).reshape(heads * 3 * HD, group)
    selfqkv_sum = layout.over_columns(contract(dqkv, tokens_all, 1, 0))
    selfqkv_grad, selfproj_grad = layout.weight_grads([selfqkv_sum], [selfproj_sum])
    tokens_part = contract(dqkv, qkv_w, 0, 0)
    low_parts = jnp.concatenate(layout.pick(layout.member_blocks(low_grad)), axis=1)
    mine = lax.dynamic_slice_in_dim(tokens_part, me * own_rows, own_rows, 0) + low_parts
    tokens_part = lax.dynamic_update_slice_in_dim(tokens_part, mine, me * own_rows, 0)
    tokens_grad = layout.unhalves(layout.team_total(layout.feature_parts(tokens_part)))

    def at_head(sums):
        spot = (layout.ring_index() * 4 + me) * HD
        return lax.dynamic_update_slice_in_dim(jnp.zeros((width,), F32), sums, spot, 0)

    up_sums = jnp.zeros((columns, 4, pre_low.shape[1] // columns), F32)
    up_sums = lax.dynamic_update_index_in_dim(
        up_sums, jnp.sum(pre_low.astype(F32), axis=0).reshape(columns, -1), me, 1
    )
    column_sum = lambda low: jnp.sum(low.astype(F32), axis=0)
    rows = jnp.stack([
        first_gain, second_gain, third_gain, first_shift, second_shift, third_shift,
        column_sum(self_own), column_sum(cross_own), column_sum(down_own),
        at_head(cross_bias_sums[0]), at_head(cross_bias_sums[1]),
    ])
    rows = layout.total(jnp.concatenate([rows, up_sums.reshape(-1, width)]))
    rows, up_sums = rows[:11], rows[11:].reshape(up_sums.shape)
    late = layout.total(jnp.stack([at_head(self_bias_sums[0]), at_head(self_bias_sums[1])]))
    row_at = (lax.axis_index("rb") * 4 + me) * normgain.shape[1]
    col_at = lax.axis_index(layout.cols)
    by_row = lax.dynamic_slice_in_dim(rows[:9], row_at, normgain.shape[1], 1)
    crossbias_grad = lax.dynamic_slice_in_dim(rows[9:], col_at * block, block, 1)
    selfbias_grad = lax.dynamic_slice_in_dim(late, col_at * block, block, 1)
    upbias_grad = lax.dynamic_index_in_dim(up_sums, col_at, 0, keepdims=False).reshape(-1)
    join_rows = lambda blocks: blocks.reshape(-1, blocks.shape[2])
    return (
        layer_out,
        tokens_grad,
        encoder_grad,
        column_rows_back(selfqkv_grad, 3),
        selfbias_grad,
        join_rows(selfproj_grad),
        by_row[6],
        column_rows_back(crossquery_grad, 1)[:, 0],
        column_rows_back(crosskv_grad, 2),
        crossbias_grad,
        join_rows(crossproj_grad),
        by_row[7],
        column_rows_back(upweight_grad, 1)[:, 0],
        upbias_grad,
        join_rows(downweight_grad),
        by_row[8],
        by_row[:3],
        by_row[3:6],
    )


def solution(mesh):
    def run(*arrays):
        dp, row, col = (mesh.shape[name] for name in ("dp", "row", "col"))
        per_col = arrays[4].shape[2] // HD // col
        seqs = arrays[3].shape[0] // dp
        assert per_col == 4 and row % 4 == 0 and col % seqs == 0
        assert (row // 4) * (col // seqs) == col
        sizes = {"dp": dp, "rb": row // 4, "rx": 2, "rc": 2, "sq": seqs, "cs": col // seqs}
        grid = Mesh(mesh.devices.reshape(tuple(sizes.values())), tuple(sizes))
        rows, cols, tokens = ("rb", "rx", "rc"), ("sq", "cs"), ("dp", "sq", "cs")
        specs = {
            "tokens": P(tokens, rows), "rc": P(rows, cols), "cr": P(cols, rows), "r3c": P(rows, None, cols),
            "c": P(cols), "r": P(rows), "2c": P(None, cols), "2r": P(None, rows),
        }
        ins = (
            "tokens", "tokens", "tokens", "dp", "r3c", "2c", "cr", "r", "rc", "r3c", "2c", "cr", "r", "rc", "c", "cr", "r", "2r", "2r",
        )
        outs = (
            "tokens", "tokens", "tokens", "r3c", "2c", "cr", "r", "rc", "r3c", "2c", "cr", "r", "rc", "c", "cr", "r", "2r", "2r",
        )
        specs["dp"] = P("dp")
        body = functools.partial(shards, Layout(sizes))
        return jax.shard_map(
            body, mesh=grid, in_specs=tuple(specs[s] for s in ins), out_specs=tuple(specs[s] for s in outs),
            check_vma=False,
        )(*arrays)

    return run
```

```python
import functools
import jax
import jax.numpy as jnp
from jax import lax
from jax.experimental import pallas as pl
from jax.experimental.pallas import tpu as pltpu
from jax.sharding import Mesh
from jax.sharding import PartitionSpec as P

HD = 64
NEGATIVE = -1e30
F32 = jnp.float32
BF16 = jnp.bfloat16


def dot_nn(a, b):
    return lax.dot_general(a, b, (((1,), (0,)), ((), ())), preferred_element_type=F32)


def allowed_mask(first_key, first_query, prefix, shape):
    key_pos = first_key + lax.broadcasted_iota(jnp.int32, shape, 0)
    query_pos = first_query + lax.broadcasted_iota(jnp.int32, shape, 1)
    return (key_pos < prefix) | (key_pos <= query_pos)


def forward_kernel(masked, bq, bk, prefix_ref, q_ref, k_ref, v_ref, o_ref, low_ref, lse_ref, keys, values, acc, peak):
    chunks, _, chunk = k_ref.shape
    per = chunk // bk
    blocks = chunks * per
    step = pl.program_id(0)
    prefix = prefix_ref[0]

    @pl.when(step == 0)
    def _():
        for c in range(chunks):
            for b in range(per):
                i = c * per + b
                keys[i] = k_ref[c, :, b * bk:(b + 1) * bk].T
                values[i, :HD, :] = v_ref[c, :, b * bk:(b + 1) * bk]
                rows = lax.broadcasted_iota(jnp.int32, (16, bk), 0)
                values[i, HD:, :] = jnp.where(rows == 0, 1.0, 0.0).astype(BF16)

    first_query = step * bq
    query = q_ref[0]
    peak[...] = jnp.full(peak.shape, NEGATIVE, F32)
    acc[...] = jnp.zeros(acc.shape, F32)

    def visit(i, use_mask):
        scores = dot_nn(keys[i], query)
        if use_mask:
            scores = jnp.where(allowed_mask(i * bk, first_query, prefix, scores.shape), scores, NEGATIVE)
        old = peak[...]
        new = jnp.maximum(old, jnp.max(scores, axis=0, keepdims=True))
        weight = jnp.exp(scores - new).astype(BF16)
        acc[...] = acc[...] * jnp.exp(old - new) + dot_nn(values[i], weight)
        peak[...] = new

    if masked:
        full = jnp.maximum(prefix, first_query + 1) // bk
        stop = (jnp.maximum(prefix, first_query + bq) + bk - 1) // bk
        lax.fori_loop(0, full, lambda i, c: (visit(i, False), c)[1], 0)
        lax.fori_loop(full, stop, lambda i, c: (visit(i, True), c)[1], 0)
    else:
        lax.fori_loop(0, blocks, lambda i, c: (visit(i, False), c)[1], 0)
    total = acc[HD:HD + 1, :]
    out = acc[:HD, :] / total
    o_ref[0] = out
    low_ref[0] = out.astype(BF16)
    lse_ref[0] = peak[...] + jnp.log(total)


def flash_forward(prefix, queries, q_part, pairs, k_part, v_part, masked, bq=1024, bk=1024):
    chunks, _, chunk = queries.shape
    length = chunks * chunk
    per = chunk // bq
    whole = lambda part: pl.BlockSpec((chunks, HD, chunk), lambda i, p: (0, part, 0))
    mine = lambda rows: pl.BlockSpec((1, rows, bq), lambda i, p: (i // per, 0, i % per))
    return pl.pallas_call(
        functools.partial(forward_kernel, masked, bq, bk),
        out_shape=(
            jax.ShapeDtypeStruct((chunks, HD, chunk), F32),
            jax.ShapeDtypeStruct((chunks, HD, chunk), BF16),
            jax.ShapeDtypeStruct((chunks, 1, chunk), F32),
        ),
        grid_spec=pltpu.PrefetchScalarGridSpec(
            num_scalar_prefetch=1,
            grid=(length // bq,),
            in_specs=[
                pl.BlockSpec((1, HD, bq), lambda i, p: (i // per, q_part, i % per)),
                whole(k_part),
                whole(v_part),
            ],
            out_specs=[mine(HD), mine(HD), mine(1)],
            scratch_shapes=[
                pltpu.VMEM((length // bk, bk, HD), BF16),
                pltpu.VMEM((length // bk, HD + 16, bk), BF16),
                pltpu.VMEM((HD + 16, bq), F32),
                pltpu.VMEM((1, bq), F32),
            ],
        ),
        cost_estimate=pl.CostEstimate(
            flops=4 * HD * length * length, transcendentals=length * length, bytes_accessed=14 * HD * length
        ),
        name="attend_self" if masked else "attend_cross",
    )(prefix, queries, pairs, pairs)


def backward_kernel(masked, bq, bk, prefix_ref, q_ref, g_ref, o_ref, lse_ref, k_ref, v_ref,
                    dq_ref, dk_ref, dv_ref, rows_q, rows_g, delta, dq_acc, dk_acc, dv_acc):
    chunks, _, chunk = q_ref.shape
    per = chunk // bq
    blocks = chunks * per
    step = pl.program_id(0)
    prefix = prefix_ref[0]

    @pl.when(step == 0)
    def _():
        for c in range(chunks):
            for b in range(per):
                i = c * per + b
                at = slice(b * bq, (b + 1) * bq)
                grad = g_ref[c, :, at]
                rows_q[i] = q_ref[c, :, at].T
                rows_g[i] = grad.T
                delta[i] = jnp.sum(grad.astype(F32) * o_ref[c, :, at], axis=0, keepdims=True)
        dq_acc[...] = jnp.zeros(dq_acc.shape, F32)

    first_key = step * bk
    key_cols = k_ref[0]
    key_rows = key_cols.T
    value_rows = v_ref[0].T
    dk_acc[...] = jnp.zeros(dk_acc.shape, F32)
    dv_acc[...] = jnp.zeros(dv_acc.shape, F32)

    def visit(i, use_mask):
        c, at = i // per, pl.ds(pl.multiple_of((i % per) * bq, bq), bq)
        scores = dot_nn(key_rows, q_ref[c, :, at])
        if use_mask:
            scores = jnp.where(allowed_mask(first_key, i * bq, prefix, scores.shape), scores, NEGATIVE)
        probs = jnp.exp(scores - lse_ref[c, :, at])
        dprobs = dot_nn(value_rows, g_ref[c, :, at])
        dscore = (probs * (dprobs - delta[i])).astype(BF16)
        dv_acc[...] += dot_nn(probs.astype(BF16), rows_g[i])
        dk_acc[...] += dot_nn(dscore, rows_q[i])
        dq_acc[i] += dot_nn(key_cols, dscore)

    if masked:
        inside = first_key + bk <= prefix
        start = jnp.where(first_key < prefix, 0, first_key // bq)
        free = jnp.where(inside, 0, jnp.minimum((first_key + bk - 1 + bq - 1) // bq, blocks))
        lax.fori_loop(start, free, lambda i, c: (visit(i, True), c)[1], 0)
        lax.fori_loop(jnp.maximum(start, free), blocks, lambda i, c: (visit(i, False), c)[1], 0)
    else:
        lax.fori_loop(0, blocks, lambda i, c: (visit(i, False), c)[1], 0)
    dk_ref[0] = dk_acc[...].T.astype(BF16)
    dv_ref[0] = dv_acc[...].T.astype(BF16)

    @pl.when(step == pl.num_programs(0) - 1)
    def _():
        for c in range(chunks):
            for b in range(per):
                low = dq_acc[c * per + b].astype(BF16)
                dq_ref[c, :, b * bq:(b + 1) * bq] = low * jnp.asarray(HD ** -0.5, BF16)


def flash_backward(prefix, queries, q_part, pairs, k_part, v_part, grads, outputs, lse, masked, bq=1024, bk=1024):
    chunks, _, chunk = queries.shape
    length = chunks * chunk
    per = chunk // bk
    whole = lambda part, rows=HD: pl.BlockSpec((chunks, rows, chunk), lambda i, p: (0, part, 0))
    mine = lambda part: pl.BlockSpec((1, HD, bk), lambda i, p: (i // per, part, i % per))
    shape = jax.ShapeDtypeStruct((chunks, HD, chunk), BF16)
    return pl.pallas_call(
        functools.partial(backward_kernel, masked, bq, bk),
        out_shape=(shape, shape, shape),
        grid_spec=pltpu.PrefetchScalarGridSpec(
            num_scalar_prefetch=1,
            grid=(length // bk,),
            in_specs=[whole(q_part), whole(0), whole(0), whole(0, 1), mine(k_part), mine(v_part)],
            out_specs=[whole(0), mine(0), mine(0)],
            scratch_shapes=[
                pltpu.VMEM((length // bq, bq, HD), BF16),
                pltpu.VMEM((length // bq, bq, HD), BF16),
                pltpu.VMEM((length // bq, 1, bq), F32),
                pltpu.VMEM((length // bq, HD, bq), F32),
                pltpu.VMEM((bk, HD), F32),
                pltpu.VMEM((bk, HD), F32),
            ],
        ),
        cost_estimate=pl.CostEstimate(
            flops=10 * HD * length * length, transcendentals=length * length, bytes_accessed=20 * HD * length
        ),
        name="attend_self_back" if masked else "attend_cross_back",
    )(prefix, queries, grads, outputs, lse, pairs, pairs)


EPSILON = 1e-05
SCALE = HD ** -0.5


def contract(left, right, left_dim, right_dim):
    return lax.dot_general(
        left, right, (((left_dim,), (right_dim,)), ((), ())), preferred_element_type=F32
    )


class Layout:
    def __init__(self, sizes):
        self.sizes = sizes
        keep = lambda names: tuple(n for n in names if sizes[n] > 1) or names[-1:]
        self.team = ("rx", "rc")
        self.cols = keep(("sq", "cs"))
        self.ring = keep(("rb", "cs"))
        self.every = ("dp", "rb", "rx", "rc", "sq", "cs")

    def count(self, names):
        total = 1
        for name in names:
            total *= self.sizes[name]
        return total

    def me(self):
        return lax.axis_index("rx") * 2 + lax.axis_index("rc")

    def swap(self, value, bits):
        if bits == 1:
            return lax.ppermute(value, "rc", [(0, 1), (1, 0)])
        if bits == 2:
            return lax.ppermute(value, "rx", [(0, 1), (1, 0)])
        return lax.ppermute(value, self.team, [(i, i ^ 3) for i in range(4)])

    def place(self, parts, spots):
        out = jnp.zeros((len(parts),) + parts[0].shape, parts[0].dtype)
        for part, spot in zip(parts, spots):
            out = lax.dynamic_update_index_in_dim(out, part, spot, 0)
        return lax.optimization_barrier(out)

    def spots(self):
        me = self.me()
        return [me, me ^ 1, me ^ 2, me ^ 3]

    def team_parts(self, value):
        core, across = self.swap(value, 1), self.swap(value, 2)
        return [value, core, across, self.swap(across, 1)]

    def pick(self, blocks):
        return [lax.dynamic_index_in_dim(blocks, spot, 0, keepdims=False) for spot in self.spots()]

    def team_send(self, parts):
        return [parts[0]] + [self.swap(parts[bits], bits) for bits in (1, 2, 3)]

    def team_total(self, parts):
        away = self.swap(jnp.stack([parts[1].astype(BF16), parts[3].astype(BF16)]), 1).astype(F32)
        away_across = self.swap((parts[2] + away[1]).astype(BF16), 2).astype(F32)
        return (parts[0] + away[0]) + away_across

    def total(self, value):
        for name in self.every:
            bits = 1
            while bits < self.sizes[name]:
                pairs = [(i, i ^ bits) for i in range(self.sizes[name])]
                value = value + lax.ppermute(value, name, pairs)
                bits *= 2
        return value

    def column_vectors(self, vector):
        size = self.count(self.cols)
        me = lax.axis_index(self.cols)
        parts, spots = [vector], [me]
        for step in range(1, size):
            pairs = [(i, (i + step) % size) for i in range(size)]
            parts.append(lax.ppermute(vector, self.cols, pairs))
            spots.append((me + size - step) % size)
        return self.place(parts, spots)

    def ring_index(self):
        return lax.axis_index("cs") * self.sizes["rb"] + lax.axis_index("rb")

    def flip(self, blocks, first, second):
        first, second = self.sizes[first], self.sizes[second]
        if first == 1 or second == 1:
            return blocks
        return blocks.reshape((first, second) + blocks.shape[1:]).swapaxes(0, 1).reshape(blocks.shape)

    def ring_exchange(self, blocks):
        blocks = lax.all_to_all(self.flip(blocks, "cs", "rb"), self.ring, 0, 0, tiled=True)
        return self.flip(blocks, "rb", "cs")

    def ring_trickle(self, blocks):
        size = self.count(self.ring)
        me = lax.axis_index(self.ring)
        blocks = self.flip(blocks, "cs", "rb")
        pick = lambda step: lax.dynamic_index_in_dim(blocks, (me + step) % size, 0, keepdims=False)
        parts, spots = [pick(0)], [me]
        for step in range(1, size):
            parts.append(lax.ppermute(pick(step), self.ring, [(i, (i + step) % size) for i in range(size)]))
            spots.append((me + size - step) % size)
        return self.flip(self.place(parts, spots), "rb", "cs")

    def block_sum(self, value):
        return lax.psum_scatter(value, self.cols, scatter_dimension=0, tiled=True)

    def halves(self, value):
        if self.sizes["rb"] == 1:
            return value
        return lax.all_to_all(value, "rb", 0, 1, tiled=True)

    def unhalves(self, value):
        if self.sizes["rb"] == 1:
            return value
        return lax.all_to_all(value, "rb", 1, 0, tiled=True)

    def feature_parts(self, value):
        width = value.shape[1] // 4
        return [value[:, i * width:(i + 1) * width] for i in range(4)]

    def team_features(self, blocks):
        rb, rows = self.sizes["rb"], blocks.shape[1]
        return blocks.reshape(4, rows, rb, -1).transpose(1, 2, 0, 3).reshape(rows, -1)

    def member_blocks(self, value):
        rb, rows = self.sizes["rb"], value.shape[0]
        return value.reshape(rows, rb, 4, -1).transpose(2, 0, 1, 3).reshape(4, rows, -1)

    def widen(self, piece):
        if self.sizes["rb"] > 1:
            piece = lax.all_gather(piece, "rb", axis=2, tiled=True)
        piece = piece.reshape(piece.shape[0], -1)
        return lax.all_gather(piece[None], self.cols, axis=0, tiled=True)

    def in_order(self, weight):
        rb = self.sizes["rb"]
        if rb == 1:
            return weight
        parts = weight.reshape(weight.shape[:-1] + (4, rb, -1))
        return jnp.swapaxes(parts, -3, -2).reshape(weight.shape)

    def out_of_order(self, weight):
        rb = self.sizes["rb"]
        if rb == 1:
            return weight
        parts = weight.reshape(weight.shape[:-1] + (rb, 4, -1))
        return jnp.swapaxes(parts, -3, -2).reshape(weight.shape)

    def over_columns(self, partial):
        total = lax.psum_scatter(partial.astype(BF16), self.cols, scatter_dimension=0, tiled=True)
        total = total.reshape(total.shape[0], 4, -1)
        if self.sizes["rb"] > 1:
            total = lax.psum_scatter(total, "rb", scatter_dimension=2, tiled=True)
        return total

    def weight_grads(self, relative, absolute):
        flat = [[piece[:, i] for i in range(4)] for piece in relative]
        flat += [self.pick(piece.transpose(1, 0, 2)) for piece in absolute]
        sizes = [piece[0].shape[0] for piece in flat]
        parts = self.team_send([jnp.concatenate([piece[i] for piece in flat]) for i in range(4)])
        low = jnp.stack(parts)
        if self.sizes["dp"] == 2:
            low = low.astype(F32) + lax.ppermute(low, "dp", [(0, 1), (1, 0)]).astype(F32)
        else:
            low = lax.psum(low.astype(F32), "dp")
        parts = [low[i] for i in range(4)]
        low = self.place(parts, self.spots())
        out, at = [], 0
        for size in sizes:
            out.append(low[:, at:at + size])
            at += size
        return out


def norm_forward(hidden, gain_row, shift_row):
    average = jnp.mean(hidden, axis=1, keepdims=True)
    square = jnp.mean(hidden * hidden, axis=1, keepdims=True)
    inverse = lax.rsqrt(square - average * average + EPSILON)
    normed = (hidden - average) * inverse
    return normed * gain_row + shift_row, normed, inverse


def norm_backward(upstream, normed, inverse, gain_row):
    scaled = upstream * gain_row
    first = jnp.mean(scaled, axis=1, keepdims=True)
    second = jnp.mean(scaled * normed, axis=1, keepdims=True)
    grad = inverse * (scaled - first - normed * second)
    return grad, jnp.sum(upstream * normed, axis=0), jnp.sum(upstream, axis=0)


def exact_gelu(inputs):
    return jax.nn.gelu(inputs, approximate=False)


def column_rows(weight):
    features, parts, width = weight.shape
    blocks = weight.reshape(features, parts, 4, width // 4).transpose(2, 1, 3, 0)
    return blocks.reshape(4, -1, features)


def column_rows_back(blocks, parts):
    features = blocks.shape[2]
    return blocks.reshape(4, parts, -1, features).transpose(3, 1, 0, 2).reshape(features, parts, -1)


def shards(
    layout, tokens, encoder, cotangent, prefixes, selfqkv, selfbias, selfproj, selfshift, crossquery,
    crosskv, crossbias, crossproj, crossshift, upweight, upbias, downweight, downbias, normgain, normshift,
):
    me = layout.me()
    split_rows = lambda weight: weight.reshape(4, -1, weight.shape[1])

    def by_token(rows):
        return layout.halves(rows)

    def gather_weights(relative, absolute, order=None):
        pieces = relative + absolute
        sizes = [piece.shape[1] for piece in pieces]
        parts = layout.team_send(layout.pick(jnp.concatenate(pieces, axis=1)))
        at = sum(piece.shape[1] for piece in relative)
        groups = []
        if relative:
            groups.append(jnp.stack([part[:at] for part in parts], axis=1))
        if absolute:
            groups.append(layout.place([part[at:] for part in parts], layout.spots()).transpose(1, 0, 2))
        piece = jnp.concatenate(groups)
        if order is not None:
            piece, _ = lax.optimization_barrier((piece, order))
        wide = layout.widen(piece)
        out, at = [], 0
        for index, size in enumerate(sizes):
            weight = wide[:, at:at + size].reshape(-1, wide.shape[2])
            out.append(weight if index < len(relative) else layout.in_order(weight))
            at += size
        return out

    (qkv_w,) = gather_weights([column_rows(selfqkv)], [])
    token_parts = layout.team_parts(by_token(tokens))
    tokens_all = jnp.concatenate(token_parts, axis=1)
    width = tokens_all.shape[1]
    group = tokens_all.shape[0]
    own_rows = group // 4
    columns = layout.count(layout.cols)
    heads = columns

    by_col = jnp.concatenate([selfbias.reshape(-1), crossbias.reshape(-1), upbias])
    by_col = layout.column_vectors(by_col)
    block = selfbias.shape[1]
    head_biases = lax.dynamic_index_in_dim(
        by_col[:, : 4 * block].reshape(columns, 4, 4, HD), me, 2, keepdims=False
    )
    up_bias = lax.dynamic_index_in_dim(
        by_col[:, 4 * block:].reshape(columns, 4, -1), me, 1, keepdims=False
    ).reshape(1, -1)
    by_row = jnp.concatenate([selfshift[None], crossshift[None], downbias[None], normgain, normshift])
    if layout.sizes["rb"] > 1:
        by_row = lax.all_gather(by_row, "rb", axis=1, tiled=True)
    by_row = layout.team_features(layout.place(layout.team_parts(by_row), layout.spots()))
    self_shift, cross_shift, down_bias = by_row[0], by_row[1], by_row[2]
    gains, shifts = by_row[3:6], by_row[6:9]

    def gather_tokens(own):
        return jnp.concatenate(layout.team_parts(own))

    def reduce_tokens(partial):
        return layout.team_total([partial[i * own_rows:(i + 1) * own_rows] for i in range(4)])

    sequence_prefix = prefixes
    if layout.sizes["sq"] > 1:
        sequence_prefix = lax.dynamic_slice_in_dim(prefixes, lax.axis_index("sq"), 1, 0)

    kv_w, self_w = gather_weights([column_rows(crosskv)], [split_rows(selfproj)])
    encoder_all = jnp.concatenate(layout.team_parts(by_token(encoder)), axis=1)
    pair = contract(kv_w, encoder_all, 1, 1).reshape(heads, 2, HD, group)
    pair_bias = jnp.stack([jnp.zeros_like(head_biases[:, 3]), head_biases[:, 3]], axis=1)
    pair = (pair + pair_bias[..., None]).astype(BF16).reshape(heads, 2 * HD, group)

    qkv = contract(qkv_w, tokens_all, 1, 1).reshape(heads, 3, HD, group)
    qkv_bias = jnp.stack([head_biases[:, 0], jnp.zeros_like(head_biases[:, 0]), head_biases[:, 1]], axis=1)
    factor = jnp.array([SCALE, 1.0, 1.0], F32)[None, :, None, None]
    qkv = ((qkv + qkv_bias[..., None]) * factor).astype(BF16).reshape(heads, 3 * HD, group)
    self_set = layout.ring_exchange(qkv)
    self_set, pair = lax.optimization_barrier((self_set, pair))
    cross_set = layout.ring_trickle(pair)
    self_out, self_low, self_lse = flash_forward(sequence_prefix, self_set, 0, self_set, 1, 2, True)
    self_low, cross_set = lax.optimization_barrier((self_low, cross_set))
    attended = layout.ring_exchange(self_low).reshape(heads * HD, group)
    spots = layout.spots()
    query_w, cross_w = gather_weights(
        [], [column_rows(crossquery[:, None]), split_rows(crossproj)], attended
    )
    up_w, down_w = gather_weights([], [column_rows(upweight[:, None]), split_rows(downweight)], query_w)

    upstream = layout.team_send(layout.pick(by_token(cotangent).reshape(4, own_rows, -1)))
    upstream = layout.team_features(layout.place(upstream, spots)).astype(F32)

    own_tokens = lax.dynamic_slice_in_dim(tokens_all, me * own_rows, own_rows, 0)
    own_tokens = layout.place(layout.feature_parts(own_tokens), spots)
    own_tokens = layout.team_features(own_tokens).astype(F32)
    self_partial = contract(attended, self_w, 0, 0).reshape(4, own_rows, width)
    first_sum = own_tokens + (layout.team_total(layout.pick(self_partial)) + self_shift)
    first_out, first_normed, first_inverse = norm_forward(first_sum, gains[0], shifts[0])
    first_all = gather_tokens(first_out.astype(BF16))

    query = contract(query_w, first_all, 1, 1).reshape(heads, HD, group)
    query = ((query + head_biases[:, 2][..., None]) * SCALE).astype(BF16)
    cross_query = layout.ring_exchange(query)
    cross_out, cross_low, cross_lse = flash_forward(sequence_prefix, cross_query, 0, cross_set, 0, 1, False)
    crossed = layout.ring_exchange(cross_low).reshape(heads * HD, group)
    second_sum = first_out + (reduce_tokens(contract(crossed, cross_w, 0, 0)) + cross_shift)
    second_out, second_normed, second_inverse = norm_forward(second_sum, gains[1], shifts[1])
    second_all = gather_tokens(second_out.astype(BF16))

    hidden_pre = contract(second_all, up_w, 1, 1) + up_bias
    hidden_act = exact_gelu(hidden_pre).astype(BF16)
    third_sum = second_out + (reduce_tokens(contract(hidden_act, down_w, 1, 0)) + down_bias)
    third_out, third_normed, third_inverse = norm_forward(third_sum, gains[2], shifts[2])
    layer_out = third_out.astype(BF16)
    layer_out = layout.team_send(layout.pick(layout.member_blocks(layer_out)))
    layer_out = layout.unhalves(layout.place(layer_out, spots).reshape(group, -1))

    third_grad, third_gain, third_shift = norm_backward(upstream, third_normed, third_inverse, gains[2])
    down_own = third_grad.astype(BF16)
    down_all = gather_tokens(down_own)
    act_grad = contract(down_all, down_w, 1, 1)
    pre_low = jax.vjp(exact_gelu, hidden_pre)[1](act_grad)[0].astype(BF16)
    second_grad = third_grad + reduce_tokens(contract(pre_low, up_w, 1, 0))
    down_sum = layout.over_columns(layout.out_of_order(contract(hidden_act, down_all, 0, 0)))
    up_sum = layout.over_columns(layout.out_of_order(contract(pre_low, second_all, 0, 0)))
    mid_grad, second_gain, second_shift = norm_backward(second_grad, second_normed, second_inverse, gains[1])
    cross_own = mid_grad.astype(BF16)
    cross_all = gather_tokens(cross_own)
    crossed_grad = contract(cross_w, cross_all, 1, 1).astype(BF16).reshape(heads, HD, group)
    crossed_grad = layout.ring_exchange(crossed_grad)
    crossproj_part = contract(crossed, cross_all, 1, 0).astype(BF16)
    crossed_grad, crossproj_part = lax.optimization_barrier((crossed_grad, crossproj_part))
    crossproj_sum = layout.over_columns(layout.out_of_order(crossproj_part))
    dquery, dkeys, dvalues = flash_backward(
        sequence_prefix, cross_query, 0, cross_set, 0, 1, crossed_grad, cross_out, cross_lse, False
    )
    cross_bias_sums = (jnp.sum(dquery.astype(F32), axis=(0, 2)), jnp.sum(dvalues.astype(F32), axis=(0, 2)))
    dquery = layout.ring_exchange(dquery).reshape(heads * HD, group)
    first_grad = mid_grad + reduce_tokens(contract(dquery, query_w, 0, 0))
    dpair = layout.ring_trickle(jnp.concatenate([dkeys, dvalues], axis=1)).reshape(heads * 2 * HD, group)
    crossquery_sum = layout.over_columns(layout.out_of_order(contract(dquery, first_all, 1, 0)))
    crosskv_sum = layout.over_columns(contract(dpair, encoder_all, 1, 0))
    encoder_grad = layout.team_total(layout.feature_parts(contract(dpair, kv_w, 0, 0)))
    encoder_grad = layout.unhalves(encoder_grad)
    low_grad, first_gain, first_shift = norm_backward(first_grad, first_normed, first_inverse, gains[0])
    self_own = low_grad.astype(BF16)
    self_all = layout.place(layout.team_parts(self_own), spots).reshape(group, width)
    attended_grad = contract(self_w, self_all, 1, 1).astype(BF16).reshape(heads, HD, group)
    attended_grad = layout.ring_exchange(attended_grad)
    selfproj_part = contract(attended, self_all, 1, 0).astype(BF16)
    sums = (up_sum, down_sum, crosskv_sum, crossproj_sum, crossquery_sum)
    attended_grad, selfproj_part, sums = lax.optimization_barrier((attended_grad, selfproj_part, sums))
    up_sum, down_sum, crosskv_sum, crossproj_sum, crossquery_sum = sums
    early_grads = layout.weight_grads([crosskv_sum], [crossproj_sum, crossquery_sum, up_sum, down_sum])
    selfproj_sum = layout.over_columns(layout.out_of_order(selfproj_part))
    dq, dk, dv = flash_backward(
        sequence_prefix, self_set, 0, self_set, 1, 2, attended_grad, self_out, self_lse, True
    )
    dq, dk, dv, early_grads, selfproj_sum = lax.optimization_barrier((dq, dk, dv, early_grads, selfproj_sum))
    crosskv_grad, crossproj_grad, crossquery_grad, upweight_grad, downweight_grad = early_grads
    self_bias_sums = (jnp.sum(dq.astype(F32), axis=(0, 2)), jnp.sum(dv.astype(F32), axis=(0, 2)))
    dqkv = layout.ring_exchange(jnp.concatenate([dq, dk, dv], axis=1)).reshape(heads * 3 * HD, group)
    selfqkv_sum = layout.over_columns(contract(dqkv, tokens_all, 1, 0))
    selfqkv_grad, selfproj_grad = layout.weight_grads([selfqkv_sum], [selfproj_sum])
    tokens_part = contract(dqkv, qkv_w, 0, 0)
    low_parts = jnp.concatenate(layout.pick(layout.member_blocks(low_grad)), axis=1)
    mine = lax.dynamic_slice_in_dim(tokens_part, me * own_rows, own_rows, 0) + low_parts
    tokens_part = lax.dynamic_update_slice_in_dim(tokens_part, mine, me * own_rows, 0)
    tokens_grad = layout.unhalves(layout.team_total(layout.feature_parts(tokens_part)))

    def at_head(sums):
        spot = (layout.ring_index() * 4 + me) * HD
        return lax.dynamic_update_slice_in_dim(jnp.zeros((width,), F32), sums, spot, 0)

    up_sums = jnp.zeros((columns, 4, pre_low.shape[1] // columns), F32)
    up_sums = lax.dynamic_update_index_in_dim(
        up_sums, jnp.sum(pre_low.astype(F32), axis=0).reshape(columns, -1), me, 1
    )
    column_sum = lambda low: jnp.sum(low.astype(F32), axis=0)
    rows = jnp.stack([
        first_gain, second_gain, third_gain, first_shift, second_shift, third_shift,
        column_sum(self_own), column_sum(cross_own), column_sum(down_own),
        at_head(cross_bias_sums[0]), at_head(cross_bias_sums[1]),
    ])
    rows = layout.total(jnp.concatenate([rows, up_sums.reshape(-1, width)]))
    rows, up_sums = rows[:11], rows[11:].reshape(up_sums.shape)
    late = layout.total(jnp.stack([at_head(self_bias_sums[0]), at_head(self_bias_sums[1])]))
    row_at = (lax.axis_index("rb") * 4 + me) * normgain.shape[1]
    col_at = lax.axis_index(layout.cols)
    by_row = lax.dynamic_slice_in_dim(rows[:9], row_at, normgain.shape[1], 1)
    crossbias_grad = lax.dynamic_slice_in_dim(rows[9:], col_at * block, block, 1)
    selfbias_grad = lax.dynamic_slice_in_dim(late, col_at * block, block, 1)
    upbias_grad = lax.dynamic_index_in_dim(up_sums, col_at, 0, keepdims=False).reshape(-1)
    join_rows = lambda blocks: blocks.reshape(-1, blocks.shape[2])
    return (
        layer_out,
        tokens_grad,
        encoder_grad,
        column_rows_back(selfqkv_grad, 3),
        selfbias_grad,
        join_rows(selfproj_grad),
        by_row[6],
        column_rows_back(crossquery_grad, 1)[:, 0],
        column_rows_back(crosskv_grad, 2),
        crossbias_grad,
        join_rows(crossproj_grad),
        by_row[7],
        column_rows_back(upweight_grad, 1)[:, 0],
        upbias_grad,
        join_rows(downweight_grad),
        by_row[8],
        by_row[:3],
        by_row[3:6],
    )


def solution(mesh):
    def run(*arrays):
        dp, row, col = (mesh.shape[name] for name in ("dp", "row", "col"))
        per_col = arrays[4].shape[2] // HD // col
        seqs = arrays[3].shape[0] // dp
        assert per_col == 4 and row % 4 == 0 and col % seqs == 0
        assert (row // 4) * (col // seqs) == col
        sizes = {"dp": dp, "rb": row // 4, "rx": 2, "rc": 2, "sq": seqs, "cs": col // seqs}
        grid = Mesh(mesh.devices.reshape(tuple(sizes.values())), tuple(sizes))
        rows, cols, tokens = ("rb", "rx", "rc"), ("sq", "cs"), ("dp", "sq", "cs")
        specs = {
            "tokens": P(tokens, rows), "rc": P(rows, cols), "cr": P(cols, rows), "r3c": P(rows, None, cols),
            "c": P(cols), "r": P(rows), "2c": P(None, cols), "2r": P(None, rows),
        }
        ins = (
            "tokens", "tokens", "tokens", "dp", "r3c", "2c", "cr", "r", "rc", "r3c", "2c", "cr", "r", "rc", "c", "cr", "r", "2r", "2r",
        )
        outs = (
            "tokens", "tokens", "tokens", "r3c", "2c", "cr", "r", "rc", "r3c", "2c", "cr", "r", "rc", "c", "cr", "r", "2r", "2r",
        )
        specs["dp"] = P("dp")
        body = functools.partial(shards, Layout(sizes))
        return jax.shard_map(
            body, mesh=grid, in_specs=tuple(specs[s] for s in ins), out_specs=tuple(specs[s] for s in outs),
            check_vma=False,
        )(*arrays)

    return run
```

```python
import functools
import jax
import jax.numpy as jnp
from jax import lax
from jax.experimental import pallas as pl
from jax.experimental.pallas import tpu as pltpu
from jax.sharding import Mesh
from jax.sharding import PartitionSpec as P

HD = 64
NEGATIVE = -1e30
F32 = jnp.float32
BF16 = jnp.bfloat16


def dot_nn(a, b):
    return lax.dot_general(a, b, (((1,), (0,)), ((), ())), preferred_element_type=F32)


def allowed_mask(first_key, first_query, prefix, shape):
    key_pos = first_key + lax.broadcasted_iota(jnp.int32, shape, 0)
    query_pos = first_query + lax.broadcasted_iota(jnp.int32, shape, 1)
    return (key_pos < prefix) | (key_pos <= query_pos)


def forward_kernel(masked, bq, bk, prefix_ref, q_ref, k_ref, v_ref, o_ref, low_ref, lse_ref, keys, values, acc, peak):
    chunks, _, chunk = k_ref.shape
    per = chunk // bk
    blocks = chunks * per
    step = pl.program_id(0)
    prefix = prefix_ref[0]

    @pl.when(step == 0)
    def _():
        for c in range(chunks):
            for b in range(per):
                i = c * per + b
                keys[i] = k_ref[c, :, b * bk:(b + 1) * bk].T
                values[i, :HD, :] = v_ref[c, :, b * bk:(b + 1) * bk]
                rows = lax.broadcasted_iota(jnp.int32, (16, bk), 0)
                values[i, HD:, :] = jnp.where(rows == 0, 1.0, 0.0).astype(BF16)

    first_query = step * bq
    query = q_ref[0]
    peak[...] = jnp.full(peak.shape, NEGATIVE, F32)
    acc[...] = jnp.zeros(acc.shape, F32)

    def visit(i, use_mask):
        scores = dot_nn(keys[i], query)
        if use_mask:
            scores = jnp.where(allowed_mask(i * bk, first_query, prefix, scores.shape), scores, NEGATIVE)
        old = peak[...]
        new = jnp.maximum(old, jnp.max(scores, axis=0, keepdims=True))
        weight = jnp.exp(scores - new).astype(BF16)
        acc[...] = acc[...] * jnp.exp(old - new) + dot_nn(values[i], weight)
        peak[...] = new

    if masked:
        full = jnp.maximum(prefix, first_query + 1) // bk
        stop = (jnp.maximum(prefix, first_query + bq) + bk - 1) // bk
        lax.fori_loop(0, full, lambda i, c: (visit(i, False), c)[1], 0)
        lax.fori_loop(full, stop, lambda i, c: (visit(i, True), c)[1], 0)
    else:
        lax.fori_loop(0, blocks, lambda i, c: (visit(i, False), c)[1], 0)
    total = acc[HD:HD + 1, :]
    out = acc[:HD, :] / total
    o_ref[0] = out
    low_ref[0] = out.astype(BF16)
    lse_ref[0] = peak[...] + jnp.log(total)


def flash_forward(prefix, queries, q_part, pairs, k_part, v_part, masked, bq=1024, bk=1024):
    chunks, _, chunk = queries.shape
    length = chunks * chunk
    per = chunk // bq
    whole = lambda part: pl.BlockSpec((chunks, HD, chunk), lambda i, p: (0, part, 0))
    mine = lambda rows: pl.BlockSpec((1, rows, bq), lambda i, p: (i // per, 0, i % per))
    return pl.pallas_call(
        functools.partial(forward_kernel, masked, bq, bk),
        out_shape=(
            jax.ShapeDtypeStruct((chunks, HD, chunk), F32),
            jax.ShapeDtypeStruct((chunks, HD, chunk), BF16),
            jax.ShapeDtypeStruct((chunks, 1, chunk), F32),
        ),
        grid_spec=pltpu.PrefetchScalarGridSpec(
            num_scalar_prefetch=1,
            grid=(length // bq,),
            in_specs=[
                pl.BlockSpec((1, HD, bq), lambda i, p: (i // per, q_part, i % per)),
                whole(k_part),
                whole(v_part),
            ],
            out_specs=[mine(HD), mine(HD), mine(1)],
            scratch_shapes=[
                pltpu.VMEM((length // bk, bk, HD), BF16),
                pltpu.VMEM((length // bk, HD + 16, bk), BF16),
                pltpu.VMEM((HD + 16, bq), F32),
                pltpu.VMEM((1, bq), F32),
            ],
        ),
        cost_estimate=pl.CostEstimate(
            flops=4 * HD * length * length, transcendentals=length * length, bytes_accessed=14 * HD * length
        ),
        name="attend_self" if masked else "attend_cross",
    )(prefix, queries, pairs, pairs)


def backward_kernel(masked, bq, bk, prefix_ref, q_ref, g_ref, o_ref, lse_ref, k_ref, v_ref,
                    dq_ref, dk_ref, dv_ref, rows_q, rows_g, delta, dq_acc, dk_acc, dv_acc):
    chunks, _, chunk = q_ref.shape
    per = chunk // bq
    blocks = chunks * per
    step = pl.program_id(0)
    prefix = prefix_ref[0]

    @pl.when(step == 0)
    def _():
        for c in range(chunks):
            for b in range(per):
                i = c * per + b
                at = slice(b * bq, (b + 1) * bq)
                grad = g_ref[c, :, at]
                rows_q[i] = q_ref[c, :, at].T
                rows_g[i] = grad.T
                delta[i] = jnp.sum(grad.astype(F32) * o_ref[c, :, at], axis=0, keepdims=True)
        dq_acc[...] = jnp.zeros(dq_acc.shape, F32)

    first_key = step * bk
    key_cols = k_ref[0]
    key_rows = key_cols.T
    value_rows = v_ref[0].T
    dk_acc[...] = jnp.zeros(dk_acc.shape, F32)
    dv_acc[...] = jnp.zeros(dv_acc.shape, F32)

    def visit(i, use_mask):
        c, at = i // per, pl.ds(pl.multiple_of((i % per) * bq, bq), bq)
        scores = dot_nn(key_rows, q_ref[c, :, at])
        if use_mask:
            scores = jnp.where(allowed_mask(first_key, i * bq, prefix, scores.shape), scores, NEGATIVE)
        probs = jnp.exp(scores - lse_ref[c, :, at])
        dprobs = dot_nn(value_rows, g_ref[c, :, at])
        dscore = (probs * (dprobs - delta[i])).astype(BF16)
        dv_acc[...] += dot_nn(probs.astype(BF16), rows_g[i])
        dk_acc[...] += dot_nn(dscore, rows_q[i])
        dq_acc[i] += dot_nn(key_cols, dscore)

    if masked:
        inside = first_key + bk <= prefix
        start = jnp.where(first_key < prefix, 0, first_key // bq)
        free = jnp.where(inside, 0, jnp.minimum((first_key + bk - 1 + bq - 1) // bq, blocks))
        lax.fori_loop(start, free, lambda i, c: (visit(i, True), c)[1], 0)
        lax.fori_loop(jnp.maximum(start, free), blocks, lambda i, c: (visit(i, False), c)[1], 0)
    else:
        lax.fori_loop(0, blocks, lambda i, c: (visit(i, False), c)[1], 0)
    dk_ref[0] = dk_acc[...].T.astype(BF16)
    dv_ref[0] = dv_acc[...].T.astype(BF16)

    @pl.when(step == pl.num_programs(0) - 1)
    def _():
        for c in range(chunks):
            for b in range(per):
                low = dq_acc[c * per + b].astype(BF16)
                dq_ref[c, :, b * bq:(b + 1) * bq] = low * jnp.asarray(HD ** -0.5, BF16)


def flash_backward(prefix, queries, q_part, pairs, k_part, v_part, grads, outputs, lse, masked, bq=1024, bk=1024):
    chunks, _, chunk = queries.shape
    length = chunks * chunk
    per = chunk // bk
    whole = lambda part, rows=HD: pl.BlockSpec((chunks, rows, chunk), lambda i, p: (0, part, 0))
    mine = lambda part: pl.BlockSpec((1, HD, bk), lambda i, p: (i // per, part, i % per))
    shape = jax.ShapeDtypeStruct((chunks, HD, chunk), BF16)
    return pl.pallas_call(
        functools.partial(backward_kernel, masked, bq, bk),
        out_shape=(shape, shape, shape),
        grid_spec=pltpu.PrefetchScalarGridSpec(
            num_scalar_prefetch=1,
            grid=(length // bk,),
            in_specs=[whole(q_part), whole(0), whole(0), whole(0, 1), mine(k_part), mine(v_part)],
            out_specs=[whole(0), mine(0), mine(0)],
            scratch_shapes=[
                pltpu.VMEM((length // bq, bq, HD), BF16),
                pltpu.VMEM((length // bq, bq, HD), BF16),
                pltpu.VMEM((length // bq, 1, bq), F32),
                pltpu.VMEM((length // bq, HD, bq), F32),
                pltpu.VMEM((bk, HD), F32),
                pltpu.VMEM((bk, HD), F32),
            ],
        ),
        cost_estimate=pl.CostEstimate(
            flops=10 * HD * length * length, transcendentals=length * length, bytes_accessed=20 * HD * length
        ),
        name="attend_self_back" if masked else "attend_cross_back",
    )(prefix, queries, grads, outputs, lse, pairs, pairs)


EPSILON = 1e-05
SCALE = HD ** -0.5


def contract(left, right, left_dim, right_dim):
    return lax.dot_general(
        left, right, (((left_dim,), (right_dim,)), ((), ())), preferred_element_type=F32
    )


class Layout:
    def __init__(self, sizes):
        self.sizes = sizes
        keep = lambda names: tuple(n for n in names if sizes[n] > 1) or names[-1:]
        self.team = ("rx", "rc")
        self.cols = keep(("sq", "cs"))
        self.ring = keep(("rb", "cs"))
        self.every = ("dp", "rb", "rx", "rc", "sq", "cs")

    def count(self, names):
        total = 1
        for name in names:
            total *= self.sizes[name]
        return total

    def me(self):
        return lax.axis_index("rx") * 2 + lax.axis_index("rc")

    def swap(self, value, bits):
        if bits == 1:
            return lax.ppermute(value, "rc", [(0, 1), (1, 0)])
        if bits == 2:
            return lax.ppermute(value, "rx", [(0, 1), (1, 0)])
        return lax.ppermute(value, self.team, [(i, i ^ 3) for i in range(4)])

    def place(self, parts, spots):
        out = jnp.zeros((len(parts),) + parts[0].shape, parts[0].dtype)
        for part, spot in zip(parts, spots):
            out = lax.dynamic_update_index_in_dim(out, part, spot, 0)
        return lax.optimization_barrier(out)

    def spots(self):
        me = self.me()
        return [me, me ^ 1, me ^ 2, me ^ 3]

    def team_parts(self, value):
        core, across = self.swap(value, 1), self.swap(value, 2)
        return [value, core, across, self.swap(across, 1)]

    def pick(self, blocks):
        return [lax.dynamic_index_in_dim(blocks, spot, 0, keepdims=False) for spot in self.spots()]

    def team_send(self, parts):
        return [parts[0]] + [self.swap(parts[bits], bits) for bits in (1, 2, 3)]

    def team_total(self, parts):
        away = self.swap(jnp.stack([parts[1].astype(BF16), parts[3].astype(BF16)]), 1).astype(F32)
        away_across = self.swap((parts[2] + away[1]).astype(BF16), 2).astype(F32)
        return (parts[0] + away[0]) + away_across

    def total(self, value):
        for name in self.every:
            bits = 1
            while bits < self.sizes[name]:
                pairs = [(i, i ^ bits) for i in range(self.sizes[name])]
                value = value + lax.ppermute(value, name, pairs)
                bits *= 2
        return value

    def column_vectors(self, vector):
        size = self.count(self.cols)
        me = lax.axis_index(self.cols)
        parts, spots = [vector], [me]
        for step in range(1, size):
            pairs = [(i, (i + step) % size) for i in range(size)]
            parts.append(lax.ppermute(vector, self.cols, pairs))
            spots.append((me + size - step) % size)
        return self.place(parts, spots)

    def ring_index(self):
        return lax.axis_index("cs") * self.sizes["rb"] + lax.axis_index("rb")

    def flip(self, blocks, first, second):
        first, second = self.sizes[first], self.sizes[second]
        if first == 1 or second == 1:
            return blocks
        return blocks.reshape((first, second) + blocks.shape[1:]).swapaxes(0, 1).reshape(blocks.shape)

    def ring_exchange(self, blocks):
        blocks = lax.all_to_all(self.flip(blocks, "cs", "rb"), self.ring, 0, 0, tiled=True)
        return self.flip(blocks, "rb", "cs")

    def ring_trickle(self, blocks):
        size = self.count(self.ring)
        me = lax.axis_index(self.ring)
        blocks = self.flip(blocks, "cs", "rb")
        pick = lambda step: lax.dynamic_index_in_dim(blocks, (me + step) % size, 0, keepdims=False)
        parts, spots = [pick(0)], [me]
        for step in range(1, size):
            parts.append(lax.ppermute(pick(step), self.ring, [(i, (i + step) % size) for i in range(size)]))
            spots.append((me + size - step) % size)
        return self.flip(self.place(parts, spots), "rb", "cs")

    def block_sum(self, value):
        return lax.psum_scatter(value, self.cols, scatter_dimension=0, tiled=True)

    def halves(self, value):
        if self.sizes["rb"] == 1:
            return value
        return lax.all_to_all(value, "rb", 0, 1, tiled=True)

    def unhalves(self, value):
        if self.sizes["rb"] == 1:
            return value
        return lax.all_to_all(value, "rb", 1, 0, tiled=True)

    def feature_parts(self, value):
        width = value.shape[1] // 4
        return [value[:, i * width:(i + 1) * width] for i in range(4)]

    def team_features(self, blocks):
        rb, rows = self.sizes["rb"], blocks.shape[1]
        return blocks.reshape(4, rows, rb, -1).transpose(1, 2, 0, 3).reshape(rows, -1)

    def member_blocks(self, value):
        rb, rows = self.sizes["rb"], value.shape[0]
        return value.reshape(rows, rb, 4, -1).transpose(2, 0, 1, 3).reshape(4, rows, -1)

    def widen(self, piece):
        if self.sizes["rb"] > 1:
            piece = lax.all_gather(piece, "rb", axis=2, tiled=True)
        piece = piece.reshape(piece.shape[0], -1)
        return lax.all_gather(piece[None], self.cols, axis=0, tiled=True)

    def in_order(self, weight):
        rb = self.sizes["rb"]
        if rb == 1:
            return weight
        parts = weight.reshape(weight.shape[:-1] + (4, rb, -1))
        return jnp.swapaxes(parts, -3, -2).reshape(weight.shape)

    def out_of_order(self, weight):
        rb = self.sizes["rb"]
        if rb == 1:
            return weight
        parts = weight.reshape(weight.shape[:-1] + (rb, 4, -1))
        return jnp.swapaxes(parts, -3, -2).reshape(weight.shape)

    def over_columns(self, partial):
        total = lax.psum_scatter(partial.astype(BF16), self.cols, scatter_dimension=0, tiled=True)
        total = total.reshape(total.shape[0], 4, -1)
        if self.sizes["rb"] > 1:
            total = lax.psum_scatter(total, "rb", scatter_dimension=2, tiled=True)
        return total

    def weight_grads(self, relative, absolute):
        flat = [[piece[:, i] for i in range(4)] for piece in relative]
        flat += [self.pick(piece.transpose(1, 0, 2)) for piece in absolute]
        sizes = [piece[0].shape[0] for piece in flat]
        parts = self.team_send([jnp.concatenate([piece[i] for piece in flat]) for i in range(4)])
        low = jnp.stack(parts)
        if self.sizes["dp"] == 2:
            low = low.astype(F32) + lax.ppermute(low, "dp", [(0, 1), (1, 0)]).astype(F32)
        else:
            low = lax.psum(low.astype(F32), "dp")
        parts = [low[i] for i in range(4)]
        low = self.place(parts, self.spots())
        out, at = [], 0
        for size in sizes:
            out.append(low[:, at:at + size])
            at += size
        return out


def norm_forward(hidden, gain_row, shift_row):
    average = jnp.mean(hidden, axis=1, keepdims=True)
    square = jnp.mean(hidden * hidden, axis=1, keepdims=True)
    inverse = lax.rsqrt(square - average * average + EPSILON)
    normed = (hidden - average) * inverse
    return normed * gain_row + shift_row, normed, inverse


def norm_backward(upstream, normed, inverse, gain_row):
    scaled = upstream * gain_row
    first = jnp.mean(scaled, axis=1, keepdims=True)
    second = jnp.mean(scaled * normed, axis=1, keepdims=True)
    grad = inverse * (scaled - first - normed * second)
    return grad, jnp.sum(upstream * normed, axis=0), jnp.sum(upstream, axis=0)


def exact_gelu(inputs):
    return jax.nn.gelu(inputs, approximate=False)


def column_rows(weight):
    features, parts, width = weight.shape
    blocks = weight.reshape(features, parts, 4, width // 4).transpose(2, 1, 3, 0)
    return blocks.reshape(4, -1, features)


def column_rows_back(blocks, parts):
    features = blocks.shape[2]
    return blocks.reshape(4, parts, -1, features).transpose(3, 1, 0, 2).reshape(features, parts, -1)


def shards(
    layout, tokens, encoder, cotangent, prefixes, selfqkv, selfbias, selfproj, selfshift, crossquery,
    crosskv, crossbias, crossproj, crossshift, upweight, upbias, downweight, downbias, normgain, normshift,
):
    me = layout.me()
    split_rows = lambda weight: weight.reshape(4, -1, weight.shape[1])

    def by_token(rows):
        return layout.halves(rows)

    def gather_weights(relative, absolute, order=None):
        pieces = relative + absolute
        sizes = [piece.shape[1] for piece in pieces]
        parts = layout.team_send(layout.pick(jnp.concatenate(pieces, axis=1)))
        at = sum(piece.shape[1] for piece in relative)
        groups = []
        if relative:
            groups.append(jnp.stack([part[:at] for part in parts], axis=1))
        if absolute:
            groups.append(layout.place([part[at:] for part in parts], layout.spots()).transpose(1, 0, 2))
        piece = jnp.concatenate(groups)
        if order is not None:
            piece, _ = lax.optimization_barrier((piece, order))
        wide = layout.widen(piece)
        out, at = [], 0
        for index, size in enumerate(sizes):
            weight = wide[:, at:at + size].reshape(-1, wide.shape[2])
            out.append(weight if index < len(relative) else layout.in_order(weight))
            at += size
        return out

    (qkv_w,) = gather_weights([column_rows(selfqkv)], [])
    token_parts = layout.team_parts(by_token(tokens))
    tokens_all = jnp.concatenate(token_parts, axis=1)
    width = tokens_all.shape[1]
    group = tokens_all.shape[0]
    own_rows = group // 4
    columns = layout.count(layout.cols)
    heads = columns

    by_col = jnp.concatenate([selfbias.reshape(-1), crossbias.reshape(-1), upbias])
    by_col = layout.column_vectors(by_col)
    block = selfbias.shape[1]
    head_biases = lax.dynamic_index_in_dim(
        by_col[:, : 4 * block].reshape(columns, 4, 4, HD), me, 2, keepdims=False
    )
    up_bias = lax.dynamic_index_in_dim(
        by_col[:, 4 * block:].reshape(columns, 4, -1), me, 1, keepdims=False
    ).reshape(1, -1)
    by_row = jnp.concatenate([selfshift[None], crossshift[None], downbias[None], normgain, normshift])
    if layout.sizes["rb"] > 1:
        by_row = lax.all_gather(by_row, "rb", axis=1, tiled=True)
    by_row = layout.team_features(layout.place(layout.team_parts(by_row), layout.spots()))
    self_shift, cross_shift, down_bias = by_row[0], by_row[1], by_row[2]
    gains, shifts = by_row[3:6], by_row[6:9]

    def gather_tokens(own):
        return jnp.concatenate(layout.team_parts(own))

    def reduce_tokens(partial):
        return layout.team_total([partial[i * own_rows:(i + 1) * own_rows] for i in range(4)])

    sequence_prefix = prefixes
    if layout.sizes["sq"] > 1:
        sequence_prefix = lax.dynamic_slice_in_dim(prefixes, lax.axis_index("sq"), 1, 0)

    kv_w, self_w, query_w, cross_w = gather_weights(
        [column_rows(crosskv)],
        [split_rows(selfproj), column_rows(crossquery[:, None]), split_rows(crossproj)],
    )
    encoder_all = jnp.concatenate(layout.team_parts(by_token(encoder)), axis=1)
    pair = contract(kv_w, encoder_all, 1, 1).reshape(heads, 2, HD, group)
    pair_bias = jnp.stack([jnp.zeros_like(head_biases[:, 3]), head_biases[:, 3]], axis=1)
    pair = (pair + pair_bias[..., None]).astype(BF16).reshape(heads, 2 * HD, group)

    qkv = contract(qkv_w, tokens_all, 1, 1).reshape(heads, 3, HD, group)
    qkv_bias = jnp.stack([head_biases[:, 0], jnp.zeros_like(head_biases[:, 0]), head_biases[:, 1]], axis=1)
    factor = jnp.array([SCALE, 1.0, 1.0], F32)[None, :, None, None]
    qkv = ((qkv + qkv_bias[..., None]) * factor).astype(BF16).reshape(heads, 3 * HD, group)
    self_set = layout.ring_exchange(qkv)
    self_set, pair = lax.optimization_barrier((self_set, pair))
    cross_set = layout.ring_trickle(pair)
    self_out, self_low, self_lse = flash_forward(sequence_prefix, self_set, 0, self_set, 1, 2, True)
    self_low, cross_set = lax.optimization_barrier((self_low, cross_set))
    attended = layout.ring_exchange(self_low).reshape(heads * HD, group)
    spots = layout.spots()
    up_w, down_w = gather_weights([], [column_rows(upweight[:, None]), split_rows(downweight)], self_low)

    upstream = layout.team_send(layout.pick(by_token(cotangent).reshape(4, own_rows, -1)))
    upstream = layout.team_features(layout.place(upstream, spots)).astype(F32)

    own_tokens = lax.dynamic_slice_in_dim(tokens_all, me * own_rows, own_rows, 0)
    own_tokens = layout.place(layout.feature_parts(own_tokens), spots)
    own_tokens = layout.team_features(own_tokens).astype(F32)
    self_partial = contract(attended, self_w, 0, 0).reshape(4, own_rows, width)
    first_sum = own_tokens + (layout.team_total(layout.pick(self_partial)) + self_shift)
    first_out, first_normed, first_inverse = norm_forward(first_sum, gains[0], shifts[0])
    first_all = gather_tokens(first_out.astype(BF16))

    query = contract(query_w, first_all, 1, 1).reshape(heads, HD, group)
    query = ((query + head_biases[:, 2][..., None]) * SCALE).astype(BF16)
    cross_query = layout.ring_exchange(query)
    cross_out, cross_low, cross_lse = flash_forward(sequence_prefix, cross_query, 0, cross_set, 0, 1, False)
    crossed = layout.ring_exchange(cross_low).reshape(heads * HD, group)
    second_sum = first_out + (reduce_tokens(contract(crossed, cross_w, 0, 0)) + cross_shift)
    second_out, second_normed, second_inverse = norm_forward(second_sum, gains[1], shifts[1])
    second_all = gather_tokens(second_out.astype(BF16))

    hidden_pre = contract(second_all, up_w, 1, 1) + up_bias
    hidden_act = exact_gelu(hidden_pre).astype(BF16)
    third_sum = second_out + (reduce_tokens(contract(hidden_act, down_w, 1, 0)) + down_bias)
    third_out, third_normed, third_inverse = norm_forward(third_sum, gains[2], shifts[2])
    layer_out = third_out.astype(BF16)
    layer_out = layout.team_send(layout.pick(layout.member_blocks(layer_out)))
    layer_out = layout.unhalves(layout.place(layer_out, spots).reshape(group, -1))

    third_grad, third_gain, third_shift = norm_backward(upstream, third_normed, third_inverse, gains[2])
    down_own = third_grad.astype(BF16)
    down_all = gather_tokens(down_own)
    act_grad = contract(down_all, down_w, 1, 1)
    pre_low = jax.vjp(exact_gelu, hidden_pre)[1](act_grad)[0].astype(BF16)
    second_grad = third_grad + reduce_tokens(contract(pre_low, up_w, 1, 0))
    down_sum = layout.over_columns(layout.out_of_order(contract(hidden_act, down_all, 0, 0)))
    up_sum = layout.over_columns(layout.out_of_order(contract(pre_low, second_all, 0, 0)))
    mid_grad, second_gain, second_shift = norm_backward(second_grad, second_normed, second_inverse, gains[1])
    cross_own = mid_grad.astype(BF16)
    cross_all = gather_tokens(cross_own)
    crossed_grad = contract(cross_w, cross_all, 1, 1).astype(BF16).reshape(heads, HD, group)
    crossed_grad = layout.ring_exchange(crossed_grad)
    crossproj_part = contract(crossed, cross_all, 1, 0).astype(BF16)
    crossed_grad, crossproj_part = lax.optimization_barrier((crossed_grad, crossproj_part))
    crossproj_sum = layout.over_columns(layout.out_of_order(crossproj_part))
    dquery, dkeys, dvalues = flash_backward(
        sequence_prefix, cross_query, 0, cross_set, 0, 1, crossed_grad, cross_out, cross_lse, False
    )
    cross_bias_sums = (jnp.sum(dquery.astype(F32), axis=(0, 2)), jnp.sum(dvalues.astype(F32), axis=(0, 2)))
    dquery = layout.ring_exchange(dquery).reshape(heads * HD, group)
    first_grad = mid_grad + reduce_tokens(contract(dquery, query_w, 0, 0))
    dpair = layout.ring_trickle(jnp.concatenate([dkeys, dvalues], axis=1)).reshape(heads * 2 * HD, group)
    crossquery_sum = layout.over_columns(layout.out_of_order(contract(dquery, first_all, 1, 0)))
    crosskv_sum = layout.over_columns(contract(dpair, encoder_all, 1, 0))
    encoder_grad = layout.team_total(layout.feature_parts(contract(dpair, kv_w, 0, 0)))
    encoder_grad = layout.unhalves(encoder_grad)
    low_grad, first_gain, first_shift = norm_backward(first_grad, first_normed, first_inverse, gains[0])
    self_own = low_grad.astype(BF16)
    self_all = layout.place(layout.team_parts(self_own), spots).reshape(group, width)
    attended_grad = contract(self_w, self_all, 1, 1).astype(BF16).reshape(heads, HD, group)
    attended_grad = layout.ring_exchange(attended_grad)
    selfproj_part = contract(attended, self_all, 1, 0).astype(BF16)
    sums = (up_sum, down_sum, crossproj_sum)
    attended_grad, selfproj_part, sums = lax.optimization_barrier((attended_grad, selfproj_part, sums))
    early_grads = layout.weight_grads([], list(sums))
    selfproj_sum = layout.over_columns(layout.out_of_order(selfproj_part))
    dq, dk, dv = flash_backward(
        sequence_prefix, self_set, 0, self_set, 1, 2, attended_grad, self_out, self_lse, True
    )
    dq, dk, dv, early_grads, selfproj_sum = lax.optimization_barrier((dq, dk, dv, early_grads, selfproj_sum))
    upweight_grad, downweight_grad, crossproj_grad = early_grads
    crosskv_grad, selfproj_grad, crossquery_grad = layout.weight_grads(
        [crosskv_sum], [selfproj_sum, crossquery_sum]
    )
    self_bias_sums = (jnp.sum(dq.astype(F32), axis=(0, 2)), jnp.sum(dv.astype(F32), axis=(0, 2)))
    dqkv = layout.ring_exchange(jnp.concatenate([dq, dk, dv], axis=1)).reshape(heads * 3 * HD, group)
    selfqkv_sum = layout.over_columns(contract(dqkv, tokens_all, 1, 0))
    (selfqkv_grad,) = layout.weight_grads([selfqkv_sum], [])
    tokens_part = contract(dqkv, qkv_w, 0, 0)
    low_parts = jnp.concatenate(layout.pick(layout.member_blocks(low_grad)), axis=1)
    mine = lax.dynamic_slice_in_dim(tokens_part, me * own_rows, own_rows, 0) + low_parts
    tokens_part = lax.dynamic_update_slice_in_dim(tokens_part, mine, me * own_rows, 0)
    tokens_grad = layout.unhalves(layout.team_total(layout.feature_parts(tokens_part)))

    def at_head(sums):
        spot = (layout.ring_index() * 4 + me) * HD
        return lax.dynamic_update_slice_in_dim(jnp.zeros((width,), F32), sums, spot, 0)

    up_sums = jnp.zeros((columns, 4, pre_low.shape[1] // columns), F32)
    up_sums = lax.dynamic_update_index_in_dim(
        up_sums, jnp.sum(pre_low.astype(F32), axis=0).reshape(columns, -1), me, 1
    )
    column_sum = lambda low: jnp.sum(low.astype(F32), axis=0)
    rows = jnp.stack([
        first_gain, second_gain, third_gain, first_shift, second_shift, third_shift,
        column_sum(self_own), column_sum(cross_own), column_sum(down_own),
        at_head(cross_bias_sums[0]), at_head(cross_bias_sums[1]),
    ])
    rows = layout.total(jnp.concatenate([rows, up_sums.reshape(-1, width)]))
    rows, up_sums = rows[:11], rows[11:].reshape(up_sums.shape)
    late = layout.total(jnp.stack([at_head(self_bias_sums[0]), at_head(self_bias_sums[1])]))
    row_at = (lax.axis_index("rb") * 4 + me) * normgain.shape[1]
    col_at = lax.axis_index(layout.cols)
    by_row = lax.dynamic_slice_in_dim(rows[:9], row_at, normgain.shape[1], 1)
    crossbias_grad = lax.dynamic_slice_in_dim(rows[9:], col_at * block, block, 1)
    selfbias_grad = lax.dynamic_slice_in_dim(late, col_at * block, block, 1)
    upbias_grad = lax.dynamic_index_in_dim(up_sums, col_at, 0, keepdims=False).reshape(-1)
    join_rows = lambda blocks: blocks.reshape(-1, blocks.shape[2])
    return (
        layer_out,
        tokens_grad,
        encoder_grad,
        column_rows_back(selfqkv_grad, 3),
        selfbias_grad,
        join_rows(selfproj_grad),
        by_row[6],
        column_rows_back(crossquery_grad, 1)[:, 0],
        column_rows_back(crosskv_grad, 2),
        crossbias_grad,
        join_rows(crossproj_grad),
        by_row[7],
        column_rows_back(upweight_grad, 1)[:, 0],
        upbias_grad,
        join_rows(downweight_grad),
        by_row[8],
        by_row[:3],
        by_row[3:6],
    )


def solution(mesh):
    def run(*arrays):
        dp, row, col = (mesh.shape[name] for name in ("dp", "row", "col"))
        per_col = arrays[4].shape[2] // HD // col
        seqs = arrays[3].shape[0] // dp
        assert per_col == 4 and row % 4 == 0 and col % seqs == 0
        assert (row // 4) * (col // seqs) == col
        sizes = {"dp": dp, "rb": row // 4, "rx": 2, "rc": 2, "sq": seqs, "cs": col // seqs}
        grid = Mesh(mesh.devices.reshape(tuple(sizes.values())), tuple(sizes))
        rows, cols, tokens = ("rb", "rx", "rc"), ("sq", "cs"), ("dp", "sq", "cs")
        specs = {
            "tokens": P(tokens, rows), "rc": P(rows, cols), "cr": P(cols, rows), "r3c": P(rows, None, cols),
            "c": P(cols), "r": P(rows), "2c": P(None, cols), "2r": P(None, rows),
        }
        ins = (
            "tokens", "tokens", "tokens", "dp", "r3c", "2c", "cr", "r", "rc", "r3c", "2c", "cr", "r", "rc", "c", "cr", "r", "2r", "2r",
        )
        outs = (
            "tokens", "tokens", "tokens", "r3c", "2c", "cr", "r", "rc", "r3c", "2c", "cr", "r", "rc", "c", "cr", "r", "2r", "2r",
        )
        specs["dp"] = P("dp")
        body = functools.partial(shards, Layout(sizes))
        return jax.shard_map(
            body, mesh=grid, in_specs=tuple(specs[s] for s in ins), out_specs=tuple(specs[s] for s in outs),
            check_vma=False,
        )(*arrays)

    return run
```

```python
import functools
import jax
import jax.numpy as jnp
from jax import lax
from jax.experimental import pallas as pl
from jax.experimental.pallas import tpu as pltpu
from jax.sharding import Mesh
from jax.sharding import PartitionSpec as P

HD = 64
NEGATIVE = -1e30
F32 = jnp.float32
BF16 = jnp.bfloat16


def dot_nn(a, b):
    return lax.dot_general(a, b, (((1,), (0,)), ((), ())), preferred_element_type=F32)


def allowed_mask(first_key, first_query, prefix, shape):
    key_pos = first_key + lax.broadcasted_iota(jnp.int32, shape, 0)
    query_pos = first_query + lax.broadcasted_iota(jnp.int32, shape, 1)
    return (key_pos < prefix) | (key_pos <= query_pos)


def forward_kernel(masked, bq, bk, prefix_ref, q_ref, k_ref, v_ref, o_ref, low_ref, lse_ref, keys, values, acc, peak):
    chunks, _, chunk = k_ref.shape
    per = chunk // bk
    blocks = chunks * per
    step = pl.program_id(0)
    prefix = prefix_ref[0]

    @pl.when(step == 0)
    def _():
        for c in range(chunks):
            for b in range(per):
                i = c * per + b
                keys[i] = k_ref[c, :, b * bk:(b + 1) * bk].T
                values[i, :HD, :] = v_ref[c, :, b * bk:(b + 1) * bk]
                rows = lax.broadcasted_iota(jnp.int32, (16, bk), 0)
                values[i, HD:, :] = jnp.where(rows == 0, 1.0, 0.0).astype(BF16)

    first_query = step * bq
    query = q_ref[0]
    peak[...] = jnp.full(peak.shape, NEGATIVE, F32)
    acc[...] = jnp.zeros(acc.shape, F32)

    def visit(i, use_mask):
        scores = dot_nn(keys[i], query)
        if use_mask:
            scores = jnp.where(allowed_mask(i * bk, first_query, prefix, scores.shape), scores, NEGATIVE)
        old = peak[...]
        new = jnp.maximum(old, jnp.max(scores, axis=0, keepdims=True))
        weight = jnp.exp(scores - new).astype(BF16)
        acc[...] = acc[...] * jnp.exp(old - new) + dot_nn(values[i], weight)
        peak[...] = new

    if masked:
        full = jnp.maximum(prefix, first_query + 1) // bk
        stop = (jnp.maximum(prefix, first_query + bq) + bk - 1) // bk
        lax.fori_loop(0, full, lambda i, c: (visit(i, False), c)[1], 0)
        lax.fori_loop(full, stop, lambda i, c: (visit(i, True), c)[1], 0)
    else:
        lax.fori_loop(0, blocks, lambda i, c: (visit(i, False), c)[1], 0)
    total = acc[HD:HD + 1, :]
    out = acc[:HD, :] / total
    o_ref[0] = out
    low_ref[0] = out.astype(BF16)
    lse_ref[0] = peak[...] + jnp.log(total)


def flash_forward(prefix, queries, q_part, pairs, k_part, v_part, masked, bq=1024, bk=1024):
    chunks, _, chunk = queries.shape
    length = chunks * chunk
    per = chunk // bq
    whole = lambda part: pl.BlockSpec((chunks, HD, chunk), lambda i, p: (0, part, 0))
    mine = lambda rows: pl.BlockSpec((1, rows, bq), lambda i, p: (i // per, 0, i % per))
    return pl.pallas_call(
        functools.partial(forward_kernel, masked, bq, bk),
        out_shape=(
            jax.ShapeDtypeStruct((chunks, HD, chunk), F32),
            jax.ShapeDtypeStruct((chunks, HD, chunk), BF16),
            jax.ShapeDtypeStruct((chunks, 1, chunk), F32),
        ),
        grid_spec=pltpu.PrefetchScalarGridSpec(
            num_scalar_prefetch=1,
            grid=(length // bq,),
            in_specs=[
                pl.BlockSpec((1, HD, bq), lambda i, p: (i // per, q_part, i % per)),
                whole(k_part),
                whole(v_part),
            ],
            out_specs=[mine(HD), mine(HD), mine(1)],
            scratch_shapes=[
                pltpu.VMEM((length // bk, bk, HD), BF16),
                pltpu.VMEM((length // bk, HD + 16, bk), BF16),
                pltpu.VMEM((HD + 16, bq), F32),
                pltpu.VMEM((1, bq), F32),
            ],
        ),
        cost_estimate=pl.CostEstimate(
            flops=4 * HD * length * length, transcendentals=length * length, bytes_accessed=14 * HD * length
        ),
        name="attend_self" if masked else "attend_cross",
    )(prefix, queries, pairs, pairs)


def backward_kernel(masked, bq, bk, prefix_ref, q_ref, g_ref, o_ref, lse_ref, k_ref, v_ref,
                    dq_ref, dk_ref, dv_ref, rows_q, rows_g, delta, dq_acc, dk_acc, dv_acc):
    chunks, _, chunk = q_ref.shape
    per = chunk // bq
    blocks = chunks * per
    step = pl.program_id(0)
    prefix = prefix_ref[0]

    @pl.when(step == 0)
    def _():
        for c in range(chunks):
            for b in range(per):
                i = c * per + b
                at = slice(b * bq, (b + 1) * bq)
                grad = g_ref[c, :, at]
                rows_q[i] = q_ref[c, :, at].T
                rows_g[i] = grad.T
                delta[i] = jnp.sum(grad.astype(F32) * o_ref[c, :, at], axis=0, keepdims=True)
        dq_acc[...] = jnp.zeros(dq_acc.shape, F32)

    first_key = step * bk
    key_cols = k_ref[0]
    key_rows = key_cols.T
    value_rows = v_ref[0].T
    dk_acc[...] = jnp.zeros(dk_acc.shape, F32)
    dv_acc[...] = jnp.zeros(dv_acc.shape, F32)

    def visit(i, use_mask):
        c, at = i // per, pl.ds(pl.multiple_of((i % per) * bq, bq), bq)
        scores = dot_nn(key_rows, q_ref[c, :, at])
        if use_mask:
            scores = jnp.where(allowed_mask(first_key, i * bq, prefix, scores.shape), scores, NEGATIVE)
        probs = jnp.exp(scores - lse_ref[c, :, at])
        dprobs = dot_nn(value_rows, g_ref[c, :, at])
        dscore = (probs * (dprobs - delta[i])).astype(BF16)
        dv_acc[...] += dot_nn(probs.astype(BF16), rows_g[i])
        dk_acc[...] += dot_nn(dscore, rows_q[i])
        dq_acc[i] += dot_nn(key_cols, dscore)

    if masked:
        inside = first_key + bk <= prefix
        start = jnp.where(first_key < prefix, 0, first_key // bq)
        free = jnp.where(inside, 0, jnp.minimum((first_key + bk - 1 + bq - 1) // bq, blocks))
        lax.fori_loop(start, free, lambda i, c: (visit(i, True), c)[1], 0)
        lax.fori_loop(jnp.maximum(start, free), blocks, lambda i, c: (visit(i, False), c)[1], 0)
    else:
        lax.fori_loop(0, blocks, lambda i, c: (visit(i, False), c)[1], 0)
    dk_ref[0] = dk_acc[...].T.astype(BF16)
    dv_ref[0] = dv_acc[...].T.astype(BF16)

    @pl.when(step == pl.num_programs(0) - 1)
    def _():
        for c in range(chunks):
            for b in range(per):
                low = dq_acc[c * per + b].astype(BF16)
                dq_ref[c, :, b * bq:(b + 1) * bq] = low * jnp.asarray(HD ** -0.5, BF16)


def flash_backward(prefix, queries, q_part, pairs, k_part, v_part, grads, outputs, lse, masked, bq=1024, bk=1024):
    chunks, _, chunk = queries.shape
    length = chunks * chunk
    per = chunk // bk
    whole = lambda part, rows=HD: pl.BlockSpec((chunks, rows, chunk), lambda i, p: (0, part, 0))
    mine = lambda part: pl.BlockSpec((1, HD, bk), lambda i, p: (i // per, part, i % per))
    shape = jax.ShapeDtypeStruct((chunks, HD, chunk), BF16)
    return pl.pallas_call(
        functools.partial(backward_kernel, masked, bq, bk),
        out_shape=(shape, shape, shape),
        grid_spec=pltpu.PrefetchScalarGridSpec(
            num_scalar_prefetch=1,
            grid=(length // bk,),
            in_specs=[whole(q_part), whole(0), whole(0), whole(0, 1), mine(k_part), mine(v_part)],
            out_specs=[whole(0), mine(0), mine(0)],
            scratch_shapes=[
                pltpu.VMEM((length // bq, bq, HD), BF16),
                pltpu.VMEM((length // bq, bq, HD), BF16),
                pltpu.VMEM((length // bq, 1, bq), F32),
                pltpu.VMEM((length // bq, HD, bq), F32),
                pltpu.VMEM((bk, HD), F32),
                pltpu.VMEM((bk, HD), F32),
            ],
        ),
        cost_estimate=pl.CostEstimate(
            flops=10 * HD * length * length, transcendentals=length * length, bytes_accessed=20 * HD * length
        ),
        name="attend_self_back" if masked else "attend_cross_back",
    )(prefix, queries, grads, outputs, lse, pairs, pairs)


EPSILON = 1e-05
SCALE = HD ** -0.5


def contract(left, right, left_dim, right_dim):
    return lax.dot_general(
        left, right, (((left_dim,), (right_dim,)), ((), ())), preferred_element_type=F32
    )


class Layout:
    def __init__(self, sizes):
        self.sizes = sizes
        keep = lambda names: tuple(n for n in names if sizes[n] > 1) or names[-1:]
        self.team = ("rx", "rc")
        self.cols = keep(("sq", "cs"))
        self.ring = keep(("rb", "cs"))
        self.every = ("dp", "rb", "rx", "rc", "sq", "cs")

    def count(self, names):
        total = 1
        for name in names:
            total *= self.sizes[name]
        return total

    def me(self):
        return lax.axis_index("rx") * 2 + lax.axis_index("rc")

    def swap(self, value, bits):
        if bits == 1:
            return lax.ppermute(value, "rc", [(0, 1), (1, 0)])
        if bits == 2:
            return lax.ppermute(value, "rx", [(0, 1), (1, 0)])
        return lax.ppermute(value, self.team, [(i, i ^ 3) for i in range(4)])

    def place(self, parts, spots):
        out = jnp.zeros((len(parts),) + parts[0].shape, parts[0].dtype)
        for part, spot in zip(parts, spots):
            out = lax.dynamic_update_index_in_dim(out, part, spot, 0)
        return lax.optimization_barrier(out)

    def spots(self):
        me = self.me()
        return [me, me ^ 1, me ^ 2, me ^ 3]

    def team_parts(self, value):
        core, across = self.swap(value, 1), self.swap(value, 2)
        return [value, core, across, self.swap(across, 1)]

    def pick(self, blocks):
        return [lax.dynamic_index_in_dim(blocks, spot, 0, keepdims=False) for spot in self.spots()]

    def team_send(self, parts):
        return [parts[0]] + [self.swap(parts[bits], bits) for bits in (1, 2, 3)]

    def team_total(self, parts):
        away = self.swap(jnp.stack([parts[1].astype(BF16), parts[3].astype(BF16)]), 1).astype(F32)
        away_across = self.swap((parts[2] + away[1]).astype(BF16), 2).astype(F32)
        return (parts[0] + away[0]) + away_across

    def total(self, value):
        for name in self.every:
            bits = 1
            while bits < self.sizes[name]:
                pairs = [(i, i ^ bits) for i in range(self.sizes[name])]
                value = value + lax.ppermute(value, name, pairs)
                bits *= 2
        return value

    def column_vectors(self, vector):
        size = self.count(self.cols)
        me = lax.axis_index(self.cols)
        parts, spots = [vector], [me]
        for step in range(1, size):
            pairs = [(i, (i + step) % size) for i in range(size)]
            parts.append(lax.ppermute(vector, self.cols, pairs))
            spots.append((me + size - step) % size)
        return self.place(parts, spots)

    def ring_index(self):
        return lax.axis_index("cs") * self.sizes["rb"] + lax.axis_index("rb")

    def flip(self, blocks, first, second):
        first, second = self.sizes[first], self.sizes[second]
        if first == 1 or second == 1:
            return blocks
        return blocks.reshape((first, second) + blocks.shape[1:]).swapaxes(0, 1).reshape(blocks.shape)

    def ring_exchange(self, blocks):
        blocks = lax.all_to_all(self.flip(blocks, "cs", "rb"), self.ring, 0, 0, tiled=True)
        return self.flip(blocks, "rb", "cs")

    def ring_trickle(self, blocks):
        size = self.count(self.ring)
        me = lax.axis_index(self.ring)
        blocks = self.flip(blocks, "cs", "rb")
        pick = lambda step: lax.dynamic_index_in_dim(blocks, (me + step) % size, 0, keepdims=False)
        parts, spots = [pick(0)], [me]
        for step in range(1, size):
            parts.append(lax.ppermute(pick(step), self.ring, [(i, (i + step) % size) for i in range(size)]))
            spots.append((me + size - step) % size)
        return self.flip(self.place(parts, spots), "rb", "cs")

    def block_sum(self, value):
        return lax.psum_scatter(value, self.cols, scatter_dimension=0, tiled=True)

    def halves(self, value):
        if self.sizes["rb"] == 1:
            return value
        return lax.all_to_all(value, "rb", 0, 1, tiled=True)

    def unhalves(self, value):
        if self.sizes["rb"] == 1:
            return value
        return lax.all_to_all(value, "rb", 1, 0, tiled=True)

    def feature_parts(self, value):
        width = value.shape[1] // 4
        return [value[:, i * width:(i + 1) * width] for i in range(4)]

    def team_features(self, blocks):
        rb, rows = self.sizes["rb"], blocks.shape[1]
        return blocks.reshape(4, rows, rb, -1).transpose(1, 2, 0, 3).reshape(rows, -1)

    def member_blocks(self, value):
        rb, rows = self.sizes["rb"], value.shape[0]
        return value.reshape(rows, rb, 4, -1).transpose(2, 0, 1, 3).reshape(4, rows, -1)

    def widen(self, piece):
        if self.sizes["rb"] > 1:
            piece = lax.all_gather(piece, "rb", axis=2, tiled=True)
        piece = piece.reshape(piece.shape[0], -1)
        return lax.all_gather(piece[None], self.cols, axis=0, tiled=True)

    def in_order(self, weight):
        rb = self.sizes["rb"]
        if rb == 1:
            return weight
        parts = weight.reshape(weight.shape[:-1] + (4, rb, -1))
        return jnp.swapaxes(parts, -3, -2).reshape(weight.shape)

    def out_of_order(self, weight):
        rb = self.sizes["rb"]
        if rb == 1:
            return weight
        parts = weight.reshape(weight.shape[:-1] + (rb, 4, -1))
        return jnp.swapaxes(parts, -3, -2).reshape(weight.shape)

    def over_columns(self, partial):
        total = lax.psum_scatter(partial.astype(BF16), self.cols, scatter_dimension=0, tiled=True)
        total = total.reshape(total.shape[0], 4, -1)
        if self.sizes["rb"] > 1:
            total = lax.psum_scatter(total, "rb", scatter_dimension=2, tiled=True)
        return total

    def weight_grads(self, relative, absolute):
        flat = [[piece[:, i] for i in range(4)] for piece in relative]
        flat += [self.pick(piece.transpose(1, 0, 2)) for piece in absolute]
        sizes = [piece[0].shape[0] for piece in flat]
        parts = self.team_send([jnp.concatenate([piece[i] for piece in flat]) for i in range(4)])
        low = jnp.stack(parts)
        if self.sizes["dp"] == 2:
            low = low.astype(F32) + lax.ppermute(low, "dp", [(0, 1), (1, 0)]).astype(F32)
        else:
            low = lax.psum(low.astype(F32), "dp")
        parts = [low[i] for i in range(4)]
        low = self.place(parts, self.spots())
        out, at = [], 0
        for size in sizes:
            out.append(low[:, at:at + size])
            at += size
        return out


def norm_forward(hidden, gain_row, shift_row):
    average = jnp.mean(hidden, axis=1, keepdims=True)
    square = jnp.mean(hidden * hidden, axis=1, keepdims=True)
    inverse = lax.rsqrt(square - average * average + EPSILON)
    normed = (hidden - average) * inverse
    return normed * gain_row + shift_row, normed, inverse


def norm_backward(upstream, normed, inverse, gain_row):
    scaled = upstream * gain_row
    first = jnp.mean(scaled, axis=1, keepdims=True)
    second = jnp.mean(scaled * normed, axis=1, keepdims=True)
    grad = inverse * (scaled - first - normed * second)
    return grad, jnp.sum(upstream * normed, axis=0), jnp.sum(upstream, axis=0)


def normal_below(inputs):
    return 0.5 * (1.0 + lax.erf(inputs * 0.5 ** 0.5))


def gelu_slope(inputs):
    return normal_below(inputs) + inputs * jnp.exp(-0.5 * inputs * inputs) * (2.0 * jnp.pi) ** -0.5


def column_rows(weight):
    features, parts, width = weight.shape
    blocks = weight.reshape(features, parts, 4, width // 4).transpose(2, 1, 3, 0)
    return blocks.reshape(4, -1, features)


def column_rows_back(blocks, parts):
    features = blocks.shape[2]
    return blocks.reshape(4, parts, -1, features).transpose(3, 1, 0, 2).reshape(features, parts, -1)


def shards(
    layout, tokens, encoder, cotangent, prefixes, selfqkv, selfbias, selfproj, selfshift, crossquery,
    crosskv, crossbias, crossproj, crossshift, upweight, upbias, downweight, downbias, normgain, normshift,
):
    me = layout.me()
    split_rows = lambda weight: weight.reshape(4, -1, weight.shape[1])

    def by_token(rows):
        return layout.halves(rows)

    def gather_weights(relative, absolute, widen=None):
        pieces = relative + absolute
        sizes = [piece.shape[1] for piece in pieces]
        parts = layout.team_send(layout.pick(jnp.concatenate(pieces, axis=1)))
        at = sum(piece.shape[1] for piece in relative)
        groups = []
        if relative:
            groups.append(jnp.stack([part[:at] for part in parts], axis=1))
        if absolute:
            groups.append(layout.place([part[at:] for part in parts], layout.spots()).transpose(1, 0, 2))
        piece = jnp.concatenate(groups)
        wide = layout.widen(piece) if widen is None else widen(piece)
        out, at = [], 0
        for index, size in enumerate(sizes):
            weight = wide[:, at:at + size].reshape(-1, wide.shape[2])
            out.append(weight if index < len(relative) else layout.in_order(weight))
            at += size
        return out

    (qkv_w,) = gather_weights([column_rows(selfqkv)], [])
    token_parts = layout.team_parts(by_token(tokens))
    tokens_all = jnp.concatenate(token_parts, axis=1)
    width = tokens_all.shape[1]
    group = tokens_all.shape[0]
    own_rows = group // 4
    columns = layout.count(layout.cols)
    heads = columns

    by_col = jnp.concatenate([selfbias.reshape(-1), crossbias.reshape(-1), upbias])
    by_col = layout.column_vectors(by_col)
    block = selfbias.shape[1]
    head_biases = lax.dynamic_index_in_dim(
        by_col[:, : 4 * block].reshape(columns, 4, 4, HD), me, 2, keepdims=False
    )
    up_bias = lax.dynamic_index_in_dim(
        by_col[:, 4 * block:].reshape(columns, 4, -1), me, 1, keepdims=False
    ).reshape(1, -1)
    by_row = jnp.concatenate([selfshift[None], crossshift[None], downbias[None], normgain, normshift])
    if layout.sizes["rb"] > 1:
        by_row = lax.all_gather(by_row, "rb", axis=1, tiled=True)
    by_row = layout.team_features(layout.place(layout.team_parts(by_row), layout.spots()))
    self_shift, cross_shift, down_bias = by_row[0], by_row[1], by_row[2]
    gains, shifts = by_row[3:6], by_row[6:9]

    def gather_tokens(own):
        return jnp.concatenate(layout.team_parts(own))

    def reduce_tokens(partial):
        return layout.team_total([partial[i * own_rows:(i + 1) * own_rows] for i in range(4)])

    sequence_prefix = prefixes
    if layout.sizes["sq"] > 1:
        sequence_prefix = lax.dynamic_slice_in_dim(prefixes, lax.axis_index("sq"), 1, 0)

    kv_w, self_w, query_w, cross_w = gather_weights(
        [column_rows(crosskv)],
        [split_rows(selfproj), column_rows(crossquery[:, None]), split_rows(crossproj)],
    )
    encoder_all = jnp.concatenate(layout.team_parts(by_token(encoder)), axis=1)
    pair = contract(kv_w, encoder_all, 1, 1).reshape(heads, 2, HD, group)
    pair_bias = jnp.stack([jnp.zeros_like(head_biases[:, 3]), head_biases[:, 3]], axis=1)
    pair = (pair + pair_bias[..., None]).astype(BF16).reshape(heads, 2 * HD, group)

    qkv = contract(qkv_w, tokens_all, 1, 1).reshape(heads, 3, HD, group)
    qkv_bias = jnp.stack([head_biases[:, 0], jnp.zeros_like(head_biases[:, 0]), head_biases[:, 1]], axis=1)
    factor = jnp.array([SCALE, 1.0, 1.0], F32)[None, :, None, None]
    qkv = ((qkv + qkv_bias[..., None]) * factor).astype(BF16).reshape(heads, 3 * HD, group)
    self_set = layout.ring_exchange(qkv)
    self_set, pair = lax.optimization_barrier((self_set, pair))
    cross_set = layout.ring_trickle(pair)
    self_out, self_low, self_lse = flash_forward(sequence_prefix, self_set, 0, self_set, 1, 2, True)
    later = []

    def widen_after(piece, low=self_low, pairs=cross_set):
        low, pairs, piece = lax.optimization_barrier((low, pairs, piece))
        later.extend([low, pairs])
        return layout.widen(piece)

    spots = layout.spots()
    up_w, down_w = gather_weights([], [column_rows(upweight[:, None]), split_rows(downweight)], widen_after)
    self_low, cross_set = later
    attended = layout.ring_exchange(self_low).reshape(heads * HD, group)

    upstream = layout.team_send(layout.pick(by_token(cotangent).reshape(4, own_rows, -1)))
    upstream = layout.team_features(layout.place(upstream, spots)).astype(F32)

    own_tokens = lax.dynamic_slice_in_dim(tokens_all, me * own_rows, own_rows, 0)
    own_tokens = layout.place(layout.feature_parts(own_tokens), spots)
    own_tokens = layout.team_features(own_tokens).astype(F32)
    self_partial = contract(attended, self_w, 0, 0).reshape(4, own_rows, width)
    first_sum = own_tokens + (layout.team_total(layout.pick(self_partial)) + self_shift)
    first_out, first_normed, first_inverse = norm_forward(first_sum, gains[0], shifts[0])
    first_all = gather_tokens(first_out.astype(BF16))

    query = contract(query_w, first_all, 1, 1).reshape(heads, HD, group)
    query = ((query + head_biases[:, 2][..., None]) * SCALE).astype(BF16)
    cross_query = layout.ring_exchange(query)
    cross_out, cross_low, cross_lse = flash_forward(sequence_prefix, cross_query, 0, cross_set, 0, 1, False)
    crossed = layout.ring_exchange(cross_low).reshape(heads * HD, group)
    second_sum = first_out + (reduce_tokens(contract(crossed, cross_w, 0, 0)) + cross_shift)
    second_out, second_normed, second_inverse = norm_forward(second_sum, gains[1], shifts[1])
    second_all = gather_tokens(second_out.astype(BF16))

    hidden_pre = contract(second_all, up_w, 1, 1) + up_bias
    hidden_act = (hidden_pre * normal_below(hidden_pre)).astype(BF16)
    third_sum = second_out + (reduce_tokens(contract(hidden_act, down_w, 1, 0)) + down_bias)
    third_out, third_normed, third_inverse = norm_forward(third_sum, gains[2], shifts[2])
    layer_out = third_out.astype(BF16)
    layer_out = layout.team_send(layout.pick(layout.member_blocks(layer_out)))
    layer_out = layout.unhalves(layout.place(layer_out, spots).reshape(group, -1))

    third_grad, third_gain, third_shift = norm_backward(upstream, third_normed, third_inverse, gains[2])
    down_own = third_grad.astype(BF16)
    down_all = gather_tokens(down_own)
    act_grad = contract(down_all, down_w, 1, 1)
    pre_low = (act_grad * gelu_slope(hidden_pre)).astype(BF16)
    second_grad = third_grad + reduce_tokens(contract(pre_low, up_w, 1, 0))
    down_sum = layout.over_columns(layout.out_of_order(contract(hidden_act, down_all, 0, 0)))
    up_sum = layout.over_columns(layout.out_of_order(contract(pre_low, second_all, 0, 0)))
    mid_grad, second_gain, second_shift = norm_backward(second_grad, second_normed, second_inverse, gains[1])
    cross_own = mid_grad.astype(BF16)
    cross_all = gather_tokens(cross_own)
    crossed_grad = contract(cross_w, cross_all, 1, 1).astype(BF16).reshape(heads, HD, group)
    crossed_grad = layout.ring_exchange(crossed_grad)
    crossproj_part = contract(crossed, cross_all, 1, 0).astype(BF16)
    crossed_grad, crossproj_part = lax.optimization_barrier((crossed_grad, crossproj_part))
    crossproj_sum = layout.over_columns(layout.out_of_order(crossproj_part))
    dquery, dkeys, dvalues = flash_backward(
        sequence_prefix, cross_query, 0, cross_set, 0, 1, crossed_grad, cross_out, cross_lse, False
    )
    cross_bias_sums = (jnp.sum(dquery.astype(F32), axis=(0, 2)), jnp.sum(dvalues.astype(F32), axis=(0, 2)))
    dquery = layout.ring_exchange(dquery).reshape(heads * HD, group)
    first_grad = mid_grad + reduce_tokens(contract(dquery, query_w, 0, 0))
    dpair = layout.ring_trickle(jnp.concatenate([dkeys, dvalues], axis=1)).reshape(heads * 2 * HD, group)
    crossquery_sum = layout.over_columns(layout.out_of_order(contract(dquery, first_all, 1, 0)))
    crosskv_sum = layout.over_columns(contract(dpair, encoder_all, 1, 0))
    encoder_grad = layout.team_total(layout.feature_parts(contract(dpair, kv_w, 0, 0)))
    encoder_grad = layout.unhalves(encoder_grad)
    low_grad, first_gain, first_shift = norm_backward(first_grad, first_normed, first_inverse, gains[0])
    self_own = low_grad.astype(BF16)
    self_all = layout.place(layout.team_parts(self_own), spots).reshape(group, width)
    attended_grad = contract(self_w, self_all, 1, 1).astype(BF16).reshape(heads, HD, group)
    attended_grad = layout.ring_exchange(attended_grad)
    selfproj_part = contract(attended, self_all, 1, 0).astype(BF16)
    sums = (up_sum, down_sum, crossproj_sum)
    attended_grad, selfproj_part, sums = lax.optimization_barrier((attended_grad, selfproj_part, sums))
    early_grads = layout.weight_grads([], list(sums))
    selfproj_sum = layout.over_columns(layout.out_of_order(selfproj_part))
    dq, dk, dv = flash_backward(
        sequence_prefix, self_set, 0, self_set, 1, 2, attended_grad, self_out, self_lse, True
    )
    dq, dk, dv, early_grads, selfproj_sum = lax.optimization_barrier((dq, dk, dv, early_grads, selfproj_sum))
    upweight_grad, downweight_grad, crossproj_grad = early_grads
    crosskv_grad, selfproj_grad, crossquery_grad = layout.weight_grads(
        [crosskv_sum], [selfproj_sum, crossquery_sum]
    )
    self_bias_sums = (jnp.sum(dq.astype(F32), axis=(0, 2)), jnp.sum(dv.astype(F32), axis=(0, 2)))
    dqkv = layout.ring_exchange(jnp.concatenate([dq, dk, dv], axis=1)).reshape(heads * 3 * HD, group)
    selfqkv_sum = layout.over_columns(contract(dqkv, tokens_all, 1, 0))
    (selfqkv_grad,) = layout.weight_grads([selfqkv_sum], [])
    tokens_part = contract(dqkv, qkv_w, 0, 0)
    low_parts = jnp.concatenate(layout.pick(layout.member_blocks(low_grad)), axis=1)
    mine = lax.dynamic_slice_in_dim(tokens_part, me * own_rows, own_rows, 0) + low_parts
    tokens_part = lax.dynamic_update_slice_in_dim(tokens_part, mine, me * own_rows, 0)
    tokens_grad = layout.unhalves(layout.team_total(layout.feature_parts(tokens_part)))

    def at_head(sums):
        spot = (layout.ring_index() * 4 + me) * HD
        return lax.dynamic_update_slice_in_dim(jnp.zeros((width,), F32), sums, spot, 0)

    up_sums = jnp.zeros((columns, 4, pre_low.shape[1] // columns), F32)
    up_sums = lax.dynamic_update_index_in_dim(
        up_sums, jnp.sum(pre_low.astype(F32), axis=0).reshape(columns, -1), me, 1
    )
    column_sum = lambda low: jnp.sum(low.astype(F32), axis=0)
    rows = jnp.stack([
        first_gain, second_gain, third_gain, first_shift, second_shift, third_shift,
        column_sum(self_own), column_sum(cross_own), column_sum(down_own),
        at_head(cross_bias_sums[0]), at_head(cross_bias_sums[1]),
    ])
    rows = layout.total(jnp.concatenate([rows, up_sums.reshape(-1, width)]))
    rows, up_sums = rows[:11], rows[11:].reshape(up_sums.shape)
    late = layout.total(jnp.stack([at_head(self_bias_sums[0]), at_head(self_bias_sums[1])]))
    row_at = (lax.axis_index("rb") * 4 + me) * normgain.shape[1]
    col_at = lax.axis_index(layout.cols)
    by_row = lax.dynamic_slice_in_dim(rows[:9], row_at, normgain.shape[1], 1)
    crossbias_grad = lax.dynamic_slice_in_dim(rows[9:], col_at * block, block, 1)
    selfbias_grad = lax.dynamic_slice_in_dim(late, col_at * block, block, 1)
    upbias_grad = lax.dynamic_index_in_dim(up_sums, col_at, 0, keepdims=False).reshape(-1)
    join_rows = lambda blocks: blocks.reshape(-1, blocks.shape[2])
    return (
        layer_out,
        tokens_grad,
        encoder_grad,
        column_rows_back(selfqkv_grad, 3),
        selfbias_grad,
        join_rows(selfproj_grad),
        by_row[6],
        column_rows_back(crossquery_grad, 1)[:, 0],
        column_rows_back(crosskv_grad, 2),
        crossbias_grad,
        join_rows(crossproj_grad),
        by_row[7],
        column_rows_back(upweight_grad, 1)[:, 0],
        upbias_grad,
        join_rows(downweight_grad),
        by_row[8],
        by_row[:3],
        by_row[3:6],
    )


def solution(mesh):
    def run(*arrays):
        dp, row, col = (mesh.shape[name] for name in ("dp", "row", "col"))
        per_col = arrays[4].shape[2] // HD // col
        seqs = arrays[3].shape[0] // dp
        assert per_col == 4 and row % 4 == 0 and col % seqs == 0
        assert (row // 4) * (col // seqs) == col
        sizes = {"dp": dp, "rb": row // 4, "rx": 2, "rc": 2, "sq": seqs, "cs": col // seqs}
        grid = Mesh(mesh.devices.reshape(tuple(sizes.values())), tuple(sizes))
        rows, cols, tokens = ("rb", "rx", "rc"), ("sq", "cs"), ("dp", "sq", "cs")
        specs = {
            "tokens": P(tokens, rows), "rc": P(rows, cols), "cr": P(cols, rows), "r3c": P(rows, None, cols),
            "c": P(cols), "r": P(rows), "2c": P(None, cols), "2r": P(None, rows),
        }
        ins = (
            "tokens", "tokens", "tokens", "dp", "r3c", "2c", "cr", "r", "rc", "r3c", "2c", "cr", "r", "rc", "c", "cr", "r", "2r", "2r",
        )
        outs = (
            "tokens", "tokens", "tokens", "r3c", "2c", "cr", "r", "rc", "r3c", "2c", "cr", "r", "rc", "c", "cr", "r", "2r", "2r",
        )
        specs["dp"] = P("dp")
        body = functools.partial(shards, Layout(sizes))
        return jax.shard_map(
            body, mesh=grid, in_specs=tuple(specs[s] for s in ins), out_specs=tuple(specs[s] for s in outs),
            check_vma=False,
        )(*arrays)

    return run
```

```python
import functools
import jax
import jax.numpy as jnp
from jax import lax
from jax.experimental import pallas as pl
from jax.experimental.pallas import tpu as pltpu
from jax.sharding import Mesh
from jax.sharding import PartitionSpec as P

HD = 64
NEGATIVE = -1e30
F32 = jnp.float32
BF16 = jnp.bfloat16


def dot_nn(a, b):
    return lax.dot_general(a, b, (((1,), (0,)), ((), ())), preferred_element_type=F32)


def allowed_mask(first_key, first_query, prefix, shape):
    key_pos = first_key + lax.broadcasted_iota(jnp.int32, shape, 0)
    query_pos = first_query + lax.broadcasted_iota(jnp.int32, shape, 1)
    return (key_pos < prefix) | (key_pos <= query_pos)


def forward_kernel(masked, bq, bk, prefix_ref, q_ref, k_ref, v_ref, o_ref, low_ref, lse_ref, keys, values, acc, peak):
    chunks, _, chunk = k_ref.shape
    per = chunk // bk
    blocks = chunks * per
    step = pl.program_id(0)
    prefix = prefix_ref[0]

    @pl.when(step == 0)
    def _():
        for c in range(chunks):
            for b in range(per):
                i = c * per + b
                keys[i] = k_ref[c, :, b * bk:(b + 1) * bk].T
                values[i, :HD, :] = v_ref[c, :, b * bk:(b + 1) * bk]
                rows = lax.broadcasted_iota(jnp.int32, (16, bk), 0)
                values[i, HD:, :] = jnp.where(rows == 0, 1.0, 0.0).astype(BF16)

    first_query = step * bq
    query = q_ref[0]
    peak[...] = jnp.full(peak.shape, NEGATIVE, F32)
    acc[...] = jnp.zeros(acc.shape, F32)

    def visit(i, use_mask):
        scores = dot_nn(keys[i], query)
        if use_mask:
            scores = jnp.where(allowed_mask(i * bk, first_query, prefix, scores.shape), scores, NEGATIVE)
        old = peak[...]
        new = jnp.maximum(old, jnp.max(scores, axis=0, keepdims=True))
        weight = jnp.exp(scores - new).astype(BF16)
        acc[...] = acc[...] * jnp.exp(old - new) + dot_nn(values[i], weight)
        peak[...] = new

    if masked:
        full = jnp.maximum(prefix, first_query + 1) // bk
        stop = (jnp.maximum(prefix, first_query + bq) + bk - 1) // bk
        lax.fori_loop(0, full, lambda i, c: (visit(i, False), c)[1], 0)
        lax.fori_loop(full, stop, lambda i, c: (visit(i, True), c)[1], 0)
    else:
        lax.fori_loop(0, blocks, lambda i, c: (visit(i, False), c)[1], 0)
    total = acc[HD:HD + 1, :]
    out = acc[:HD, :] / total
    o_ref[0] = out
    low_ref[0] = out.astype(BF16)
    lse_ref[0] = peak[...] + jnp.log(total)


def flash_forward(prefix, queries, q_part, pairs, k_part, v_part, masked, bq=1024, bk=1024):
    chunks, _, chunk = queries.shape
    length = chunks * chunk
    per = chunk // bq
    whole = lambda part: pl.BlockSpec((chunks, HD, chunk), lambda i, p: (0, part, 0))
    mine = lambda rows: pl.BlockSpec((1, rows, bq), lambda i, p: (i // per, 0, i % per))
    return pl.pallas_call(
        functools.partial(forward_kernel, masked, bq, bk),
        out_shape=(
            jax.ShapeDtypeStruct((chunks, HD, chunk), F32),
            jax.ShapeDtypeStruct((chunks, HD, chunk), BF16),
            jax.ShapeDtypeStruct((chunks, 1, chunk), F32),
        ),
        grid_spec=pltpu.PrefetchScalarGridSpec(
            num_scalar_prefetch=1,
            grid=(length // bq,),
            in_specs=[
                pl.BlockSpec((1, HD, bq), lambda i, p: (i // per, q_part, i % per)),
                whole(k_part),
                whole(v_part),
            ],
            out_specs=[mine(HD), mine(HD), mine(1)],
            scratch_shapes=[
                pltpu.VMEM((length // bk, bk, HD), BF16),
                pltpu.VMEM((length // bk, HD + 16, bk), BF16),
                pltpu.VMEM((HD + 16, bq), F32),
                pltpu.VMEM((1, bq), F32),
            ],
        ),
        cost_estimate=pl.CostEstimate(
            flops=4 * HD * length * length, transcendentals=length * length, bytes_accessed=14 * HD * length
        ),
        name="attend_self" if masked else "attend_cross",
    )(prefix, queries, pairs, pairs)


def backward_kernel(masked, bq, bk, prefix_ref, q_ref, g_ref, o_ref, lse_ref, k_ref, v_ref,
                    dq_ref, dk_ref, dv_ref, rows_q, rows_g, delta, dq_acc, dk_acc, dv_acc):
    chunks, _, chunk = q_ref.shape
    per = chunk // bq
    blocks = chunks * per
    step = pl.program_id(0)
    prefix = prefix_ref[0]

    @pl.when(step == 0)
    def _():
        for c in range(chunks):
            for b in range(per):
                i = c * per + b
                at = slice(b * bq, (b + 1) * bq)
                grad = g_ref[c, :, at]
                rows_q[i] = q_ref[c, :, at].T
                rows_g[i] = grad.T
                delta[i] = jnp.sum(grad.astype(F32) * o_ref[c, :, at], axis=0, keepdims=True)
        dq_acc[...] = jnp.zeros(dq_acc.shape, F32)

    first_key = step * bk
    key_cols = k_ref[0]
    key_rows = key_cols.T
    value_rows = v_ref[0].T
    dk_acc[...] = jnp.zeros(dk_acc.shape, F32)
    dv_acc[...] = jnp.zeros(dv_acc.shape, F32)

    def visit(i, use_mask):
        c, at = i // per, pl.ds(pl.multiple_of((i % per) * bq, bq), bq)
        scores = dot_nn(key_rows, q_ref[c, :, at])
        if use_mask:
            scores = jnp.where(allowed_mask(first_key, i * bq, prefix, scores.shape), scores, NEGATIVE)
        probs = jnp.exp(scores - lse_ref[c, :, at])
        dprobs = dot_nn(value_rows, g_ref[c, :, at])
        dscore = (probs * (dprobs - delta[i])).astype(BF16)
        dv_acc[...] += dot_nn(probs.astype(BF16), rows_g[i])
        dk_acc[...] += dot_nn(dscore, rows_q[i])
        dq_acc[i] += dot_nn(key_cols, dscore)

    if masked:
        inside = first_key + bk <= prefix
        start = jnp.where(first_key < prefix, 0, first_key // bq)
        free = jnp.where(inside, 0, jnp.minimum((first_key + bk - 1 + bq - 1) // bq, blocks))
        lax.fori_loop(start, free, lambda i, c: (visit(i, True), c)[1], 0)
        lax.fori_loop(jnp.maximum(start, free), blocks, lambda i, c: (visit(i, False), c)[1], 0)
    else:
        lax.fori_loop(0, blocks, lambda i, c: (visit(i, False), c)[1], 0)
    dk_ref[0] = dk_acc[...].T.astype(BF16)
    dv_ref[0] = dv_acc[...].T.astype(BF16)

    @pl.when(step == pl.num_programs(0) - 1)
    def _():
        for c in range(chunks):
            for b in range(per):
                low = dq_acc[c * per + b].astype(BF16)
                dq_ref[c, :, b * bq:(b + 1) * bq] = low * jnp.asarray(HD ** -0.5, BF16)


def flash_backward(prefix, queries, q_part, pairs, k_part, v_part, grads, outputs, lse, masked, bq=1024, bk=1024):
    chunks, _, chunk = queries.shape
    length = chunks * chunk
    per = chunk // bk
    whole = lambda part, rows=HD: pl.BlockSpec((chunks, rows, chunk), lambda i, p: (0, part, 0))
    mine = lambda part: pl.BlockSpec((1, HD, bk), lambda i, p: (i // per, part, i % per))
    shape = jax.ShapeDtypeStruct((chunks, HD, chunk), BF16)
    return pl.pallas_call(
        functools.partial(backward_kernel, masked, bq, bk),
        out_shape=(shape, shape, shape),
        grid_spec=pltpu.PrefetchScalarGridSpec(
            num_scalar_prefetch=1,
            grid=(length // bk,),
            in_specs=[whole(q_part), whole(0), whole(0), whole(0, 1), mine(k_part), mine(v_part)],
            out_specs=[whole(0), mine(0), mine(0)],
            scratch_shapes=[
                pltpu.VMEM((length // bq, bq, HD), BF16),
                pltpu.VMEM((length // bq, bq, HD), BF16),
                pltpu.VMEM((length // bq, 1, bq), F32),
                pltpu.VMEM((length // bq, HD, bq), F32),
                pltpu.VMEM((bk, HD), F32),
                pltpu.VMEM((bk, HD), F32),
            ],
        ),
        cost_estimate=pl.CostEstimate(
            flops=10 * HD * length * length, transcendentals=length * length, bytes_accessed=20 * HD * length
        ),
        name="attend_self_back" if masked else "attend_cross_back",
    )(prefix, queries, grads, outputs, lse, pairs, pairs)


EPSILON = 1e-05
SCALE = HD ** -0.5


def contract(left, right, left_dim, right_dim):
    return lax.dot_general(
        left, right, (((left_dim,), (right_dim,)), ((), ())), preferred_element_type=F32
    )


class Layout:
    def __init__(self, sizes):
        self.sizes = sizes
        keep = lambda names: tuple(n for n in names if sizes[n] > 1) or names[-1:]
        self.team = ("rx", "rc")
        self.cols = keep(("sq", "cs"))
        self.ring = keep(("rb", "cs"))
        self.every = ("dp", "rb", "rx", "rc", "sq", "cs")

    def count(self, names):
        total = 1
        for name in names:
            total *= self.sizes[name]
        return total

    def me(self):
        return lax.axis_index("rx") * 2 + lax.axis_index("rc")

    def swap(self, value, bits):
        if bits == 1:
            return lax.ppermute(value, "rc", [(0, 1), (1, 0)])
        if bits == 2:
            return lax.ppermute(value, "rx", [(0, 1), (1, 0)])
        return lax.ppermute(value, self.team, [(i, i ^ 3) for i in range(4)])

    def place(self, parts, spots):
        out = jnp.zeros((len(parts),) + parts[0].shape, parts[0].dtype)
        for part, spot in zip(parts, spots):
            out = lax.dynamic_update_index_in_dim(out, part, spot, 0)
        return lax.optimization_barrier(out)

    def spots(self):
        me = self.me()
        return [me, me ^ 1, me ^ 2, me ^ 3]

    def team_parts(self, value):
        core, across = self.swap(value, 1), self.swap(value, 2)
        return [value, core, across, self.swap(across, 1)]

    def pick(self, blocks):
        return [lax.dynamic_index_in_dim(blocks, spot, 0, keepdims=False) for spot in self.spots()]

    def team_send(self, parts):
        return [parts[0]] + [self.swap(parts[bits], bits) for bits in (1, 2, 3)]

    def team_total(self, parts):
        away = self.swap(jnp.stack([parts[1].astype(BF16), parts[3].astype(BF16)]), 1).astype(F32)
        away_across = self.swap((parts[2] + away[1]).astype(BF16), 2).astype(F32)
        return (parts[0] + away[0]) + away_across

    def total(self, value):
        for name in self.every:
            bits = 1
            while bits < self.sizes[name]:
                pairs = [(i, i ^ bits) for i in range(self.sizes[name])]
                value = value + lax.ppermute(value, name, pairs)
                bits *= 2
        return value

    def column_vectors(self, vector):
        size = self.count(self.cols)
        me = lax.axis_index(self.cols)
        parts, spots = [vector], [me]
        for step in range(1, size):
            pairs = [(i, (i + step) % size) for i in range(size)]
            parts.append(lax.ppermute(vector, self.cols, pairs))
            spots.append((me + size - step) % size)
        return self.place(parts, spots)

    def ring_index(self):
        return lax.axis_index("cs") * self.sizes["rb"] + lax.axis_index("rb")

    def flip(self, blocks, first, second):
        first, second = self.sizes[first], self.sizes[second]
        if first == 1 or second == 1:
            return blocks
        return blocks.reshape((first, second) + blocks.shape[1:]).swapaxes(0, 1).reshape(blocks.shape)

    def ring_exchange(self, blocks):
        blocks = lax.all_to_all(self.flip(blocks, "cs", "rb"), self.ring, 0, 0, tiled=True)
        return self.flip(blocks, "rb", "cs")

    def ring_trickle(self, blocks):
        size = self.count(self.ring)
        me = lax.axis_index(self.ring)
        blocks = self.flip(blocks, "cs", "rb")
        pick = lambda step: lax.dynamic_index_in_dim(blocks, (me + step) % size, 0, keepdims=False)
        parts, spots = [pick(0)], [me]
        for step in range(1, size):
            parts.append(lax.ppermute(pick(step), self.ring, [(i, (i + step) % size) for i in range(size)]))
            spots.append((me + size - step) % size)
        return self.flip(self.place(parts, spots), "rb", "cs")

    def block_sum(self, value):
        return lax.psum_scatter(value, self.cols, scatter_dimension=0, tiled=True)

    def halves(self, value):
        if self.sizes["rb"] == 1:
            return value
        return lax.all_to_all(value, "rb", 0, 1, tiled=True)

    def unhalves(self, value):
        if self.sizes["rb"] == 1:
            return value
        return lax.all_to_all(value, "rb", 1, 0, tiled=True)

    def feature_parts(self, value):
        width = value.shape[1] // 4
        return [value[:, i * width:(i + 1) * width] for i in range(4)]

    def team_features(self, blocks):
        rb, rows = self.sizes["rb"], blocks.shape[1]
        return blocks.reshape(4, rows, rb, -1).transpose(1, 2, 0, 3).reshape(rows, -1)

    def member_blocks(self, value):
        rb, rows = self.sizes["rb"], value.shape[0]
        return value.reshape(rows, rb, 4, -1).transpose(2, 0, 1, 3).reshape(4, rows, -1)

    def widen(self, piece):
        if self.sizes["rb"] > 1:
            piece = lax.all_gather(piece, "rb", axis=2, tiled=True)
        piece = piece.reshape(piece.shape[0], -1)
        return lax.all_gather(piece[None], self.cols, axis=0, tiled=True)

    def in_order(self, weight):
        rb = self.sizes["rb"]
        if rb == 1:
            return weight
        parts = weight.reshape(weight.shape[:-1] + (4, rb, -1))
        return jnp.swapaxes(parts, -3, -2).reshape(weight.shape)

    def out_of_order(self, weight):
        rb = self.sizes["rb"]
        if rb == 1:
            return weight
        parts = weight.reshape(weight.shape[:-1] + (rb, 4, -1))
        return jnp.swapaxes(parts, -3, -2).reshape(weight.shape)

    def over_columns(self, partial):
        total = lax.psum_scatter(partial.astype(BF16), self.cols, scatter_dimension=0, tiled=True)
        total = total.reshape(total.shape[0], 4, -1)
        if self.sizes["rb"] > 1:
            total = lax.psum_scatter(total, "rb", scatter_dimension=2, tiled=True)
        return total

    def weight_grads(self, relative, absolute):
        flat = [[piece[:, i] for i in range(4)] for piece in relative]
        flat += [self.pick(piece.transpose(1, 0, 2)) for piece in absolute]
        sizes = [piece[0].shape[0] for piece in flat]
        parts = self.team_send([jnp.concatenate([piece[i] for piece in flat]) for i in range(4)])
        low = jnp.stack(parts)
        if self.sizes["dp"] == 2:
            low = low.astype(F32) + lax.ppermute(low, "dp", [(0, 1), (1, 0)]).astype(F32)
        else:
            low = lax.psum(low.astype(F32), "dp")
        parts = [low[i] for i in range(4)]
        low = self.place(parts, self.spots())
        out, at = [], 0
        for size in sizes:
            out.append(low[:, at:at + size])
            at += size
        return out


def norm_forward(hidden, gain_row, shift_row):
    average = jnp.mean(hidden, axis=1, keepdims=True)
    square = jnp.mean(hidden * hidden, axis=1, keepdims=True)
    inverse = lax.rsqrt(square - average * average + EPSILON)
    normed = (hidden - average) * inverse
    return normed * gain_row + shift_row, normed, inverse


def norm_backward(upstream, normed, inverse, gain_row):
    scaled = upstream * gain_row
    first = jnp.mean(scaled, axis=1, keepdims=True)
    second = jnp.mean(scaled * normed, axis=1, keepdims=True)
    grad = inverse * (scaled - first - normed * second)
    return grad, jnp.sum(upstream * normed, axis=0), jnp.sum(upstream, axis=0)


def normal_below(inputs):
    return 0.5 * (1.0 + lax.erf(inputs * 0.5 ** 0.5))


def gelu_slope(inputs):
    return normal_below(inputs) + inputs * jnp.exp(-0.5 * inputs * inputs) * (2.0 * jnp.pi) ** -0.5


def column_rows(weight):
    features, parts, width = weight.shape
    blocks = weight.reshape(features, parts, 4, width // 4).transpose(2, 1, 3, 0)
    return blocks.reshape(4, -1, features)


def column_rows_back(blocks, parts):
    features = blocks.shape[2]
    return blocks.reshape(4, parts, -1, features).transpose(3, 1, 0, 2).reshape(features, parts, -1)


def shards(
    layout, tokens, encoder, cotangent, prefixes, selfqkv, selfbias, selfproj, selfshift, crossquery,
    crosskv, crossbias, crossproj, crossshift, upweight, upbias, downweight, downbias, normgain, normshift,
):
    me = layout.me()
    split_rows = lambda weight: weight.reshape(4, -1, weight.shape[1])

    def by_token(rows):
        return layout.halves(rows)

    def gather_weights(relative, absolute, widen=None):
        pieces = relative + absolute
        sizes = [piece.shape[1] for piece in pieces]
        parts = layout.team_send(layout.pick(jnp.concatenate(pieces, axis=1)))
        at = sum(piece.shape[1] for piece in relative)
        groups = []
        if relative:
            groups.append(jnp.stack([part[:at] for part in parts], axis=1))
        if absolute:
            groups.append(layout.place([part[at:] for part in parts], layout.spots()).transpose(1, 0, 2))
        piece = jnp.concatenate(groups)
        wide = layout.widen(piece) if widen is None else widen(piece)
        out, at = [], 0
        for index, size in enumerate(sizes):
            weight = wide[:, at:at + size].reshape(-1, wide.shape[2])
            out.append(weight if index < len(relative) else layout.in_order(weight))
            at += size
        return out

    (qkv_w,) = gather_weights([column_rows(selfqkv)], [])
    token_parts = layout.team_parts(by_token(tokens))
    tokens_all = jnp.concatenate(token_parts, axis=1)
    width = tokens_all.shape[1]
    group = tokens_all.shape[0]
    own_rows = group // 4
    columns = layout.count(layout.cols)
    heads = columns

    by_col = jnp.concatenate([selfbias.reshape(-1), crossbias.reshape(-1), upbias])
    by_col = layout.column_vectors(by_col)
    block = selfbias.shape[1]
    head_biases = lax.dynamic_index_in_dim(
        by_col[:, : 4 * block].reshape(columns, 4, 4, HD), me, 2, keepdims=False
    )
    up_bias = lax.dynamic_index_in_dim(
        by_col[:, 4 * block:].reshape(columns, 4, -1), me, 1, keepdims=False
    ).reshape(1, -1)
    by_row = jnp.concatenate([selfshift[None], crossshift[None], downbias[None], normgain, normshift])
    if layout.sizes["rb"] > 1:
        by_row = lax.all_gather(by_row, "rb", axis=1, tiled=True)
    by_row = layout.team_features(layout.place(layout.team_parts(by_row), layout.spots()))
    self_shift, cross_shift, down_bias = by_row[0], by_row[1], by_row[2]
    gains, shifts = by_row[3:6], by_row[6:9]

    def gather_tokens(own):
        return jnp.concatenate(layout.team_parts(own))

    def reduce_tokens(partial):
        return layout.team_total([partial[i * own_rows:(i + 1) * own_rows] for i in range(4)])

    sequence_prefix = prefixes
    if layout.sizes["sq"] > 1:
        sequence_prefix = lax.dynamic_slice_in_dim(prefixes, lax.axis_index("sq"), 1, 0)

    kv_w, self_w, query_w, cross_w = gather_weights(
        [column_rows(crosskv)],
        [split_rows(selfproj), column_rows(crossquery[:, None]), split_rows(crossproj)],
    )
    encoder_all = jnp.concatenate(layout.team_parts(by_token(encoder)), axis=1)
    pair = contract(kv_w, encoder_all, 1, 1).reshape(heads, 2, HD, group)
    pair_bias = jnp.stack([jnp.zeros_like(head_biases[:, 3]), head_biases[:, 3]], axis=1)
    pair = (pair + pair_bias[..., None]).astype(BF16).reshape(heads, 2 * HD, group)

    qkv = contract(qkv_w, tokens_all, 1, 1).reshape(heads, 3, HD, group)
    qkv_bias = jnp.stack([head_biases[:, 0], jnp.zeros_like(head_biases[:, 0]), head_biases[:, 1]], axis=1)
    factor = jnp.array([SCALE, 1.0, 1.0], F32)[None, :, None, None]
    qkv = ((qkv + qkv_bias[..., None]) * factor).astype(BF16).reshape(heads, 3 * HD, group)
    self_set = layout.ring_exchange(qkv)
    self_out, self_low, self_lse = flash_forward(sequence_prefix, self_set, 0, self_set, 1, 2, True)
    self_low, pair = lax.optimization_barrier((self_low, pair))
    cross_set = layout.ring_trickle(pair)
    attended = layout.ring_exchange(self_low).reshape(heads * HD, group)

    def widen_after(piece):
        piece = lax.optimization_barrier((attended, cross_set, piece))[2]
        return layout.widen(piece)

    spots = layout.spots()
    up_w, down_w = gather_weights([], [column_rows(upweight[:, None]), split_rows(downweight)], widen_after)

    upstream = layout.team_send(layout.pick(by_token(cotangent).reshape(4, own_rows, -1)))
    upstream = layout.team_features(layout.place(upstream, spots)).astype(F32)

    own_tokens = lax.dynamic_slice_in_dim(tokens_all, me * own_rows, own_rows, 0)
    own_tokens = layout.place(layout.feature_parts(own_tokens), spots)
    own_tokens = layout.team_features(own_tokens).astype(F32)
    self_partial = contract(attended, self_w, 0, 0).reshape(4, own_rows, width)
    first_sum = own_tokens + (layout.team_total(layout.pick(self_partial)) + self_shift)
    first_out, first_normed, first_inverse = norm_forward(first_sum, gains[0], shifts[0])
    first_all = gather_tokens(first_out.astype(BF16))

    query = contract(query_w, first_all, 1, 1).reshape(heads, HD, group)
    query = ((query + head_biases[:, 2][..., None]) * SCALE).astype(BF16)
    cross_query = layout.ring_exchange(query)
    cross_out, cross_low, cross_lse = flash_forward(sequence_prefix, cross_query, 0, cross_set, 0, 1, False)
    crossed = layout.ring_exchange(cross_low).reshape(heads * HD, group)
    second_sum = first_out + (reduce_tokens(contract(crossed, cross_w, 0, 0)) + cross_shift)
    second_out, second_normed, second_inverse = norm_forward(second_sum, gains[1], shifts[1])
    second_all = gather_tokens(second_out.astype(BF16))

    hidden_pre = contract(second_all, up_w, 1, 1) + up_bias
    hidden_act = (hidden_pre * normal_below(hidden_pre)).astype(BF16)
    third_sum = second_out + (reduce_tokens(contract(hidden_act, down_w, 1, 0)) + down_bias)
    third_out, third_normed, third_inverse = norm_forward(third_sum, gains[2], shifts[2])
    layer_out = third_out.astype(BF16)
    layer_out = layout.team_send(layout.pick(layout.member_blocks(layer_out)))
    layer_out = layout.unhalves(layout.place(layer_out, spots).reshape(group, -1))

    third_grad, third_gain, third_shift = norm_backward(upstream, third_normed, third_inverse, gains[2])
    down_own = third_grad.astype(BF16)
    down_all = gather_tokens(down_own)
    act_grad = contract(down_all, down_w, 1, 1)
    pre_low = (act_grad * gelu_slope(hidden_pre)).astype(BF16)
    second_grad = third_grad + reduce_tokens(contract(pre_low, up_w, 1, 0))
    down_sum = layout.over_columns(layout.out_of_order(contract(hidden_act, down_all, 0, 0)))
    up_sum = layout.over_columns(layout.out_of_order(contract(pre_low, second_all, 0, 0)))
    mid_grad, second_gain, second_shift = norm_backward(second_grad, second_normed, second_inverse, gains[1])
    cross_own = mid_grad.astype(BF16)
    cross_all = gather_tokens(cross_own)
    crossed_grad = contract(cross_w, cross_all, 1, 1).astype(BF16).reshape(heads, HD, group)
    crossed_grad = layout.ring_exchange(crossed_grad)
    crossproj_part = contract(crossed, cross_all, 1, 0).astype(BF16)
    crossed_grad, crossproj_part = lax.optimization_barrier((crossed_grad, crossproj_part))
    crossproj_sum = layout.over_columns(layout.out_of_order(crossproj_part))
    dquery, dkeys, dvalues = flash_backward(
        sequence_prefix, cross_query, 0, cross_set, 0, 1, crossed_grad, cross_out, cross_lse, False
    )
    cross_bias_sums = (jnp.sum(dquery.astype(F32), axis=(0, 2)), jnp.sum(dvalues.astype(F32), axis=(0, 2)))
    dquery = layout.ring_exchange(dquery).reshape(heads * HD, group)
    first_grad = mid_grad + reduce_tokens(contract(dquery, query_w, 0, 0))
    dpair = layout.ring_trickle(jnp.concatenate([dkeys, dvalues], axis=1)).reshape(heads * 2 * HD, group)
    crossquery_sum = layout.over_columns(layout.out_of_order(contract(dquery, first_all, 1, 0)))
    crosskv_sum = layout.over_columns(contract(dpair, encoder_all, 1, 0))
    encoder_grad = layout.team_total(layout.feature_parts(contract(dpair, kv_w, 0, 0)))
    encoder_grad = layout.unhalves(encoder_grad)
    low_grad, first_gain, first_shift = norm_backward(first_grad, first_normed, first_inverse, gains[0])
    self_own = low_grad.astype(BF16)
    self_all = layout.place(layout.team_parts(self_own), spots).reshape(group, width)
    attended_grad = contract(self_w, self_all, 1, 1).astype(BF16).reshape(heads, HD, group)
    attended_grad = layout.ring_exchange(attended_grad)
    selfproj_part = contract(attended, self_all, 1, 0).astype(BF16)
    sums = (up_sum, down_sum, crossproj_sum)
    attended_grad, selfproj_part, sums = lax.optimization_barrier((attended_grad, selfproj_part, sums))
    early_grads = layout.weight_grads([], list(sums))
    selfproj_sum = layout.over_columns(layout.out_of_order(selfproj_part))
    dq, dk, dv = flash_backward(
        sequence_prefix, self_set, 0, self_set, 1, 2, attended_grad, self_out, self_lse, True
    )
    dq, dk, dv, early_grads, selfproj_sum = lax.optimization_barrier((dq, dk, dv, early_grads, selfproj_sum))
    upweight_grad, downweight_grad, crossproj_grad = early_grads
    crosskv_grad, selfproj_grad, crossquery_grad = layout.weight_grads(
        [crosskv_sum], [selfproj_sum, crossquery_sum]
    )
    self_bias_sums = (jnp.sum(dq.astype(F32), axis=(0, 2)), jnp.sum(dv.astype(F32), axis=(0, 2)))
    dqkv = layout.ring_exchange(jnp.concatenate([dq, dk, dv], axis=1)).reshape(heads * 3 * HD, group)
    selfqkv_sum = layout.over_columns(contract(dqkv, tokens_all, 1, 0))
    (selfqkv_grad,) = layout.weight_grads([selfqkv_sum], [])
    tokens_part = contract(dqkv, qkv_w, 0, 0)
    low_parts = jnp.concatenate(layout.pick(layout.member_blocks(low_grad)), axis=1)
    mine = lax.dynamic_slice_in_dim(tokens_part, me * own_rows, own_rows, 0) + low_parts
    tokens_part = lax.dynamic_update_slice_in_dim(tokens_part, mine, me * own_rows, 0)
    tokens_grad = layout.unhalves(layout.team_total(layout.feature_parts(tokens_part)))

    def at_head(sums):
        spot = (layout.ring_index() * 4 + me) * HD
        return lax.dynamic_update_slice_in_dim(jnp.zeros((width,), F32), sums, spot, 0)

    up_sums = jnp.zeros((columns, 4, pre_low.shape[1] // columns), F32)
    up_sums = lax.dynamic_update_index_in_dim(
        up_sums, jnp.sum(pre_low.astype(F32), axis=0).reshape(columns, -1), me, 1
    )
    column_sum = lambda low: jnp.sum(low.astype(F32), axis=0)
    rows = jnp.stack([
        first_gain, second_gain, third_gain, first_shift, second_shift, third_shift,
        column_sum(self_own), column_sum(cross_own), column_sum(down_own),
        at_head(cross_bias_sums[0]), at_head(cross_bias_sums[1]),
    ])
    rows = layout.total(jnp.concatenate([rows, up_sums.reshape(-1, width)]))
    rows, up_sums = rows[:11], rows[11:].reshape(up_sums.shape)
    late = layout.total(jnp.stack([at_head(self_bias_sums[0]), at_head(self_bias_sums[1])]))
    row_at = (lax.axis_index("rb") * 4 + me) * normgain.shape[1]
    col_at = lax.axis_index(layout.cols)
    by_row = lax.dynamic_slice_in_dim(rows[:9], row_at, normgain.shape[1], 1)
    crossbias_grad = lax.dynamic_slice_in_dim(rows[9:], col_at * block, block, 1)
    selfbias_grad = lax.dynamic_slice_in_dim(late, col_at * block, block, 1)
    upbias_grad = lax.dynamic_index_in_dim(up_sums, col_at, 0, keepdims=False).reshape(-1)
    join_rows = lambda blocks: blocks.reshape(-1, blocks.shape[2])
    return (
        layer_out,
        tokens_grad,
        encoder_grad,
        column_rows_back(selfqkv_grad, 3),
        selfbias_grad,
        join_rows(selfproj_grad),
        by_row[6],
        column_rows_back(crossquery_grad, 1)[:, 0],
        column_rows_back(crosskv_grad, 2),
        crossbias_grad,
        join_rows(crossproj_grad),
        by_row[7],
        column_rows_back(upweight_grad, 1)[:, 0],
        upbias_grad,
        join_rows(downweight_grad),
        by_row[8],
        by_row[:3],
        by_row[3:6],
    )


def solution(mesh):
    def run(*arrays):
        dp, row, col = (mesh.shape[name] for name in ("dp", "row", "col"))
        per_col = arrays[4].shape[2] // HD // col
        seqs = arrays[3].shape[0] // dp
        assert per_col == 4 and row % 4 == 0 and col % seqs == 0
        assert (row // 4) * (col // seqs) == col
        sizes = {"dp": dp, "rb": row // 4, "rx": 2, "rc": 2, "sq": seqs, "cs": col // seqs}
        grid = Mesh(mesh.devices.reshape(tuple(sizes.values())), tuple(sizes))
        rows, cols, tokens = ("rb", "rx", "rc"), ("sq", "cs"), ("dp", "sq", "cs")
        specs = {
            "tokens": P(tokens, rows), "rc": P(rows, cols), "cr": P(cols, rows), "r3c": P(rows, None, cols),
            "c": P(cols), "r": P(rows), "2c": P(None, cols), "2r": P(None, rows),
        }
        ins = (
            "tokens", "tokens", "tokens", "dp", "r3c", "2c", "cr", "r", "rc", "r3c", "2c", "cr", "r", "rc", "c", "cr", "r", "2r", "2r",
        )
        outs = (
            "tokens", "tokens", "tokens", "r3c", "2c", "cr", "r", "rc", "r3c", "2c", "cr", "r", "rc", "c", "cr", "r", "2r", "2r",
        )
        specs["dp"] = P("dp")
        body = functools.partial(shards, Layout(sizes))
        return jax.shard_map(
            body, mesh=grid, in_specs=tuple(specs[s] for s in ins), out_specs=tuple(specs[s] for s in outs),
            check_vma=False,
        )(*arrays)

    return run
```

```python
import functools
import jax
import jax.numpy as jnp
from jax import lax
from jax.experimental import pallas as pl
from jax.experimental.pallas import tpu as pltpu
from jax.sharding import Mesh
from jax.sharding import PartitionSpec as P

HD = 64
NEGATIVE = -1e30
F32 = jnp.float32
BF16 = jnp.bfloat16


def dot_nn(a, b):
    return lax.dot_general(a, b, (((1,), (0,)), ((), ())), preferred_element_type=F32)


def allowed_mask(first_key, first_query, prefix, shape):
    key_pos = first_key + lax.broadcasted_iota(jnp.int32, shape, 0)
    query_pos = first_query + lax.broadcasted_iota(jnp.int32, shape, 1)
    return (key_pos < prefix) | (key_pos <= query_pos)


def forward_kernel(masked, bq, bk, prefix_ref, q_ref, k_ref, v_ref, o_ref, low_ref, lse_ref, keys, values, acc, peak):
    chunks, _, chunk = k_ref.shape
    per = chunk // bk
    blocks = chunks * per
    step = pl.program_id(0)
    prefix = prefix_ref[0]

    @pl.when(step == 0)
    def _():
        for c in range(chunks):
            for b in range(per):
                i = c * per + b
                keys[i] = k_ref[c, :, b * bk:(b + 1) * bk].T
                values[i, :HD, :] = v_ref[c, :, b * bk:(b + 1) * bk]
                rows = lax.broadcasted_iota(jnp.int32, (16, bk), 0)
                values[i, HD:, :] = jnp.where(rows == 0, 1.0, 0.0).astype(BF16)

    first_query = step * bq
    query = q_ref[0]
    peak[...] = jnp.full(peak.shape, NEGATIVE, F32)
    acc[...] = jnp.zeros(acc.shape, F32)

    def visit(i, use_mask):
        scores = dot_nn(keys[i], query)
        if use_mask:
            scores = jnp.where(allowed_mask(i * bk, first_query, prefix, scores.shape), scores, NEGATIVE)
        old = peak[...]
        new = jnp.maximum(old, jnp.max(scores, axis=0, keepdims=True))
        weight = jnp.exp(scores - new).astype(BF16)
        acc[...] = acc[...] * jnp.exp(old - new) + dot_nn(values[i], weight)
        peak[...] = new

    if masked:
        full = jnp.maximum(prefix, first_query + 1) // bk
        stop = (jnp.maximum(prefix, first_query + bq) + bk - 1) // bk
        lax.fori_loop(0, full, lambda i, c: (visit(i, False), c)[1], 0)
        lax.fori_loop(full, stop, lambda i, c: (visit(i, True), c)[1], 0)
    else:
        lax.fori_loop(0, blocks, lambda i, c: (visit(i, False), c)[1], 0)
    total = acc[HD:HD + 1, :]
    out = acc[:HD, :] / total
    o_ref[0] = out
    low_ref[0] = out.astype(BF16)
    lse_ref[0] = peak[...] + jnp.log(total)


def flash_forward(prefix, queries, q_part, pairs, k_part, v_part, masked, bq=1024, bk=1024):
    chunks, _, chunk = queries.shape
    length = chunks * chunk
    per = chunk // bq
    whole = lambda part: pl.BlockSpec((chunks, HD, chunk), lambda i, p: (0, part, 0))
    mine = lambda rows: pl.BlockSpec((1, rows, bq), lambda i, p: (i // per, 0, i % per))
    return pl.pallas_call(
        functools.partial(forward_kernel, masked, bq, bk),
        out_shape=(
            jax.ShapeDtypeStruct((chunks, HD, chunk), F32),
            jax.ShapeDtypeStruct((chunks, HD, chunk), BF16),
            jax.ShapeDtypeStruct((chunks, 1, chunk), F32),
        ),
        grid_spec=pltpu.PrefetchScalarGridSpec(
            num_scalar_prefetch=1,
            grid=(length // bq,),
            in_specs=[
                pl.BlockSpec((1, HD, bq), lambda i, p: (i // per, q_part, i % per)),
                whole(k_part),
                whole(v_part),
            ],
            out_specs=[mine(HD), mine(HD), mine(1)],
            scratch_shapes=[
                pltpu.VMEM((length // bk, bk, HD), BF16),
                pltpu.VMEM((length // bk, HD + 16, bk), BF16),
                pltpu.VMEM((HD + 16, bq), F32),
                pltpu.VMEM((1, bq), F32),
            ],
        ),
        cost_estimate=pl.CostEstimate(
            flops=4 * HD * length * length, transcendentals=length * length, bytes_accessed=14 * HD * length
        ),
        name="attend_self" if masked else "attend_cross",
    )(prefix, queries, pairs, pairs)


def backward_kernel(masked, bq, bk, prefix_ref, q_ref, g_ref, o_ref, lse_ref, k_ref, v_ref,
                    dq_ref, dk_ref, dv_ref, rows_q, rows_g, delta, dq_acc, dk_acc, dv_acc):
    chunks, _, chunk = q_ref.shape
    per = chunk // bq
    blocks = chunks * per
    step = pl.program_id(0)
    prefix = prefix_ref[0]

    @pl.when(step == 0)
    def _():
        for c in range(chunks):
            for b in range(per):
                i = c * per + b
                at = slice(b * bq, (b + 1) * bq)
                grad = g_ref[c, :, at]
                rows_q[i] = q_ref[c, :, at].T
                rows_g[i] = grad.T
                delta[i] = jnp.sum(grad.astype(F32) * o_ref[c, :, at], axis=0, keepdims=True)
        dq_acc[...] = jnp.zeros(dq_acc.shape, F32)

    first_key = step * bk
    key_cols = k_ref[0]
    key_rows = key_cols.T
    value_rows = v_ref[0].T
    dk_acc[...] = jnp.zeros(dk_acc.shape, F32)
    dv_acc[...] = jnp.zeros(dv_acc.shape, F32)

    def visit(i, use_mask):
        c, at = i // per, pl.ds(pl.multiple_of((i % per) * bq, bq), bq)
        scores = dot_nn(key_rows, q_ref[c, :, at])
        if use_mask:
            scores = jnp.where(allowed_mask(first_key, i * bq, prefix, scores.shape), scores, NEGATIVE)
        probs = jnp.exp(scores - lse_ref[c, :, at])
        dprobs = dot_nn(value_rows, g_ref[c, :, at])
        dscore = (probs * (dprobs - delta[i])).astype(BF16)
        dv_acc[...] += dot_nn(probs.astype(BF16), rows_g[i])
        dk_acc[...] += dot_nn(dscore, rows_q[i])
        dq_acc[i] += dot_nn(key_cols, dscore)

    if masked:
        inside = first_key + bk <= prefix
        start = jnp.where(first_key < prefix, 0, first_key // bq)
        free = jnp.where(inside, 0, jnp.minimum((first_key + bk - 1 + bq - 1) // bq, blocks))
        lax.fori_loop(start, free, lambda i, c: (visit(i, True), c)[1], 0)
        lax.fori_loop(jnp.maximum(start, free), blocks, lambda i, c: (visit(i, False), c)[1], 0)
    else:
        lax.fori_loop(0, blocks, lambda i, c: (visit(i, False), c)[1], 0)
    dk_ref[0] = dk_acc[...].T.astype(BF16)
    dv_ref[0] = dv_acc[...].T.astype(BF16)

    @pl.when(step == pl.num_programs(0) - 1)
    def _():
        for c in range(chunks):
            for b in range(per):
                low = dq_acc[c * per + b].astype(BF16)
                dq_ref[c, :, b * bq:(b + 1) * bq] = low * jnp.asarray(HD ** -0.5, BF16)


def flash_backward(prefix, queries, q_part, pairs, k_part, v_part, grads, outputs, lse, masked, bq=1024, bk=1024):
    chunks, _, chunk = queries.shape
    length = chunks * chunk
    per = chunk // bk
    whole = lambda part, rows=HD: pl.BlockSpec((chunks, rows, chunk), lambda i, p: (0, part, 0))
    mine = lambda part: pl.BlockSpec((1, HD, bk), lambda i, p: (i // per, part, i % per))
    shape = jax.ShapeDtypeStruct((chunks, HD, chunk), BF16)
    return pl.pallas_call(
        functools.partial(backward_kernel, masked, bq, bk),
        out_shape=(shape, shape, shape),
        grid_spec=pltpu.PrefetchScalarGridSpec(
            num_scalar_prefetch=1,
            grid=(length // bk,),
            in_specs=[whole(q_part), whole(0), whole(0), whole(0, 1), mine(k_part), mine(v_part)],
            out_specs=[whole(0), mine(0), mine(0)],
            scratch_shapes=[
                pltpu.VMEM((length // bq, bq, HD), BF16),
                pltpu.VMEM((length // bq, bq, HD), BF16),
                pltpu.VMEM((length // bq, 1, bq), F32),
                pltpu.VMEM((length // bq, HD, bq), F32),
                pltpu.VMEM((bk, HD), F32),
                pltpu.VMEM((bk, HD), F32),
            ],
        ),
        cost_estimate=pl.CostEstimate(
            flops=10 * HD * length * length, transcendentals=length * length, bytes_accessed=20 * HD * length
        ),
        name="attend_self_back" if masked else "attend_cross_back",
    )(prefix, queries, grads, outputs, lse, pairs, pairs)


EPSILON = 1e-05
SCALE = HD ** -0.5


def contract(left, right, left_dim, right_dim):
    return lax.dot_general(
        left, right, (((left_dim,), (right_dim,)), ((), ())), preferred_element_type=F32
    )


class Layout:
    def __init__(self, sizes):
        self.sizes = sizes
        keep = lambda names: tuple(n for n in names if sizes[n] > 1) or names[-1:]
        self.team = ("rx", "rc")
        self.cols = keep(("sq", "cs"))
        self.ring = keep(("rb", "cs"))
        self.every = ("dp", "rb", "rx", "rc", "sq", "cs")

    def count(self, names):
        total = 1
        for name in names:
            total *= self.sizes[name]
        return total

    def me(self):
        return lax.axis_index("rx") * 2 + lax.axis_index("rc")

    def swap(self, value, bits):
        if bits == 1:
            return lax.ppermute(value, "rc", [(0, 1), (1, 0)])
        if bits == 2:
            return lax.ppermute(value, "rx", [(0, 1), (1, 0)])
        return lax.ppermute(value, self.team, [(i, i ^ 3) for i in range(4)])

    def place(self, parts, spots):
        out = jnp.zeros((len(parts),) + parts[0].shape, parts[0].dtype)
        for part, spot in zip(parts, spots):
            out = lax.dynamic_update_index_in_dim(out, part, spot, 0)
        return lax.optimization_barrier(out)

    def spots(self):
        me = self.me()
        return [me, me ^ 1, me ^ 2, me ^ 3]

    def team_parts(self, value):
        core, across = self.swap(value, 1), self.swap(value, 2)
        return [value, core, across, self.swap(across, 1)]

    def pick(self, blocks):
        return [lax.dynamic_index_in_dim(blocks, spot, 0, keepdims=False) for spot in self.spots()]

    def team_send(self, parts):
        return [parts[0]] + [self.swap(parts[bits], bits) for bits in (1, 2, 3)]

    def team_total(self, parts):
        away = self.swap(jnp.stack([parts[1].astype(BF16), parts[3].astype(BF16)]), 1).astype(F32)
        away_across = self.swap((parts[2] + away[1]).astype(BF16), 2).astype(F32)
        return (parts[0] + away[0]) + away_across

    def total(self, value):
        for name in self.every:
            bits = 1
            while bits < self.sizes[name]:
                pairs = [(i, i ^ bits) for i in range(self.sizes[name])]
                value = value + lax.ppermute(value, name, pairs)
                bits *= 2
        return value

    def column_vectors(self, vector):
        size = self.count(self.cols)
        me = lax.axis_index(self.cols)
        parts, spots = [vector], [me]
        for step in range(1, size):
            pairs = [(i, (i + step) % size) for i in range(size)]
            parts.append(lax.ppermute(vector, self.cols, pairs))
            spots.append((me + size - step) % size)
        return self.place(parts, spots)

    def ring_index(self):
        return lax.axis_index("cs") * self.sizes["rb"] + lax.axis_index("rb")

    def flip(self, blocks, first, second):
        first, second = self.sizes[first], self.sizes[second]
        if first == 1 or second == 1:
            return blocks
        return blocks.reshape((first, second) + blocks.shape[1:]).swapaxes(0, 1).reshape(blocks.shape)

    def ring_exchange(self, blocks):
        blocks = lax.all_to_all(self.flip(blocks, "cs", "rb"), self.ring, 0, 0, tiled=True)
        return self.flip(blocks, "rb", "cs")

    def ring_trickle(self, blocks):
        size = self.count(self.ring)
        me = lax.axis_index(self.ring)
        blocks = self.flip(blocks, "cs", "rb")
        pick = lambda step: lax.dynamic_index_in_dim(blocks, (me + step) % size, 0, keepdims=False)
        parts, spots = [pick(0)], [me]
        for step in range(1, size):
            parts.append(lax.ppermute(pick(step), self.ring, [(i, (i + step) % size) for i in range(size)]))
            spots.append((me + size - step) % size)
        return self.flip(self.place(parts, spots), "rb", "cs")

    def block_sum(self, value):
        return lax.psum_scatter(value, self.cols, scatter_dimension=0, tiled=True)

    def halves(self, value):
        if self.sizes["rb"] == 1:
            return value
        return lax.all_to_all(value, "rb", 0, 1, tiled=True)

    def unhalves(self, value):
        if self.sizes["rb"] == 1:
            return value
        return lax.all_to_all(value, "rb", 1, 0, tiled=True)

    def feature_parts(self, value):
        width = value.shape[1] // 4
        return [value[:, i * width:(i + 1) * width] for i in range(4)]

    def team_features(self, blocks):
        rb, rows = self.sizes["rb"], blocks.shape[1]
        return blocks.reshape(4, rows, rb, -1).transpose(1, 2, 0, 3).reshape(rows, -1)

    def member_blocks(self, value):
        rb, rows = self.sizes["rb"], value.shape[0]
        return value.reshape(rows, rb, 4, -1).transpose(2, 0, 1, 3).reshape(4, rows, -1)

    def widen(self, piece):
        if self.sizes["rb"] > 1:
            piece = lax.all_gather(piece, "rb", axis=2, tiled=True)
        piece = piece.reshape(piece.shape[0], -1)
        return lax.all_gather(piece[None], self.cols, axis=0, tiled=True)

    def in_order(self, weight):
        rb = self.sizes["rb"]
        if rb == 1:
            return weight
        parts = weight.reshape(weight.shape[:-1] + (4, rb, -1))
        return jnp.swapaxes(parts, -3, -2).reshape(weight.shape)

    def out_of_order(self, weight):
        rb = self.sizes["rb"]
        if rb == 1:
            return weight
        parts = weight.reshape(weight.shape[:-1] + (rb, 4, -1))
        return jnp.swapaxes(parts, -3, -2).reshape(weight.shape)

    def over_columns(self, partial):
        total = lax.psum_scatter(partial.astype(BF16), self.cols, scatter_dimension=0, tiled=True)
        total = total.reshape(total.shape[0], 4, -1)
        if self.sizes["rb"] > 1:
            total = lax.psum_scatter(total, "rb", scatter_dimension=2, tiled=True)
        return total

    def weight_grads(self, relative, absolute):
        flat = [[piece[:, i] for i in range(4)] for piece in relative]
        flat += [self.pick(piece.transpose(1, 0, 2)) for piece in absolute]
        sizes = [piece[0].shape[0] for piece in flat]
        parts = self.team_send([jnp.concatenate([piece[i] for piece in flat]) for i in range(4)])
        low = jnp.stack(parts)
        if self.sizes["dp"] == 2:
            low = low.astype(F32) + lax.ppermute(low, "dp", [(0, 1), (1, 0)]).astype(F32)
        else:
            low = lax.psum(low.astype(F32), "dp")
        parts = [low[i] for i in range(4)]
        low = self.place(parts, self.spots())
        out, at = [], 0
        for size in sizes:
            out.append(low[:, at:at + size])
            at += size
        return out


def norm_forward(hidden, gain_row, shift_row):
    average = jnp.mean(hidden, axis=1, keepdims=True)
    square = jnp.mean(hidden * hidden, axis=1, keepdims=True)
    inverse = lax.rsqrt(square - average * average + EPSILON)
    normed = (hidden - average) * inverse
    return normed * gain_row + shift_row, normed, inverse


def norm_backward(upstream, normed, inverse, gain_row):
    scaled = upstream * gain_row
    first = jnp.mean(scaled, axis=1, keepdims=True)
    second = jnp.mean(scaled * normed, axis=1, keepdims=True)
    grad = inverse * (scaled - first - normed * second)
    return grad, jnp.sum(upstream * normed, axis=0), jnp.sum(upstream, axis=0)


def normal_below(inputs):
    return 0.5 * (1.0 + lax.erf(inputs * 0.5 ** 0.5))


def gelu_slope(inputs):
    return normal_below(inputs) + inputs * jnp.exp(-0.5 * inputs * inputs) * (2.0 * jnp.pi) ** -0.5


def column_rows(weight):
    features, parts, width = weight.shape
    blocks = weight.reshape(features, parts, 4, width // 4).transpose(2, 1, 3, 0)
    return blocks.reshape(4, -1, features)


def column_rows_back(blocks, parts):
    features = blocks.shape[2]
    return blocks.reshape(4, parts, -1, features).transpose(3, 1, 0, 2).reshape(features, parts, -1)


def shards(
    layout, tokens, encoder, cotangent, prefixes, selfqkv, selfbias, selfproj, selfshift, crossquery,
    crosskv, crossbias, crossproj, crossshift, upweight, upbias, downweight, downbias, normgain, normshift,
):
    me = layout.me()
    split_rows = lambda weight: weight.reshape(4, -1, weight.shape[1])

    def by_token(rows):
        return layout.halves(rows)

    def gather_weights(relative, absolute, widen=None):
        pieces = relative + absolute
        sizes = [piece.shape[1] for piece in pieces]
        parts = layout.team_send(layout.pick(jnp.concatenate(pieces, axis=1)))
        at = sum(piece.shape[1] for piece in relative)
        groups = []
        if relative:
            groups.append(jnp.stack([part[:at] for part in parts], axis=1))
        if absolute:
            groups.append(layout.place([part[at:] for part in parts], layout.spots()).transpose(1, 0, 2))
        piece = jnp.concatenate(groups)
        wide = layout.widen(piece) if widen is None else widen(piece)
        out, at = [], 0
        for index, size in enumerate(sizes):
            weight = wide[:, at:at + size].reshape(-1, wide.shape[2])
            out.append(weight if index < len(relative) else layout.in_order(weight))
            at += size
        return out

    (qkv_w,) = gather_weights([column_rows(selfqkv)], [])
    token_parts = layout.team_parts(by_token(tokens))
    tokens_all = jnp.concatenate(token_parts, axis=1)
    width = tokens_all.shape[1]
    group = tokens_all.shape[0]
    own_rows = group // 4
    columns = layout.count(layout.cols)
    heads = columns

    by_col = jnp.concatenate([selfbias.reshape(-1), crossbias.reshape(-1), upbias])
    by_col = layout.column_vectors(by_col)
    block = selfbias.shape[1]
    head_biases = lax.dynamic_index_in_dim(
        by_col[:, : 4 * block].reshape(columns, 4, 4, HD), me, 2, keepdims=False
    )
    up_bias = lax.dynamic_index_in_dim(
        by_col[:, 4 * block:].reshape(columns, 4, -1), me, 1, keepdims=False
    ).reshape(1, -1)
    by_row = jnp.concatenate([selfshift[None], crossshift[None], downbias[None], normgain, normshift])
    if layout.sizes["rb"] > 1:
        by_row = lax.all_gather(by_row, "rb", axis=1, tiled=True)
    by_row = layout.team_features(layout.place(layout.team_parts(by_row), layout.spots()))
    self_shift, cross_shift, down_bias = by_row[0], by_row[1], by_row[2]
    gains, shifts = by_row[3:6], by_row[6:9]

    def gather_tokens(own):
        return jnp.concatenate(layout.team_parts(own))

    def reduce_tokens(partial):
        return layout.team_total([partial[i * own_rows:(i + 1) * own_rows] for i in range(4)])

    sequence_prefix = prefixes
    if layout.sizes["sq"] > 1:
        sequence_prefix = lax.dynamic_slice_in_dim(prefixes, lax.axis_index("sq"), 1, 0)

    kv_w, self_w, query_w = gather_weights(
        [column_rows(crosskv)],
        [split_rows(selfproj), column_rows(crossquery[:, None])],
    )
    encoder_all = jnp.concatenate(layout.team_parts(by_token(encoder)), axis=1)
    pair = contract(kv_w, encoder_all, 1, 1).reshape(heads, 2, HD, group)
    pair_bias = jnp.stack([jnp.zeros_like(head_biases[:, 3]), head_biases[:, 3]], axis=1)
    pair = (pair + pair_bias[..., None]).astype(BF16).reshape(heads, 2 * HD, group)

    qkv = contract(qkv_w, tokens_all, 1, 1).reshape(heads, 3, HD, group)
    qkv_bias = jnp.stack([head_biases[:, 0], jnp.zeros_like(head_biases[:, 0]), head_biases[:, 1]], axis=1)
    factor = jnp.array([SCALE, 1.0, 1.0], F32)[None, :, None, None]
    qkv = ((qkv + qkv_bias[..., None]) * factor).astype(BF16).reshape(heads, 3 * HD, group)
    self_set = layout.ring_exchange(qkv)
    self_set, pair = lax.optimization_barrier((self_set, pair))
    cross_set = layout.ring_trickle(pair)
    self_out, self_low, self_lse = flash_forward(sequence_prefix, self_set, 0, self_set, 1, 2, True)
    later = []

    def widen_after(piece, low=self_low, pairs=cross_set):
        low, pairs, piece = lax.optimization_barrier((low, pairs, piece))
        later.extend([low, pairs])
        return layout.widen(piece)

    spots = layout.spots()
    cross_w, up_w, down_w = gather_weights(
        [], [split_rows(crossproj), column_rows(upweight[:, None]), split_rows(downweight)], widen_after
    )
    self_low, cross_set = later
    attended = layout.ring_exchange(self_low).reshape(heads * HD, group)

    upstream = layout.team_send(layout.pick(by_token(cotangent).reshape(4, own_rows, -1)))
    upstream = layout.team_features(layout.place(upstream, spots)).astype(F32)

    own_tokens = lax.dynamic_slice_in_dim(tokens_all, me * own_rows, own_rows, 0)
    own_tokens = layout.place(layout.feature_parts(own_tokens), spots)
    own_tokens = layout.team_features(own_tokens).astype(F32)
    self_partial = contract(attended, self_w, 0, 0).reshape(4, own_rows, width)
    first_sum = own_tokens + (layout.team_total(layout.pick(self_partial)) + self_shift)
    first_out, first_normed, first_inverse = norm_forward(first_sum, gains[0], shifts[0])
    first_all = gather_tokens(first_out.astype(BF16))

    query = contract(query_w, first_all, 1, 1).reshape(heads, HD, group)
    query = ((query + head_biases[:, 2][..., None]) * SCALE).astype(BF16)
    cross_query = layout.ring_exchange(query)
    cross_out, cross_low, cross_lse = flash_forward(sequence_prefix, cross_query, 0, cross_set, 0, 1, False)
    crossed = layout.ring_exchange(cross_low).reshape(heads * HD, group)
    second_sum = first_out + (reduce_tokens(contract(crossed, cross_w, 0, 0)) + cross_shift)
    second_out, second_normed, second_inverse = norm_forward(second_sum, gains[1], shifts[1])
    second_all = gather_tokens(second_out.astype(BF16))

    hidden_pre = contract(second_all, up_w, 1, 1) + up_bias
    hidden_act = (hidden_pre * normal_below(hidden_pre)).astype(BF16)
    third_sum = second_out + (reduce_tokens(contract(hidden_act, down_w, 1, 0)) + down_bias)
    third_out, third_normed, third_inverse = norm_forward(third_sum, gains[2], shifts[2])
    layer_out = third_out.astype(BF16)
    layer_out = layout.team_send(layout.pick(layout.member_blocks(layer_out)))
    layer_out = layout.unhalves(layout.place(layer_out, spots).reshape(group, -1))

    third_grad, third_gain, third_shift = norm_backward(upstream, third_normed, third_inverse, gains[2])
    down_own = third_grad.astype(BF16)
    down_all = gather_tokens(down_own)
    act_grad = contract(down_all, down_w, 1, 1)
    pre_low = (act_grad * gelu_slope(hidden_pre)).astype(BF16)
    second_grad = third_grad + reduce_tokens(contract(pre_low, up_w, 1, 0))
    down_sum = layout.over_columns(layout.out_of_order(contract(hidden_act, down_all, 0, 0)))
    up_sum = layout.over_columns(layout.out_of_order(contract(pre_low, second_all, 0, 0)))
    mid_grad, second_gain, second_shift = norm_backward(second_grad, second_normed, second_inverse, gains[1])
    cross_own = mid_grad.astype(BF16)
    cross_all = gather_tokens(cross_own)
    crossed_grad = contract(cross_w, cross_all, 1, 1).astype(BF16).reshape(heads, HD, group)
    crossed_grad = layout.ring_exchange(crossed_grad)
    crossproj_part = contract(crossed, cross_all, 1, 0).astype(BF16)
    crossed_grad, crossproj_part = lax.optimization_barrier((crossed_grad, crossproj_part))
    crossproj_sum = layout.over_columns(layout.out_of_order(crossproj_part))
    dquery, dkeys, dvalues = flash_backward(
        sequence_prefix, cross_query, 0, cross_set, 0, 1, crossed_grad, cross_out, cross_lse, False
    )
    cross_bias_sums = (jnp.sum(dquery.astype(F32), axis=(0, 2)), jnp.sum(dvalues.astype(F32), axis=(0, 2)))
    dquery = layout.ring_exchange(dquery).reshape(heads * HD, group)
    first_grad = mid_grad + reduce_tokens(contract(dquery, query_w, 0, 0))
    dpair = layout.ring_trickle(jnp.concatenate([dkeys, dvalues], axis=1)).reshape(heads * 2 * HD, group)
    crossquery_sum = layout.over_columns(layout.out_of_order(contract(dquery, first_all, 1, 0)))
    crosskv_sum = layout.over_columns(contract(dpair, encoder_all, 1, 0))
    encoder_grad = layout.team_total(layout.feature_parts(contract(dpair, kv_w, 0, 0)))
    encoder_grad = layout.unhalves(encoder_grad)
    low_grad, first_gain, first_shift = norm_backward(first_grad, first_normed, first_inverse, gains[0])
    self_own = low_grad.astype(BF16)
    self_all = layout.place(layout.team_parts(self_own), spots).reshape(group, width)
    attended_grad = contract(self_w, self_all, 1, 1).astype(BF16).reshape(heads, HD, group)
    attended_grad = layout.ring_exchange(attended_grad)
    selfproj_part = contract(attended, self_all, 1, 0).astype(BF16)
    sums = (up_sum, down_sum, crossproj_sum)
    attended_grad, selfproj_part, sums = lax.optimization_barrier((attended_grad, selfproj_part, sums))
    early_grads = layout.weight_grads([], list(sums))
    selfproj_sum = layout.over_columns(layout.out_of_order(selfproj_part))
    dq, dk, dv = flash_backward(
        sequence_prefix, self_set, 0, self_set, 1, 2, attended_grad, self_out, self_lse, True
    )
    dq, dk, dv, early_grads, selfproj_sum = lax.optimization_barrier((dq, dk, dv, early_grads, selfproj_sum))
    upweight_grad, downweight_grad, crossproj_grad = early_grads
    crosskv_grad, selfproj_grad, crossquery_grad = layout.weight_grads(
        [crosskv_sum], [selfproj_sum, crossquery_sum]
    )
    self_bias_sums = (jnp.sum(dq.astype(F32), axis=(0, 2)), jnp.sum(dv.astype(F32), axis=(0, 2)))
    dqkv = layout.ring_exchange(jnp.concatenate([dq, dk, dv], axis=1)).reshape(heads * 3 * HD, group)
    selfqkv_sum = layout.over_columns(contract(dqkv, tokens_all, 1, 0))
    (selfqkv_grad,) = layout.weight_grads([selfqkv_sum], [])
    tokens_part = contract(dqkv, qkv_w, 0, 0)
    low_parts = jnp.concatenate(layout.pick(layout.member_blocks(low_grad)), axis=1)
    mine = lax.dynamic_slice_in_dim(tokens_part, me * own_rows, own_rows, 0) + low_parts
    tokens_part = lax.dynamic_update_slice_in_dim(tokens_part, mine, me * own_rows, 0)
    tokens_grad = layout.unhalves(layout.team_total(layout.feature_parts(tokens_part)))

    def at_head(sums):
        spot = (layout.ring_index() * 4 + me) * HD
        return lax.dynamic_update_slice_in_dim(jnp.zeros((width,), F32), sums, spot, 0)

    up_sums = jnp.zeros((columns, 4, pre_low.shape[1] // columns), F32)
    up_sums = lax.dynamic_update_index_in_dim(
        up_sums, jnp.sum(pre_low.astype(F32), axis=0).reshape(columns, -1), me, 1
    )
    column_sum = lambda low: jnp.sum(low.astype(F32), axis=0)
    rows = jnp.stack([
        first_gain, second_gain, third_gain, first_shift, second_shift, third_shift,
        column_sum(self_own), column_sum(cross_own), column_sum(down_own),
        at_head(cross_bias_sums[0]), at_head(cross_bias_sums[1]),
    ])
    rows = layout.total(jnp.concatenate([rows, up_sums.reshape(-1, width)]))
    rows, up_sums = rows[:11], rows[11:].reshape(up_sums.shape)
    late = layout.total(jnp.stack([at_head(self_bias_sums[0]), at_head(self_bias_sums[1])]))
    row_at = (lax.axis_index("rb") * 4 + me) * normgain.shape[1]
    col_at = lax.axis_index(layout.cols)
    by_row = lax.dynamic_slice_in_dim(rows[:9], row_at, normgain.shape[1], 1)
    crossbias_grad = lax.dynamic_slice_in_dim(rows[9:], col_at * block, block, 1)
    selfbias_grad = lax.dynamic_slice_in_dim(late, col_at * block, block, 1)
    upbias_grad = lax.dynamic_index_in_dim(up_sums, col_at, 0, keepdims=False).reshape(-1)
    join_rows = lambda blocks: blocks.reshape(-1, blocks.shape[2])
    return (
        layer_out,
        tokens_grad,
        encoder_grad,
        column_rows_back(selfqkv_grad, 3),
        selfbias_grad,
        join_rows(selfproj_grad),
        by_row[6],
        column_rows_back(crossquery_grad, 1)[:, 0],
        column_rows_back(crosskv_grad, 2),
        crossbias_grad,
        join_rows(crossproj_grad),
        by_row[7],
        column_rows_back(upweight_grad, 1)[:, 0],
        upbias_grad,
        join_rows(downweight_grad),
        by_row[8],
        by_row[:3],
        by_row[3:6],
    )


def solution(mesh):
    def run(*arrays):
        dp, row, col = (mesh.shape[name] for name in ("dp", "row", "col"))
        per_col = arrays[4].shape[2] // HD // col
        seqs = arrays[3].shape[0] // dp
        assert per_col == 4 and row % 4 == 0 and col % seqs == 0
        assert (row // 4) * (col // seqs) == col
        sizes = {"dp": dp, "rb": row // 4, "rx": 2, "rc": 2, "sq": seqs, "cs": col // seqs}
        grid = Mesh(mesh.devices.reshape(tuple(sizes.values())), tuple(sizes))
        rows, cols, tokens = ("rb", "rx", "rc"), ("sq", "cs"), ("dp", "sq", "cs")
        specs = {
            "tokens": P(tokens, rows), "rc": P(rows, cols), "cr": P(cols, rows), "r3c": P(rows, None, cols),
            "c": P(cols), "r": P(rows), "2c": P(None, cols), "2r": P(None, rows),
        }
        ins = (
            "tokens", "tokens", "tokens", "dp", "r3c", "2c", "cr", "r", "rc", "r3c", "2c", "cr", "r", "rc", "c", "cr", "r", "2r", "2r",
        )
        outs = (
            "tokens", "tokens", "tokens", "r3c", "2c", "cr", "r", "rc", "r3c", "2c", "cr", "r", "rc", "c", "cr", "r", "2r", "2r",
        )
        specs["dp"] = P("dp")
        body = functools.partial(shards, Layout(sizes))
        return jax.shard_map(
            body, mesh=grid, in_specs=tuple(specs[s] for s in ins), out_specs=tuple(specs[s] for s in outs),
            check_vma=False,
        )(*arrays)

    return run
```
